128 devices in a mesh: lat: 8 (over x, y_lo), lon: 16 (over y_hi, z, core).
Axes of the slice: x: 4, y: 4 (y_hi: 2, y_lo: 2; y = y_hi * 2 + y_lo), z: 4, core: 2. Of those that a mesh axis runs over, the one named last changes fastest.
Arguments:
- innovations: float32 [25, 65536], P(None, ('lat', 'lon')), may hold values from -6 to 6
- owners: int32 [65536, 1], P(('lat', 'lon')), may hold values from 0 to 127, as said below
- prof_row: int32 [65536], P(('lat', 'lon')), may hold values from 0 to 254
- prof_col: int32 [65536], P(('lat', 'lon')), may hold values from 0 to 126
- interp_weights: float32 [4, 65536], P(None, ('lat', 'lon')), may hold values from 0.1 to 1
- model_tiles: float32 [25, 4096, 8, 128], P(None, ('lat', 'lon')), may hold values from -6 to 6
- model_ids: int32 [1, 4096], P(None, ('lat', 'lon')), may hold values from 0 to 31, as said below
- face_x: float32 [2048, 2048], P('lat', 'lon'), may hold values from 0.02 to 0.12
- face_y: float32 [2048, 2048], P('lat', 'lon'), may hold values from 0.02 to 0.12
- cross_term: float32 [2048, 2048], P('lat', 'lon'), may hold values from -0.08 to 0.08
- wet_mask: int32 [2048, 2048], P('lat', 'lon'), may hold values 0 or 1
- norm_factor: float32 [25, 2048, 2048], P(None, 'lat', 'lon'), may hold values from 0.4 to 2.5
Outputs:
- smoothed: float32 [25, 2048, 2048], P(None, 'lat', 'lon')
- profile_values: float32 [25, 65536], P(None, ('lat', 'lon'))
The draws below stay inside these ranges and needn't reach their ends.
Inputs may be any that keep to these rules, and one draw needn't show every extreme that they name: `owners`: among the 512 profiles of one device no owner appears more than 8 times; in every draw one owner appears exactly 8 times among every device's profiles. Owners count analysis blocks in lat-major order. `model_ids`: the 32 slots of the model device at lat index i and lon index g form as many equal groups as the lon axis has devices; group j holds tiles of the analysis block at lat index i and lon index j, and every analysis block's 32 tiles appear exactly once over its lat row.
All inputs are finite; a program needn't handle non-finite values. No bound on the sum of `wet_mask` on one device may be relied on, other than what follows from the above.
Results may differ from the reference program's by a relative error of at most 0.00002.
Values sent between devices are 32-bit elements; how exact they have to be, the bound alone decides.
A program may use at most 128 MiB of HBM per device.

```python
import math
import jax
import jax.numpy as jnp
from jax import lax

LEV = 25
LAT_DEV = 256
LON_DEV = 128
TILES_DEV = 32
TLAT = 8
TLON = 128
STEPS = 10
P_DEV = 512
CAP = 8
PROFILES = 65536
NLAT = 2048
NLON = 2048
MODEL_SLOTS = 4096
N_LAT = 8
N_LON = 16


def draw_owners(key, part):
    count = N_LAT * N_LON
    hottest = jax.random.randint(jax.random.fold_in(key, 1), (), 0, count)

    def block_owners(block):
        block_key = jax.random.fold_in(key, 100 + block)
        others = jax.random.permutation(jax.random.fold_in(block_key, 1), count - 1)
        others = others + (others >= hottest).astype(jnp.int32)
        position = jnp.arange(P_DEV, dtype=jnp.int32)
        picked = others[jnp.maximum(position - CAP, 0) % (count - 1)]
        chosen = jnp.where(position < CAP, hottest, picked)
        shuffle = jax.random.permutation(jax.random.fold_in(block_key, 2), P_DEV)
        return chosen[shuffle]
    blocks = jax.vmap(block_owners)(jnp.arange(count, dtype=jnp.int32))
    return blocks.reshape(count * P_DEV, 1).astype(jnp.int32)


def draw_model_ids(key, part):
    group_size = TILES_DEV // N_LON
    block_keys = jax.random.split(key, N_LAT * N_LON)
    orders = jax.vmap(lambda single_key: jax.random.permutation(single_key, TILES_DEV))(block_keys)
    orders = orders.reshape(N_LAT, N_LON, N_LON, group_size)
    placed = jnp.transpose(orders, (0, 2, 1, 3))
    return placed.reshape(1, -1).astype(jnp.int32)


def touch_ends(result, key, smallest, largest):
    spot = [jax.random.randint(jax.random.fold_in(key, axis), (), 0, length) for axis, length in enumerate(result.shape)]
    main_axis = result.shape.index(max(result.shape))
    neighbour = spot[:main_axis] + [(spot[main_axis] + 1) % result.shape[main_axis]] + spot[main_axis + 1:]
    return result.at[tuple(spot)].set(smallest).at[tuple(neighbour)].set(largest)


def steps_of(own_key, extent, cuts, least, top_value):
    factor_of = 1.0
    for dim, parts in cuts:
        steps = jax.random.uniform(jax.random.fold_in(jax.random.fold_in(own_key, 6), dim), (parts,), jnp.float32, least / len(cuts), top_value / len(cuts))
        factor_of = factor_of * jnp.repeat(jnp.exp(steps), extent[dim] // parts).reshape((-1,) + (1,) * (len(extent) - 1 - dim))
    return factor_of


def bell_draw(stream_key, dims, scale, bound, cuts=(), kind=jnp.bfloat16):
    array = scale * jax.random.normal(stream_key, dims, jnp.float32)
    if cuts:
        array = array * steps_of(stream_key, dims, cuts, -0.22, 0.18)
    return jnp.clip(array, -bound, bound).astype(kind)


def setup_inputs(seed: int = 0) -> dict:
    arg_keys = jax.random.split(jax.random.key(seed), 13)
    return {
        "innovations": bell_draw(arg_keys[0], (LEV, PROFILES), 1.0, 6.0, ((1, 128),), jnp.float32),
        "owners": draw_owners(jax.random.fold_in(arg_keys[12], 71), 0),
        "prof_row": touch_ends(jax.random.randint(arg_keys[2], (PROFILES,), 0, LAT_DEV - 1), jax.random.fold_in(arg_keys[2], 1), 0, (LAT_DEV - 1) - 1).astype(jnp.int32),
        "prof_col": touch_ends(jax.random.randint(arg_keys[3], (PROFILES,), 0, LON_DEV - 1), jax.random.fold_in(arg_keys[3], 1), 0, (LON_DEV - 1) - 1).astype(jnp.int32),
        "interp_weights": jnp.clip(0.1 + 0.9 * jax.random.uniform(arg_keys[4], (4, PROFILES), jnp.float32) ** steps_of(arg_keys[4], (4, PROFILES), ((1, 128),), -0.2, 0.2), 0.1, 1.0),
        "model_tiles": bell_draw(arg_keys[5], (LEV, MODEL_SLOTS, TLAT, TLON), 1.0, 6.0, ((1, 128),), jnp.float32),
        "model_ids": draw_model_ids(jax.random.fold_in(arg_keys[12], 71), 0),
        "face_x": jnp.clip(0.02 + 0.09999999776482582 * jax.random.uniform(arg_keys[7], (NLAT, NLON), jnp.float32) ** steps_of(arg_keys[7], (NLAT, NLON), ((0, 8), (1, 16)), -0.2, 0.2), 0.02, 0.12),
        "face_y": jnp.clip(0.02 + 0.09999999776482582 * jax.random.uniform(arg_keys[8], (NLAT, NLON), jnp.float32) ** steps_of(arg_keys[8], (NLAT, NLON), ((0, 8), (1, 16)), -0.2, 0.2), 0.02, 0.12),
        "cross_term": jnp.clip(jax.random.uniform(arg_keys[9], (NLAT, NLON), jnp.float32, -0.08, 0.08) * steps_of(arg_keys[9], (NLAT, NLON), ((0, 8), (1, 16)), -0.4, 0.0), -0.08, 0.08),
        "wet_mask": touch_ends((jax.random.randint(arg_keys[10], (NLAT, NLON), 0, 10) < 9).astype(jnp.int32), jax.random.fold_in(arg_keys[10], 1), 0, 1),
        "norm_factor": jnp.clip(jnp.exp(math.log(2.5) - 1.8325814 * jax.random.uniform(arg_keys[11], (LEV, NLAT, NLON), jnp.float32) ** steps_of(arg_keys[11], (LEV, NLAT, NLON), ((1, 8), (2, 16)), -0.2, 0.2)), 0.4, 2.5),
    }


def face_weights(stack):
    face_east = stack[0]
    face_north = stack[1]
    twist_field = stack[2]
    wet_cells = stack[3]
    east_face = face_east[1:-1, 1:-1] * wet_cells[1:-1, 1:-1] * wet_cells[1:-1, 2:]
    west_face = face_east[1:-1, :-2] * wet_cells[1:-1, :-2] * wet_cells[1:-1, 1:-1]
    north_face = face_north[1:-1, 1:-1] * wet_cells[1:-1, 1:-1] * wet_cells[2:, 1:-1]
    south_face = face_north[:-2, 1:-1] * wet_cells[:-2, 1:-1] * wet_cells[1:-1, 1:-1]
    twist_face = twist_field[1:-1, 1:-1] * wet_cells[1:-1, 1:-1]
    return (east_face, west_face, north_face, south_face, twist_face)


def widen(plane):
    padding = [(0, 0)] * (plane.ndim - 2) + [(1, 1), (0, 0)]
    padded = jnp.pad(plane, padding)
    return jnp.concatenate([padded[..., -1:], padded, padded[..., :1]], axis=-1)


def advance_level(padded, weights):
    east_face, west_face, north_face, south_face, twist_face = weights
    centre = padded[1:-1, 1:-1]
    return (centre + east_face * (padded[1:-1, 2:] - centre) + west_face * (padded[1:-1, :-2] - centre)
            + north_face * (padded[2:, 1:-1] - centre) + south_face * (padded[:-2, 1:-1] - centre)
            + 0.25 * twist_face * (padded[2:, 2:] - padded[2:, :-2] - padded[:-2, 2:] + padded[:-2, :-2]))


def reference(innovations, owners, prof_row, prof_col, interp_weights, model_tiles, model_ids, face_x, face_y, cross_term, wet_mask, norm_factor):
    lat_total = LAT_DEV * N_LAT
    lon_total = LON_DEV * N_LON
    group_size = TILES_DEV // N_LON
    slot_index = jnp.arange(MODEL_SLOTS, dtype=jnp.int32)
    model_device = slot_index // TILES_DEV
    target_lon = (slot_index % TILES_DEV) // group_size
    row_start = (model_device // N_LON) * LAT_DEV + model_ids[0] * TLAT
    col_start = target_lon * LON_DEV
    row_grid = row_start[:, None, None] + jnp.arange(TLAT, dtype=jnp.int32)[None, :, None]
    col_grid = col_start[:, None, None] + jnp.arange(TLON, dtype=jnp.int32)[None, None, :]
    increment = jnp.zeros((LEV, lat_total, lon_total), jnp.float32).at[:, row_grid, col_grid].set(model_tiles)

    owner_list = owners[:, 0]
    base_row = (owner_list // N_LON) * LAT_DEV + prof_row
    base_col = (owner_list % N_LON) * LON_DEV + prof_col
    base_cell = base_row * lon_total + base_col
    corner_cells = jnp.concatenate([base_cell, base_cell + 1, base_cell + lon_total, base_cell + lon_total + 1])
    spread = jnp.concatenate([innovations * interp_weights[corner][None, :] for corner in range(4)], axis=1)
    observed = jnp.zeros((LEV, lat_total * lon_total), jnp.float32).at[:, corner_cells].add(spread)
    observed = observed.reshape(LEV, lat_total, lon_total)
    field = norm_factor * (observed + increment)

    stacked = jnp.stack([face_x, face_y, cross_term, wet_mask.astype(jnp.float32)])
    weights = face_weights(widen(stacked))

    def smooth_level(plane):
        def one_step(number, values):
            return advance_level(widen(values), weights)
        return lax.fori_loop(0, STEPS, one_step, plane)

    field = lax.map(smooth_level, field)
    smoothed = norm_factor * field
    flat_field = smoothed.reshape(LEV, -1)
    sampled = (interp_weights[0][None, :] * flat_field[:, base_cell]
               + interp_weights[1][None, :] * flat_field[:, base_cell + 1]
               + interp_weights[2][None, :] * flat_field[:, base_cell + lon_total]
               + interp_weights[3][None, :] * flat_field[:, base_cell + lon_total + 1])
    return (smoothed, sampled)
```

```python
import functools

import jax
import jax.numpy as jnp
from jax import lax
from jax.experimental import pallas as pl
from jax.experimental.pallas import tpu as pltpu
from jax.sharding import PartitionSpec as P

STEPS = 10
HALO = 16
LANES = 128
SLOTS = LANES // HALO
CHUNK = 8
EDGE = 4
MESH = pl.DeviceIdType.MESH


def lane_ids(shape):
    return lax.broadcasted_iota(jnp.int32, shape, len(shape) - 1)


def exchange_kernel(
    n_lat,
    n_lon,
    field,
    coef,
    west_cols,
    east_cols,
    south_field,
    north_field,
    south_coef,
    north_coef,
    pack_first,
    pack_last,
    send_sem,
    recv_sem,
):
    lat = lax.axis_index("lat")
    lon = lax.axis_index("lon")
    up = lax.rem(lat + 1, n_lat)
    down = lax.rem(lat + n_lat - 1, n_lat)
    right = lax.rem(lon + 1, n_lon)
    left = lax.rem(lon + n_lon - 1, n_lon)
    rows = field.shape[1]

    barrier = pltpu.get_barrier_semaphore()
    for there in (
        (lat, right),
        (lat, left),
        (up, lon),
        (down, lon),
        (up, right),
        (up, left),
        (down, right),
        (down, left),
    ):
        pl.semaphore_signal(barrier, inc=1, device_id=there, device_id_type=MESH)
    pl.semaphore_wait(barrier, 8)

    copies = []

    def send(source, target, there):
        number = len(copies)
        copy = pltpu.make_async_remote_copy(
            src_ref=source,
            dst_ref=target,
            send_sem=send_sem.at[number],
            recv_sem=recv_sem.at[number],
            device_id=there,
            device_id_type=MESH,
        )
        copy.start()
        copies.append(copy)

    first = pl.ds(0, HALO)
    last = pl.ds(rows - HALO, HALO)
    send(field.at[:, last, :], south_field, (up, lon))
    send(field.at[:, first, :], north_field, (down, lon))
    send(coef.at[:, last, :], south_coef, (up, lon))
    send(coef.at[:, first, :], north_coef, (down, lon))

    levels = field.shape[0]
    planes = levels + coef.shape[0]
    slot = lane_ids((rows, LANES)) // HALO
    for tile in range(pack_first.shape[0]):
        low = jnp.zeros((rows, LANES), jnp.float32)
        high = jnp.zeros((rows, LANES), jnp.float32)
        for k in range(SLOTS):
            plane = tile * SLOTS + k
            if plane >= planes:
                continue
            values = field[plane] if plane < levels else coef[plane - levels]
            if k:
                values = pltpu.roll(values, HALO * k, 1)
            low = jnp.where(slot == k, values, low)
            high = jnp.where(slot == (k + SLOTS - 1) % SLOTS, values, high)
        pack_first[tile] = low
        pack_last[tile] = high

    own = pl.ds(HALO, rows)
    above = pl.ds(HALO + rows, HALO)
    send(pack_last, west_cols.at[:, own, :], (lat, right))
    send(pack_first, east_cols.at[:, own, :], (lat, left))
    send(pack_last.at[:, last, :], west_cols.at[:, first, :], (up, right))
    send(pack_first.at[:, last, :], east_cols.at[:, first, :], (up, left))
    send(pack_last.at[:, first, :], west_cols.at[:, above, :], (down, right))
    send(pack_first.at[:, first, :], east_cols.at[:, above, :], (down, left))
    for copy in copies:
        copy.wait()


def exchange(field, coef, n_lat, n_lon):
    levels, rows, lanes = field.shape
    planes = levels + coef.shape[0]
    tiles = -(-planes // SLOTS)
    whole = pl.BlockSpec(memory_space=pltpu.VMEM)
    packed = jax.ShapeDtypeStruct((tiles, rows + 2 * HALO, lanes), jnp.float32)
    edge_field = jax.ShapeDtypeStruct((levels, HALO, lanes), jnp.float32)
    edge_coef = jax.ShapeDtypeStruct((coef.shape[0], HALO, lanes), jnp.float32)
    return pl.pallas_call(
        functools.partial(exchange_kernel, n_lat, n_lon),
        out_shape=(packed, packed, edge_field, edge_field, edge_coef, edge_coef),
        in_specs=[whole] * 2,
        out_specs=[whole] * 6,
        scratch_shapes=[
            pltpu.VMEM((tiles, rows, lanes), jnp.float32),
            pltpu.VMEM((tiles, rows, lanes), jnp.float32),
            pltpu.SemaphoreType.DMA((10,)),
            pltpu.SemaphoreType.DMA((10,)),
        ],
        compiler_params=pltpu.CompilerParams(
            collective_id=0, has_side_effects=True, vmem_limit_bytes=40 << 20
        ),
    )(field, coef)


def rolled(main, side, shift):
    lanes = lane_ids(main.shape)
    seam = lanes == (0 if shift == 1 else LANES - 1)
    main = pltpu.roll(main, shift % LANES, 1)
    side = pltpu.roll(side, shift % LANES, 1)
    return jnp.where(seam, side, main), jnp.where(seam, main, side)


def diffuse_kernel(
    n_lat,
    field,
    coef,
    norm,
    west_cols,
    east_cols,
    south_field,
    north_field,
    south_coef,
    north_coef,
    out,
    main,
    side,
    raw,
    weights,
):
    lat = lax.axis_index("lat")
    levels, rows, lanes = field.shape
    tall = rows + 2 * HALO
    has_south = lat > 0
    has_north = lat < n_lat - 1

    lane = lane_ids((tall, lanes))
    row = lax.broadcasted_iota(jnp.int32, (tall, lanes), 0)
    inside = jnp.logical_and(
        jnp.logical_or(row >= HALO, has_south), jnp.logical_or(row < HALO + rows, has_north)
    )
    from_east = jnp.logical_and(lane < HALO, inside)
    from_west = jnp.logical_and(lane >= lanes - HALO, inside)

    def side_plane(plane):
        tile, k = divmod(plane, SLOTS)
        east = east_cols[tile]
        west = west_cols[tile]
        if k:
            east = pltpu.roll(east, lanes - HALO * k, 1)
            west = pltpu.roll(west, lanes - HALO * k, 1)
        return jnp.where(from_east, east, jnp.where(from_west, west, 0.0))

    for level in range(levels):
        main[0, level, pl.ds(0, HALO), :] = jnp.where(has_south, south_field[level], 0.0)
        main[0, level, pl.ds(HALO, rows), :] = field[level]
        main[0, level, pl.ds(HALO + rows, HALO), :] = jnp.where(has_north, north_field[level], 0.0)
        side[0, level] = side_plane(level)
    for number in range(coef.shape[0]):
        raw[number, 0, pl.ds(0, HALO), :] = jnp.where(has_south, south_coef[number], 0.0)
        raw[number, 0, pl.ds(HALO, rows), :] = coef[number]
        raw[number, 0, pl.ds(HALO + rows, HALO), :] = jnp.where(
            has_north, north_coef[number], 0.0
        )
        raw[number, 1] = side_plane(levels + number)

    count = (tall - 2 * EDGE) // CHUNK

    def make_weights(step, carry):
        start = EDGE + step * CHUNK
        here = pl.ds(start, CHUNK)
        below = pl.ds(start - 1, CHUNK)
        above = pl.ds(start + 1, CHUNK)
        face_x = (raw[0, 0, here, :], raw[0, 1, here, :])
        cross = (raw[2, 0, here, :], raw[2, 1, here, :])
        wet = (raw[3, 0, here, :], raw[3, 1, here, :])
        wet_right = rolled(*wet, -1)
        east = tuple(face_x[t] * wet[t] * wet_right[t] for t in range(2))
        west = rolled(*east, 1)
        twist = tuple(0.25 * cross[t] * wet[t] for t in range(2))
        twist_right = rolled(*twist, 1)
        twist_left = rolled(*twist, -1)
        for t in range(2):
            north = raw[1, t, here, :] * wet[t] * raw[3, t, above, :]
            south = raw[1, t, below, :] * raw[3, t, below, :] * wet[t]
            keep = 1.0 - (east[t] + west[t] + north + south)
            for number, value in enumerate(
                (keep, north, south, west[t], twist_right[t], east[t], -twist_left[t])
            ):
                weights[number, t, pl.ds(step * CHUNK, CHUNK), :] = value
        return carry

    lax.fori_loop(0, count, make_weights, 0)

    seam_right = lane_ids((CHUNK, lanes)) == lanes - 1
    seam_left = lane_ids((CHUNK, lanes)) == 0

    def sweep(source, target):
        def one_chunk(step, carry):
            start = EDGE + step * CHUNK
            here = pl.ds(start, CHUNK)
            below = pl.ds(start - 1, CHUNK)
            above = pl.ds(start + 1, CHUNK)
            own = pl.ds(step * CHUNK, CHUNK)
            table = [[weights[number, t, own, :] for number in range(7)] for t in range(2)]

            for level in range(levels):
                partial, going_left, going_right = [], [], []
                for t, buffer in enumerate((main, side)):
                    keep, north, south, to_left, twist_left, to_right, twist_right = table[t]
                    centre = buffer[source, level, here, :]
                    upper = buffer[source, level, above, :]
                    lower = buffer[source, level, below, :]
                    tilt = upper - lower
                    partial.append(keep * centre + (north * upper + south * lower))
                    going_left.append(pltpu.roll(to_left * centre + twist_left * tilt, lanes - 1, 1))
                    going_right.append(pltpu.roll(to_right * centre + twist_right * tilt, 1, 1))
                for t, buffer in enumerate((main, side)):
                    buffer[target, level, here, :] = (
                        partial[t]
                        + jnp.where(seam_right, going_left[1 - t], going_left[t])
                        + jnp.where(seam_left, going_right[1 - t], going_right[t])
                    )
            return carry

        lax.fori_loop(0, count, one_chunk, 0)

    def two_steps(number, carry):
        sweep(0, 1)
        sweep(1, 0)
        return carry

    lax.fori_loop(0, STEPS // 2, two_steps, 0)
    for level in range(levels):
        out[level] = norm[level] * main[0, level, pl.ds(HALO, rows), :]


def diffuse(field, coef, norm, halos, n_lat):
    levels, rows, lanes = field.shape
    tall = rows + 2 * HALO
    whole = pl.BlockSpec(memory_space=pltpu.VMEM)
    return pl.pallas_call(
        functools.partial(diffuse_kernel, n_lat),
        out_shape=jax.ShapeDtypeStruct(field.shape, jnp.float32),
        in_specs=[whole] * (3 + len(halos)),
        out_specs=whole,
        scratch_shapes=[
            pltpu.VMEM((2, levels, tall, lanes), jnp.float32),
            pltpu.VMEM((2, levels, tall, lanes), jnp.float32),
            pltpu.VMEM((coef.shape[0], 2, tall, lanes), jnp.float32),
            pltpu.VMEM((7, 2, tall - 2 * EDGE, lanes), jnp.float32),
        ],
        compiler_params=pltpu.CompilerParams(vmem_limit_bytes=56 << 20),
    )(field, coef, norm, *halos)


def on_device(
    innovations,
    owners,
    prof_row,
    prof_col,
    interp_weights,
    model_tiles,
    model_ids,
    face_x,
    face_y,
    cross_term,
    wet_mask,
    norm_factor,
):
    levels = norm_factor.shape[0]
    lat_cells = norm_factor.shape[1]
    lon_cells = norm_factor.shape[2]
    moved_tiles, moved_ids = (
        lax.all_to_all(model_tiles, "lon", split_axis=1, concat_axis=1, tiled=True),
        lax.all_to_all(model_ids, "lon", split_axis=1, concat_axis=1, tiled=True),
    )
    increment = jnp.zeros_like(moved_tiles).at[:, moved_ids[0]].set(moved_tiles)
    increment = increment.reshape(levels, lat_cells, lon_cells)
    devices = lax.axis_size(("lat", "lon"))
    local_count = innovations.shape[1]
    capacity = 2 * local_count // devices
    owner_list = owners[:, 0]
    one_hot = (owner_list[:, None] == jnp.arange(devices, dtype=jnp.int32)[None, :]).astype(
        jnp.int32
    )
    running = jnp.cumsum(one_hot, axis=0)
    rank_in = jnp.sum(running * one_hot, axis=1) - 1
    slot_of = owner_list * capacity + rank_in
    payload = jnp.concatenate([innovations, interp_weights], axis=0)
    send_float = (
        jnp.zeros((levels + 4, devices * capacity), jnp.float32).at[:, slot_of].set(payload)
    )
    location = prof_row * lon_cells + prof_col
    send_index = jnp.zeros((1, devices * capacity), jnp.int32).at[0, slot_of].set(location)
    recv_float, recv_index = (
        lax.all_to_all(send_float, ("lat", "lon"), split_axis=1, concat_axis=1, tiled=True),
        lax.all_to_all(send_index, ("lat", "lon"), split_axis=1, concat_axis=1, tiled=True),
    )
    base_cell = recv_index[0]
    recv_values = recv_float[:levels]
    recv_weights = recv_float[levels:]
    corner_cells = jnp.concatenate(
        [base_cell, base_cell + 1, base_cell + lon_cells, base_cell + lon_cells + 1]
    )
    spread = jnp.concatenate(
        [recv_values * recv_weights[corner][None, :] for corner in range(4)], axis=1
    )
    observed = (
        jnp.zeros((levels, lat_cells * lon_cells), jnp.float32).at[:, corner_cells].add(spread)
    )
    observed = observed.reshape(levels, lat_cells, lon_cells)
    field = norm_factor * (observed + increment)
    coef = jnp.stack([face_x, face_y, cross_term, wet_mask.astype(jnp.float32)])
    n_lat = lax.axis_size("lat")
    halos = exchange(field, coef, n_lat, lax.axis_size("lon"))
    smoothed = diffuse(field, coef, norm_factor, halos, n_lat)
    flat_field = smoothed.reshape(levels, -1)
    sampled = (
        recv_weights[0][None, :] * flat_field[:, base_cell]
        + recv_weights[1][None, :] * flat_field[:, base_cell + 1]
        + recv_weights[2][None, :] * flat_field[:, base_cell + lon_cells]
        + recv_weights[3][None, :] * flat_field[:, base_cell + lon_cells + 1]
    )
    returned = lax.all_to_all(sampled, ("lat", "lon"), split_axis=1, concat_axis=1, tiled=True)
    profile_values = returned[:, slot_of]
    return (smoothed, profile_values)


def solution(mesh):
    in_specs = (
        P(None, ("lat", "lon")),
        P(("lat", "lon"), None),
        P(("lat", "lon")),
        P(("lat", "lon")),
        P(None, ("lat", "lon")),
        P(None, ("lat", "lon"), None, None),
        P(None, ("lat", "lon")),
        P("lat", "lon"),
        P("lat", "lon"),
        P("lat", "lon"),
        P("lat", "lon"),
        P(None, "lat", "lon"),
    )
    out_specs = (P(None, "lat", "lon"), P(None, ("lat", "lon")))
    return jax.shard_map(
        on_device, mesh=mesh, in_specs=in_specs, out_specs=out_specs, check_vma=False
    )
```

```python
import functools

import jax
import jax.numpy as jnp
from jax import lax
from jax.experimental import pallas as pl
from jax.experimental.pallas import tpu as pltpu
from jax.sharding import PartitionSpec as P

STEPS = 10
CAPACITY = 8
PAD = 32
HALO = 16
LANES = 128
COLS = 12
PAIRS = 5
CHUNK = 40
EDGE = 4
MESH = pl.DeviceIdType.MESH


def lane_ids(shape):
    return lax.broadcasted_iota(jnp.int32, shape, len(shape) - 1)


def exchange_kernel(
    n_lat,
    n_lon,
    field,
    coef,
    west_cols,
    east_cols,
    south_field,
    north_field,
    south_coef,
    north_coef,
    pack_first,
    pack_last,
    send_sem,
    recv_sem,
):
    lat = lax.axis_index("lat")
    lon = lax.axis_index("lon")
    up = lax.rem(lat + 1, n_lat)
    down = lax.rem(lat + n_lat - 1, n_lat)
    right = lax.rem(lon + 1, n_lon)
    left = lax.rem(lon + n_lon - 1, n_lon)
    rows = field.shape[1]

    barrier = pltpu.get_barrier_semaphore()
    for there in (
        (lat, right),
        (lat, left),
        (up, lon),
        (down, lon),
        (up, right),
        (up, left),
        (down, right),
        (down, left),
    ):
        pl.semaphore_signal(barrier, inc=1, device_id=there, device_id_type=MESH)
    pl.semaphore_wait(barrier, 8)

    copies = []

    def send(source, target, there):
        number = len(copies)
        copy = pltpu.make_async_remote_copy(
            src_ref=source,
            dst_ref=target,
            send_sem=send_sem.at[number],
            recv_sem=recv_sem.at[number],
            device_id=there,
            device_id_type=MESH,
        )
        copy.start()
        copies.append(copy)

    first = pl.ds(0, HALO)
    last = pl.ds(rows - HALO, HALO)
    send(field.at[:, last, :], south_field, (up, lon))
    send(field.at[:, first, :], north_field, (down, lon))
    send(coef.at[:, last, :], south_coef, (up, lon))
    send(coef.at[:, first, :], north_coef, (down, lon))

    levels = field.shape[0]
    planes = levels + (levels % 2) + coef.shape[0]
    lane = lane_ids((rows, LANES))

    def within(start):
        start = start % LANES
        return jnp.logical_and(lane >= start, lane < start + COLS)

    for tile in range(pack_first.shape[0]):
        low = jnp.zeros((rows, LANES), jnp.float32)
        high = jnp.zeros((rows, LANES), jnp.float32)
        for k in range(PAIRS):
            for half in range(2):
                plane = 2 * (tile * PAIRS + k) + half
                if plane >= planes or levels <= plane < levels + (levels % 2):
                    continue
                values = field[plane] if plane < levels else coef[plane - planes + coef.shape[0]]
                shift = COLS * k + (LANES // 2) * half
                if shift:
                    values = pltpu.roll(values, shift, 1)
                low = jnp.where(within(shift), values, low)
                high = jnp.where(within(LANES - COLS + shift), values, high)
        pack_first[tile] = low
        pack_last[tile] = high

    own = pl.ds(HALO, rows)
    above = pl.ds(HALO + rows, HALO)
    send(pack_last, west_cols.at[:, own, :], (lat, right))
    send(pack_first, east_cols.at[:, own, :], (lat, left))
    send(pack_last.at[:, last, :], west_cols.at[:, first, :], (up, right))
    send(pack_first.at[:, last, :], east_cols.at[:, first, :], (up, left))
    send(pack_last.at[:, first, :], west_cols.at[:, above, :], (down, right))
    send(pack_first.at[:, first, :], east_cols.at[:, above, :], (down, left))
    for copy in copies:
        copy.wait()


def exchange(field, coef, n_lat, n_lon):
    levels, rows, lanes = field.shape
    pairs = (levels + 1) // 2 + coef.shape[0] // 2
    tiles = -(-pairs // PAIRS)
    whole = pl.BlockSpec(memory_space=pltpu.VMEM)
    packed = jax.ShapeDtypeStruct((tiles, rows + 2 * HALO, lanes), jnp.float32)
    edge_field = jax.ShapeDtypeStruct((levels, HALO, lanes), jnp.float32)
    edge_coef = jax.ShapeDtypeStruct((coef.shape[0], HALO, lanes), jnp.float32)
    return pl.pallas_call(
        functools.partial(exchange_kernel, n_lat, n_lon),
        out_shape=(packed, packed, edge_field, edge_field, edge_coef, edge_coef),
        in_specs=[whole] * 2,
        out_specs=[whole] * 6,
        scratch_shapes=[
            pltpu.VMEM((tiles, rows, lanes), jnp.float32),
            pltpu.VMEM((tiles, rows, lanes), jnp.float32),
            pltpu.SemaphoreType.DMA((10,)),
            pltpu.SemaphoreType.DMA((10,)),
        ],
        compiler_params=pltpu.CompilerParams(
            collective_id=0, has_side_effects=True, vmem_limit_bytes=40 << 20
        ),
    )(field, coef)


def diffuse_kernel(
    n_lat,
    field,
    coef,
    norm,
    west_cols,
    east_cols,
    south_field,
    north_field,
    south_coef,
    north_coef,
    corner_weights,
    corner_cells,
    out,
    sampled,
    grid,
    other,
    raw,
    weights,
    turned,
):
    lat = lax.axis_index("lat")
    levels, rows, lanes = field.shape
    tall = rows + 2 * HALO
    half = lanes // 2
    strips = (levels + 1) // 2
    has_south = lat > 0
    has_north = lat < n_lat - 1

    lane = lane_ids((tall, lanes)) % half
    upper_half = lane_ids((tall, lanes)) >= half
    row = lax.broadcasted_iota(jnp.int32, (tall, lanes), 0)
    inside = jnp.logical_and(
        jnp.logical_or(row >= HALO, has_south), jnp.logical_or(row < HALO + rows, has_north)
    )
    west_side = lane < half // 2
    from_west = lane < COLS
    from_east = lane >= half - COLS

    def turn(values, shift):
        shift = shift % lanes
        return pltpu.roll(values, shift, 1) if shift else values

    def strip(pair, first, second):
        tile, k = divmod(pair, PAIRS)
        low = jnp.where(west_side, turn(first, COLS), turn(first, half - COLS))
        high = jnp.where(west_side, turn(second, COLS + half), turn(second, -COLS))
        own = jnp.where(upper_half, high, low)
        east = turn(east_cols[tile], half - COLS - COLS * k)
        west = turn(west_cols[tile], COLS - COLS * k)
        halo = jnp.where(inside, jnp.where(from_east, east, west), 0.0)
        return jnp.where(jnp.logical_or(from_east, from_west), halo, own)

    for level in range(levels):
        grid[level, pl.ds(0, HALO), :] = jnp.where(has_south, south_field[level], 0.0)
        grid[level, pl.ds(HALO, rows), :] = field[level]
        grid[level, pl.ds(HALO + rows, HALO), :] = jnp.where(has_north, north_field[level], 0.0)
    for number in range(coef.shape[0]):
        raw[0, number, pl.ds(0, HALO), :] = jnp.where(has_south, south_coef[number], 0.0)
        raw[0, number, pl.ds(HALO, rows), :] = coef[number]
        raw[0, number, pl.ds(HALO + rows, HALO), :] = jnp.where(
            has_north, north_coef[number], 0.0
        )
    for pair in range(strips):
        first = grid[2 * pair]
        second = grid[min(2 * pair + 1, levels - 1)]
        grid[levels + pair] = strip(pair, first, second)
    for number in range(0, coef.shape[0], 2):
        pair = strips + number // 2
        for offset in range(2):
            plane = raw[0, number + offset]
            both = strip(pair, plane, plane)
            mirrored = turn(both, half)
            raw[1, number + offset] = jnp.where(
                upper_half, mirrored if offset == 0 else both, both if offset == 0 else mirrored
            )

    count = (tall - 2 * EDGE) // CHUNK

    def make_weights(step, carry):
        start = EDGE + step * CHUNK
        here = pl.ds(start, CHUNK)
        below = pl.ds(start - 1, CHUNK)
        above = pl.ds(start + 1, CHUNK)
        for kind in range(2):
            wet = raw[kind, 3, here, :]
            east = raw[kind, 0, here, :] * wet * turn(wet, -1)
            west = turn(east, 1)
            twist = 0.25 * raw[kind, 2, here, :] * wet
            north = raw[kind, 1, here, :] * wet * raw[kind, 3, above, :]
            south = raw[kind, 1, below, :] * raw[kind, 3, below, :] * wet
            keep = 1.0 - (east + west + north + south)
            for number, value in enumerate(
                (keep, north, south, west, turn(twist, 1), east, -turn(twist, -1))
            ):
                weights[kind, number, pl.ds(step * CHUNK, CHUNK), :] = value
        return carry

    lax.fori_loop(0, count, make_weights, 0)

    def sweep(source, target):
        def one_chunk(step, carry):
            start = EDGE + step * CHUNK
            here = pl.ds(start, CHUNK)
            below = pl.ds(start - 1, CHUNK)
            above = pl.ds(start + 1, CHUNK)
            own = pl.ds(step * CHUNK, CHUNK)
            for kind, planes in enumerate((range(levels), range(levels, levels + strips))):
                keep, north, south, to_left, twist_left, to_right, twist_right = (
                    weights[kind, number, own, :] for number in range(7)
                )
                for plane in planes:
                    centre = source[plane, here, :]
                    upper = source[plane, above, :]
                    lower = source[plane, below, :]
                    tilt = upper - lower
                    target[plane, here, :] = (
                        keep * centre
                        + (north * upper + south * lower)
                        + turn(to_left * centre + twist_left * tilt, -1)
                        + turn(to_right * centre + twist_right * tilt, 1)
                    )
            return carry

        lax.fori_loop(0, count, one_chunk, 0)

    def two_steps(number, carry):
        sweep(grid, other)
        sweep(other, grid)
        return carry

    lax.fori_loop(0, STEPS // 2, two_steps, 0)

    column = lane_ids((rows, lanes))
    inner = pl.ds(HALO, rows)
    for level in range(levels):
        edges = grid[levels + level // 2, inner, :]
        move = half * (level % 2)
        result = jnp.where(
            column < STEPS,
            turn(edges, -COLS - move),
            jnp.where(column >= lanes - STEPS, turn(edges, half + COLS - move), grid[level, inner, :]),
        )
        result = norm[level] * result
        out[level] = result
        turned[pl.ds(level, rows, stride=PAD), :] = result
    for level in range(levels, PAD):
        turned[pl.ds(level, rows, stride=PAD), :] = jnp.zeros((rows, lanes), jnp.float32)

    spots = corner_cells.shape[0] // 2
    lane8 = lane_ids((8, lanes))
    lane32 = lane_ids((PAD, lanes))

    def sample_tile(tile, carry):
        def sample_group(group, found):
            for u in range(8):
                spot = tile * lanes + group * 8 + u
                lower, upper = corner_masks(corner_weights, corner_cells, spot, spots, lane8)
                start = pl.multiple_of(corner_cells[spot] * PAD, PAD)
                low = turned[pl.ds(start, PAD), :].reshape(PAD // 8, 8, lanes)
                high = turned[pl.ds(start + PAD, PAD), :].reshape(PAD // 8, 8, lanes)
                total = jnp.sum((low * lower + high * upper).reshape(PAD, lanes), axis=1, keepdims=True)
                found = jnp.where(lane32 == group * 8 + u, total, found)
            return found

        found = lax.fori_loop(0, lanes // 8, sample_group, jnp.zeros((PAD, lanes), jnp.float32))
        square = jnp.concatenate([found, jnp.zeros((lanes - PAD, lanes), jnp.float32)], axis=0)
        sampled[pl.ds(pl.multiple_of(tile * lanes, lanes), lanes), :] = square.T
        return carry

    lax.fori_loop(0, spots // lanes, sample_tile, 0)


def diffuse(field, coef, norm, halos, corner_weights, corner_cells, n_lat):
    levels, rows, lanes = field.shape
    tall = rows + 2 * HALO
    whole = pl.BlockSpec(memory_space=pltpu.VMEM)
    scalars = pl.BlockSpec(memory_space=pltpu.SMEM)
    planes = levels + (levels + 1) // 2
    return pl.pallas_call(
        functools.partial(diffuse_kernel, n_lat),
        out_shape=(
            jax.ShapeDtypeStruct(field.shape, jnp.float32),
            jax.ShapeDtypeStruct((corner_cells.shape[0] // 2, lanes), jnp.float32),
        ),
        in_specs=[whole] * (3 + len(halos)) + [scalars] * 2,
        out_specs=(whole, whole),
        scratch_shapes=[
            pltpu.VMEM((planes, tall, lanes), jnp.float32),
            pltpu.VMEM((planes, tall, lanes), jnp.float32),
            pltpu.VMEM((2, coef.shape[0], tall, lanes), jnp.float32),
            pltpu.VMEM((2, 7, tall - 2 * EDGE, lanes), jnp.float32),
            pltpu.VMEM((rows * PAD, lanes), jnp.float32),
        ],
        compiler_params=pltpu.CompilerParams(vmem_limit_bytes=56 << 20),
    )(field, coef, norm, *halos, corner_weights, corner_cells)


def corner_masks(corner_weights, corner_cells, spot, spots, lane):
    column = corner_cells[spots + spot]
    here = lane == column
    beside = lane == column + 1
    lower = jnp.where(
        here, corner_weights[spot], jnp.where(beside, corner_weights[spots + spot], 0.0)
    )
    upper = jnp.where(
        here,
        corner_weights[2 * spots + spot],
        jnp.where(beside, corner_weights[3 * spots + spot], 0.0),
    )
    return lower, upper


def route_kernel(innovations, weights, place, owner_column, owner_row, ids, packet, slots, table):
    levels, count = innovations.shape
    total = packet.shape[0]
    same = owner_column[...] == owner_row[...]
    earlier = lax.broadcasted_iota(jnp.int32, (count, count), 0) < lax.broadcasted_iota(
        jnp.int32, (count, count), 1
    )
    rank = jnp.sum(jnp.where(jnp.logical_and(same, earlier), 1, 0), axis=0, keepdims=True)
    slot = owner_row[...] * CAPACITY + rank
    slots[...] = slot

    table[...] = jnp.zeros_like(table)
    table[pl.ds(0, levels), :] = innovations[...]
    table[pl.ds(levels, 4), :] = weights[...]
    table[pl.ds(levels + 4, 2), :] = place[...].astype(jnp.float32)
    flipped = jnp.concatenate(
        [table[:, pl.ds(start, LANES)].T for start in range(0, count, LANES)], axis=0
    )
    chosen = lax.broadcasted_iota(jnp.int32, (total, count), 0) == slot
    sent = jnp.dot(
        jnp.where(chosen, 1.0, 0.0),
        flipped,
        precision=lax.Precision.HIGHEST,
        preferred_element_type=jnp.float32,
    )
    lane = lane_ids((total, LANES))
    group = lax.broadcasted_iota(jnp.int32, (total, LANES), 0) // CAPACITY
    per_device = 2
    group = lax.rem(group, ids.shape[1] // per_device) * per_device
    numbers = jnp.concatenate(
        [ids[...].astype(jnp.float32), jnp.zeros((1, LANES - ids.shape[1]), jnp.float32)], axis=1
    )
    for t in range(per_device):
        number = jnp.sum(jnp.where(lane == group + t, numbers, 0.0), axis=1, keepdims=True)
        sent = jnp.where(lane == PAD + t, number, sent)
    packet[...] = sent


def route(innovations, weights, place, owners, ids, devices):
    whole = pl.BlockSpec(memory_space=pltpu.VMEM)
    count = innovations.shape[1]
    return pl.pallas_call(
        route_kernel,
        out_shape=(
            jax.ShapeDtypeStruct((devices * CAPACITY, LANES), jnp.float32),
            jax.ShapeDtypeStruct((1, count), jnp.int32),
        ),
        in_specs=[whole] * 6,
        out_specs=(whole, whole),
        scratch_shapes=[pltpu.VMEM((LANES, count), jnp.float32)],
        compiler_params=pltpu.CompilerParams(vmem_limit_bytes=32 << 20),
    )(innovations, weights, place, owners, owners.reshape(1, count), ids)


def spread_kernel(levels, corner_weights, corner_cells, packet, observed, first, second):
    total, lanes = packet.shape
    lane8 = lane_ids((8, lanes))
    is_level = lax.broadcasted_iota(jnp.int32, (PAD, lanes), 0) < levels
    parts = (first, second)
    for part in parts:
        part[...] = jnp.zeros_like(part)

    def spread_tile(tile, carry):
        start = pl.multiple_of(tile * lanes, lanes)
        values = jnp.where(is_level, packet[pl.ds(start, lanes), :].T[:PAD], 0.0)

        def spread_group(group, carry):
            moved = pltpu.roll(values, lax.rem(lanes - group * 8, lanes), 1)
            for u in range(8):
                spot = tile * lanes + group * 8 + u
                lower, upper = corner_masks(corner_weights, corner_cells, spot, total, lane8)
                value = jnp.broadcast_to(moved[:, u : u + 1], (PAD, lanes)).reshape(
                    PAD // 8, 8, lanes
                )
                added = jnp.concatenate(
                    [(value * lower).reshape(PAD, lanes), (value * upper).reshape(PAD, lanes)], axis=0
                )
                where = pl.ds(pl.multiple_of(corner_cells[spot] * PAD, PAD), 2 * PAD)
                part = parts[u % len(parts)]
                part[where, :] = part[where, :] + added
            return carry

        lax.fori_loop(0, lanes // 8, spread_group, 0)
        return carry

    lax.fori_loop(0, total // lanes, spread_tile, 0)
    observed[...] = first[...] + second[...]


def spread(corner_weights, corner_cells, packet, levels, rows):
    lanes = packet.shape[1]
    whole = pl.BlockSpec(memory_space=pltpu.VMEM)
    scalars = pl.BlockSpec(memory_space=pltpu.SMEM)
    return pl.pallas_call(
        functools.partial(spread_kernel, levels),
        out_shape=jax.ShapeDtypeStruct((rows * PAD, lanes), jnp.float32),
        in_specs=[scalars, scalars, whole],
        out_specs=whole,
        scratch_shapes=[pltpu.VMEM((rows * PAD, lanes), jnp.float32)] * 2,
        compiler_params=pltpu.CompilerParams(vmem_limit_bytes=40 << 20),
    )(corner_weights, corner_cells, packet)


def combine_kernel(ids, observed, tiles, norm, field):
    slots, levels, depth, lanes = tiles.shape

    def one_tile(slot, carry):
        row = pl.multiple_of(ids[slot] * depth, depth)
        rows = pl.ds(row, depth)
        for level in range(levels):
            seen = observed[pl.ds(row * PAD + level, depth, stride=PAD), :]
            field[level, rows, :] = norm[level, rows, :] * (seen + tiles[slot, level])
        return carry

    lax.fori_loop(0, slots, one_tile, 0)


def combine(ids, observed, tiles, norm):
    whole = pl.BlockSpec(memory_space=pltpu.VMEM)
    return pl.pallas_call(
        combine_kernel,
        out_shape=jax.ShapeDtypeStruct(norm.shape, jnp.float32),
        in_specs=[pl.BlockSpec(memory_space=pltpu.SMEM)] + [whole] * 3,
        out_specs=whole,
        compiler_params=pltpu.CompilerParams(vmem_limit_bytes=40 << 20),
    )(ids, observed, tiles, norm)


def collect_kernel(levels, returned, slots, out):
    total, lanes = returned.shape
    count = slots.shape[1]
    flipped = jnp.concatenate(
        [returned[pl.ds(start, lanes), :].T[:PAD] for start in range(0, total, lanes)], axis=1
    )
    chosen = lax.broadcasted_iota(jnp.int32, (total, count), 0) == slots[...]
    values = jnp.dot(
        flipped,
        jnp.where(chosen, 1.0, 0.0),
        precision=lax.Precision.HIGHEST,
        preferred_element_type=jnp.float32,
    )
    out[...] = values[:levels]


def collect(returned, slots, levels):
    whole = pl.BlockSpec(memory_space=pltpu.VMEM)
    return pl.pallas_call(
        functools.partial(collect_kernel, levels),
        out_shape=jax.ShapeDtypeStruct((levels, slots.shape[1]), jnp.float32),
        in_specs=[whole] * 2,
        out_specs=whole,
        compiler_params=pltpu.CompilerParams(vmem_limit_bytes=32 << 20),
    )(returned, slots)


def on_device(
    innovations,
    owners,
    prof_row,
    prof_col,
    interp_weights,
    model_tiles,
    model_ids,
    face_x,
    face_y,
    cross_term,
    wet_mask,
    norm_factor,
):
    levels, rows, lanes = norm_factor.shape
    n_lat = lax.axis_size("lat")
    n_lon = lax.axis_size("lon")
    devices = n_lat * n_lon
    both = ("lat", "lon")
    place = jnp.stack([prof_row, prof_col])
    packet, slots = route(innovations, interp_weights, place, owners, model_ids, devices)
    packet = lax.all_to_all(packet.reshape(devices, CAPACITY, LANES), both, 0, 0, tiled=True)
    tiles = lax.all_to_all(model_tiles, "lon", split_axis=1, concat_axis=1, tiled=True)
    tiles = jnp.transpose(tiles, (1, 0, 2, 3))
    same_lat = lax.dynamic_slice_in_dim(packet[:, 0], lax.axis_index("lat") * n_lon, n_lon, 0)
    ids = same_lat[:, PAD : PAD + 2].reshape(-1).astype(jnp.int32)
    packet = packet.reshape(devices * CAPACITY, LANES)
    corner_weights = packet[:, levels : levels + 4].T.reshape(-1)
    corner_cells = packet[:, levels + 4 : levels + 6].T.reshape(-1).astype(jnp.int32)
    observed = spread(corner_weights, corner_cells, packet, levels, rows)
    field = combine(ids, observed, tiles, norm_factor)
    coef = jnp.stack([face_x, face_y, cross_term, wet_mask.astype(jnp.float32)])
    halos = exchange(field, coef, n_lat, n_lon)
    smoothed, sampled = diffuse(
        field, coef, norm_factor, halos, corner_weights, corner_cells, n_lat
    )
    returned = lax.all_to_all(sampled.reshape(devices, CAPACITY, LANES), both, 0, 0, tiled=True)
    profile_values = collect(returned.reshape(devices * CAPACITY, LANES), slots, levels)
    return (smoothed, profile_values)


def solution(mesh):
    in_specs = (
        P(None, ("lat", "lon")),
        P(("lat", "lon"), None),
        P(("lat", "lon")),
        P(("lat", "lon")),
        P(None, ("lat", "lon")),
        P(None, ("lat", "lon"), None, None),
        P(None, ("lat", "lon")),
        P("lat", "lon"),
        P("lat", "lon"),
        P("lat", "lon"),
        P("lat", "lon"),
        P(None, "lat", "lon"),
    )
    out_specs = (P(None, "lat", "lon"), P(None, ("lat", "lon")))
    return jax.shard_map(
        on_device, mesh=mesh, in_specs=in_specs, out_specs=out_specs, check_vma=False
    )
```

```python
import functools

import jax
import jax.numpy as jnp
from jax import lax
from jax.experimental import pallas as pl
from jax.experimental.pallas import tpu as pltpu
from jax.sharding import PartitionSpec as P

STEPS = 10
CAPACITY = 8
PAD = 32
UNROLL = 32
HALO = 16
LANES = 128
COLS = 12
PAIRS = 5
CHUNK = 40
EDGE = 4
MESH = pl.DeviceIdType.MESH


def lane_ids(shape):
    return lax.broadcasted_iota(jnp.int32, shape, len(shape) - 1)


def exchange_kernel(
    n_lat,
    n_lon,
    field,
    coef,
    west_cols,
    east_cols,
    south_field,
    north_field,
    south_coef,
    north_coef,
    pack_first,
    pack_last,
    send_sem,
    recv_sem,
):
    lat = lax.axis_index("lat")
    lon = lax.axis_index("lon")
    up = lax.rem(lat + 1, n_lat)
    down = lax.rem(lat + n_lat - 1, n_lat)
    right = lax.rem(lon + 1, n_lon)
    left = lax.rem(lon + n_lon - 1, n_lon)
    rows = field.shape[1]

    barrier = pltpu.get_barrier_semaphore()
    for there in (
        (lat, right),
        (lat, left),
        (up, lon),
        (down, lon),
        (up, right),
        (up, left),
        (down, right),
        (down, left),
    ):
        pl.semaphore_signal(barrier, inc=1, device_id=there, device_id_type=MESH)
    pl.semaphore_wait(barrier, 8)

    copies = []

    def send(source, target, there):
        number = len(copies)
        copy = pltpu.make_async_remote_copy(
            src_ref=source,
            dst_ref=target,
            send_sem=send_sem.at[number],
            recv_sem=recv_sem.at[number],
            device_id=there,
            device_id_type=MESH,
        )
        copy.start()
        copies.append(copy)

    first = pl.ds(0, HALO)
    last = pl.ds(rows - HALO, HALO)
    send(field.at[:, last, :], south_field, (up, lon))
    send(field.at[:, first, :], north_field, (down, lon))
    send(coef.at[:, last, :], south_coef, (up, lon))
    send(coef.at[:, first, :], north_coef, (down, lon))

    levels = field.shape[0]
    planes = levels + (levels % 2) + coef.shape[0]
    lane = lane_ids((rows, LANES))

    def within(start):
        start = start % LANES
        return jnp.logical_and(lane >= start, lane < start + COLS)

    for tile in range(pack_first.shape[0]):
        low = jnp.zeros((rows, LANES), jnp.float32)
        high = jnp.zeros((rows, LANES), jnp.float32)
        for k in range(PAIRS):
            for half in range(2):
                plane = 2 * (tile * PAIRS + k) + half
                if plane >= planes or levels <= plane < levels + (levels % 2):
                    continue
                values = field[plane] if plane < levels else coef[plane - planes + coef.shape[0]]
                shift = COLS * k + (LANES // 2) * half
                if shift:
                    values = pltpu.roll(values, shift, 1)
                low = jnp.where(within(shift), values, low)
                high = jnp.where(within(LANES - COLS + shift), values, high)
        pack_first[tile] = low
        pack_last[tile] = high

    own = pl.ds(HALO, rows)
    above = pl.ds(HALO + rows, HALO)
    send(pack_last, west_cols.at[:, own, :], (lat, right))
    send(pack_first, east_cols.at[:, own, :], (lat, left))
    send(pack_last.at[:, last, :], west_cols.at[:, first, :], (up, right))
    send(pack_first.at[:, last, :], east_cols.at[:, first, :], (up, left))
    send(pack_last.at[:, first, :], west_cols.at[:, above, :], (down, right))
    send(pack_first.at[:, first, :], east_cols.at[:, above, :], (down, left))
    for copy in copies:
        copy.wait()


def exchange(field, coef, n_lat, n_lon):
    levels, rows, lanes = field.shape
    pairs = (levels + 1) // 2 + coef.shape[0] // 2
    tiles = -(-pairs // PAIRS)
    whole = pl.BlockSpec(memory_space=pltpu.VMEM)
    packed = jax.ShapeDtypeStruct((tiles, rows + 2 * HALO, lanes), jnp.float32)
    edge_field = jax.ShapeDtypeStruct((levels, HALO, lanes), jnp.float32)
    edge_coef = jax.ShapeDtypeStruct((coef.shape[0], HALO, lanes), jnp.float32)
    return pl.pallas_call(
        functools.partial(exchange_kernel, n_lat, n_lon),
        out_shape=(packed, packed, edge_field, edge_field, edge_coef, edge_coef),
        in_specs=[whole] * 2,
        out_specs=[whole] * 6,
        scratch_shapes=[
            pltpu.VMEM((tiles, rows, lanes), jnp.float32),
            pltpu.VMEM((tiles, rows, lanes), jnp.float32),
            pltpu.SemaphoreType.DMA((10,)),
            pltpu.SemaphoreType.DMA((10,)),
        ],
        compiler_params=pltpu.CompilerParams(
            collective_id=0, has_side_effects=True, vmem_limit_bytes=40 << 20
        ),
    )(field, coef)


def diffuse_kernel(
    n_lat,
    field,
    coef,
    norm,
    west_cols,
    east_cols,
    south_field,
    north_field,
    south_coef,
    north_coef,
    corner_weights,
    corner_cells,
    out,
    sampled,
    grid,
    other,
    raw,
    weights,
    turned,
    gathered,
):
    lat = lax.axis_index("lat")
    levels, rows, lanes = field.shape
    tall = rows + 2 * HALO
    half = lanes // 2
    strips = (levels + 1) // 2
    has_south = lat > 0
    has_north = lat < n_lat - 1

    lane = lane_ids((tall, lanes)) % half
    upper_half = lane_ids((tall, lanes)) >= half
    row = lax.broadcasted_iota(jnp.int32, (tall, lanes), 0)
    inside = jnp.logical_and(
        jnp.logical_or(row >= HALO, has_south), jnp.logical_or(row < HALO + rows, has_north)
    )
    west_side = lane < half // 2
    from_west = lane < COLS
    from_east = lane >= half - COLS

    def turn(values, shift):
        shift = shift % lanes
        return pltpu.roll(values, shift, 1) if shift else values

    def strip(pair, first, second):
        tile, k = divmod(pair, PAIRS)
        low = jnp.where(west_side, turn(first, COLS), turn(first, half - COLS))
        high = jnp.where(west_side, turn(second, COLS + half), turn(second, -COLS))
        own = jnp.where(upper_half, high, low)
        east = turn(east_cols[tile], half - COLS - COLS * k)
        west = turn(west_cols[tile], COLS - COLS * k)
        halo = jnp.where(inside, jnp.where(from_east, east, west), 0.0)
        return jnp.where(jnp.logical_or(from_east, from_west), halo, own)

    for level in range(levels):
        grid[level, pl.ds(0, HALO), :] = jnp.where(has_south, south_field[level], 0.0)
        grid[level, pl.ds(HALO, rows), :] = field[level]
        grid[level, pl.ds(HALO + rows, HALO), :] = jnp.where(has_north, north_field[level], 0.0)
    for number in range(coef.shape[0]):
        raw[0, number, pl.ds(0, HALO), :] = jnp.where(has_south, south_coef[number], 0.0)
        raw[0, number, pl.ds(HALO, rows), :] = coef[number]
        raw[0, number, pl.ds(HALO + rows, HALO), :] = jnp.where(
            has_north, north_coef[number], 0.0
        )
    for pair in range(strips):
        first = grid[2 * pair]
        second = grid[min(2 * pair + 1, levels - 1)]
        grid[levels + pair] = strip(pair, first, second)
    for number in range(0, coef.shape[0], 2):
        pair = strips + number // 2
        for offset in range(2):
            plane = raw[0, number + offset]
            both = strip(pair, plane, plane)
            mirrored = turn(both, half)
            raw[1, number + offset] = jnp.where(
                upper_half, mirrored if offset == 0 else both, both if offset == 0 else mirrored
            )

    count = (tall - 2 * EDGE) // CHUNK

    def make_weights(step, carry):
        start = EDGE + step * CHUNK
        here = pl.ds(start, CHUNK)
        below = pl.ds(start - 1, CHUNK)
        above = pl.ds(start + 1, CHUNK)
        for kind in range(2):
            wet = raw[kind, 3, here, :]
            east = raw[kind, 0, here, :] * wet * turn(wet, -1)
            west = turn(east, 1)
            twist = 0.25 * raw[kind, 2, here, :] * wet
            north = raw[kind, 1, here, :] * wet * raw[kind, 3, above, :]
            south = raw[kind, 1, below, :] * raw[kind, 3, below, :] * wet
            keep = 1.0 - (east + west + north + south)
            for number, value in enumerate(
                (keep, north, south, west, turn(twist, 1), east, -turn(twist, -1))
            ):
                weights[kind, number, pl.ds(step * CHUNK, CHUNK), :] = value
        return carry

    lax.fori_loop(0, count, make_weights, 0)

    def sweep(source, target):
        def one_chunk(step, carry):
            start = EDGE + step * CHUNK
            here = pl.ds(start, CHUNK)
            below = pl.ds(start - 1, CHUNK)
            above = pl.ds(start + 1, CHUNK)
            own = pl.ds(step * CHUNK, CHUNK)
            for kind, planes in enumerate((range(levels), range(levels, levels + strips))):
                keep, north, south, to_left, twist_left, to_right, twist_right = (
                    weights[kind, number, own, :] for number in range(7)
                )
                for plane in planes:
                    centre = source[plane, here, :]
                    upper = source[plane, above, :]
                    lower = source[plane, below, :]
                    tilt = upper - lower
                    target[plane, here, :] = (
                        keep * centre
                        + (north * upper + south * lower)
                        + turn(to_left * centre + twist_left * tilt, -1)
                        + turn(to_right * centre + twist_right * tilt, 1)
                    )
            return carry

        lax.fori_loop(0, count, one_chunk, 0)

    def two_steps(number, carry):
        sweep(grid, other)
        sweep(other, grid)
        return carry

    lax.fori_loop(0, STEPS // 2, two_steps, 0)

    column = lane_ids((rows, lanes))
    inner = pl.ds(HALO, rows)
    for level in range(levels):
        edges = grid[levels + level // 2, inner, :]
        move = half * (level % 2)
        result = jnp.where(
            column < STEPS,
            turn(edges, -COLS - move),
            jnp.where(column >= lanes - STEPS, turn(edges, half + COLS - move), grid[level, inner, :]),
        )
        result = norm[level] * result
        out[level] = result
        turned[pl.ds(level, rows, stride=PAD), :] = result
    for level in range(levels, PAD):
        turned[pl.ds(level, rows, stride=PAD), :] = jnp.zeros((rows, lanes), jnp.float32)

    lane8 = lane_ids((8, lanes))
    lane_pad = lane_ids((PAD, lanes))
    per_row = lanes // PAD

    def sample_tile(tile, carry):
        for q in range(per_row):
            block = tile * per_row + q

            def sample_group(group, found):
                for u in range(UNROLL):
                    spot = group * UNROLL + u
                    row, lower, upper = corner_masks(corner_weights, corner_cells, block, spot, lane8)
                    start = pl.multiple_of(row * PAD, PAD)
                    low = turned[pl.ds(start, PAD), :].reshape(PAD // 8, 8, lanes)
                    high = turned[pl.ds(start + PAD, PAD), :].reshape(PAD // 8, 8, lanes)
                    mixed = (low * lower + high * upper).reshape(PAD, lanes)
                    total = jnp.sum(mixed, axis=1, keepdims=True)
                    found = jnp.where(lane_pad == spot, total, found)
                return found

            gathered[pl.ds(PAD * q, PAD), :] = lax.fori_loop(
                0, lanes // UNROLL, sample_group, jnp.zeros((PAD, lanes), jnp.float32)
            )
        sampled[pl.ds(pl.multiple_of(tile * lanes, lanes), lanes), :] = gathered[...].T
        return carry

    lax.fori_loop(0, sampled.shape[0] // lanes, sample_tile, 0)


def diffuse(field, coef, norm, halos, corner_weights, corner_cells, n_lat):
    levels, rows, lanes = field.shape
    tall = rows + 2 * HALO
    whole = pl.BlockSpec(memory_space=pltpu.VMEM)
    scalars = pl.BlockSpec(memory_space=pltpu.SMEM)
    planes = levels + (levels + 1) // 2
    return pl.pallas_call(
        functools.partial(diffuse_kernel, n_lat),
        out_shape=(
            jax.ShapeDtypeStruct(field.shape, jnp.float32),
            jax.ShapeDtypeStruct((corner_cells.shape[0] * PAD, lanes), jnp.float32),
        ),
        in_specs=[whole] * (3 + len(halos)) + [scalars] * 2,
        out_specs=(whole, whole),
        scratch_shapes=[
            pltpu.VMEM((planes, tall, lanes), jnp.float32),
            pltpu.VMEM((planes, tall, lanes), jnp.float32),
            pltpu.VMEM((2, coef.shape[0], tall, lanes), jnp.float32),
            pltpu.VMEM((2, 7, tall - 2 * EDGE, lanes), jnp.float32),
            pltpu.VMEM((rows * PAD, lanes), jnp.float32),
            pltpu.VMEM((lanes, lanes), jnp.float32),
        ],
        compiler_params=pltpu.CompilerParams(vmem_limit_bytes=56 << 20),
    )(field, coef, norm, *halos, corner_weights, corner_cells)


def corner_masks(corner_weights, corner_cells, block, spot, lane):
    column = corner_cells[block, 6, spot]
    here = lane == column
    beside = lane == column + 1
    first, second, third, fourth = (corner_weights[block, 1 + c, spot] for c in range(4))
    lower = jnp.where(here, first, jnp.where(beside, second, 0.0))
    upper = jnp.where(here, third, jnp.where(beside, fourth, 0.0))
    return corner_cells[block, 5, spot], lower, upper


def one_hot_slots(slots, q, rows):
    shape = (rows, slots.shape[1])
    number = lax.broadcasted_iota(jnp.int32, shape, 0) * (LANES // PAD) + q
    return jnp.where(number == slots, 1.0, 0.0)


def route_kernel(innovations, weights, place, owner_column, owner_row, ids, packet, slots, table):
    levels, count = innovations.shape
    total = packet.shape[0]
    same = owner_column[...] == owner_row[...]
    earlier = lax.broadcasted_iota(jnp.int32, (count, count), 0) < lax.broadcasted_iota(
        jnp.int32, (count, count), 1
    )
    rank = jnp.sum(jnp.where(jnp.logical_and(same, earlier), 1, 0), axis=0, keepdims=True)
    slot = owner_row[...] * CAPACITY + rank
    slots[...] = slot

    table[...] = jnp.zeros_like(table)
    table[pl.ds(0, levels), :] = innovations[...]
    table[pl.ds(levels, 4), :] = weights[...]
    table[pl.ds(levels + 4, 2), :] = place[...].astype(jnp.float32)
    flipped = jnp.concatenate(
        [table[:, pl.ds(start, LANES)].T for start in range(0, count, LANES)], axis=0
    )
    sent = jnp.zeros((total, LANES), jnp.float32)
    for q in range(LANES // PAD):
        moved = pltpu.roll(flipped, PAD * q, 1) if q else flipped
        sent += jnp.dot(
            one_hot_slots(slot, q, total),
            moved,
            precision=lax.Precision.HIGHEST,
            preferred_element_type=jnp.float32,
        )
    lane = lane_ids((total, LANES))
    row = lax.broadcasted_iota(jnp.int32, (total, LANES), 0)
    per_device = 2
    row_group = CAPACITY * PAD // LANES
    group = lax.rem(row // row_group, ids.shape[1] // per_device) * per_device
    first_row = lax.rem(row, row_group) == 0
    numbers = jnp.concatenate(
        [ids[...].astype(jnp.float32), jnp.zeros((1, LANES - ids.shape[1]), jnp.float32)], axis=1
    )
    for t in range(per_device):
        number = jnp.sum(jnp.where(lane == group + t, numbers, 0.0), axis=1, keepdims=True)
        spare = jnp.logical_and(first_row, lane == PAD * (t + 1) - 1)
        sent = jnp.where(spare, number, sent)
    packet[...] = sent


def route(innovations, weights, place, owners, ids, devices):
    whole = pl.BlockSpec(memory_space=pltpu.VMEM)
    count = innovations.shape[1]
    return pl.pallas_call(
        route_kernel,
        out_shape=(
            jax.ShapeDtypeStruct((devices * CAPACITY * PAD // LANES, LANES), jnp.float32),
            jax.ShapeDtypeStruct((1, count), jnp.int32),
        ),
        in_specs=[whole] * 6,
        out_specs=(whole, whole),
        scratch_shapes=[pltpu.VMEM((LANES, count), jnp.float32)],
        compiler_params=pltpu.CompilerParams(vmem_limit_bytes=32 << 20),
    )(innovations, weights, place, owners, owners.reshape(1, count), ids)


def post_kernel(n_lat, n_lon, source, target, send_sem, recv_sem, local_sem):
    lat = lax.axis_index("lat")
    lon = lax.axis_index("lon")
    me = lat * n_lon + lon
    devices = n_lat * n_lon
    barrier = pltpu.get_barrier_semaphore()

    def there(step):
        other = lax.rem(me + step, devices)
        return other, (other // n_lon, lax.rem(other, n_lon))

    def greet(step, carry):
        pl.semaphore_signal(barrier, inc=1, device_id=there(step)[1], device_id_type=MESH)
        return carry

    def transfer(step):
        other, device = there(step)
        return pltpu.make_async_remote_copy(
            src_ref=source.at[other],
            dst_ref=target.at[me],
            send_sem=send_sem.at[step],
            recv_sem=recv_sem.at[step],
            device_id=device,
            device_id_type=MESH,
        )

    def send(step, carry):
        transfer(step).start()
        return carry

    def arrive(step, carry):
        transfer(step).wait()
        return carry

    own = pltpu.make_async_copy(source.at[me], target.at[me], local_sem)
    own.start()
    lax.fori_loop(1, devices, greet, 0)
    pl.semaphore_wait(barrier, devices - 1)
    lax.fori_loop(1, devices, send, 0)
    lax.fori_loop(1, devices, arrive, 0)
    own.wait()


def post(packet, n_lat, n_lon, collective_id):
    devices = n_lat * n_lon
    whole = pl.BlockSpec(memory_space=pltpu.VMEM)
    blocks = packet.reshape(devices, -1, LANES)
    received = pl.pallas_call(
        functools.partial(post_kernel, n_lat, n_lon),
        out_shape=jax.ShapeDtypeStruct(blocks.shape, jnp.float32),
        in_specs=[whole],
        out_specs=whole,
        scratch_shapes=[
            pltpu.SemaphoreType.DMA((devices,)),
            pltpu.SemaphoreType.DMA((devices,)),
            pltpu.SemaphoreType.DMA,
        ],
        compiler_params=pltpu.CompilerParams(
            collective_id=collective_id, has_side_effects=True, vmem_limit_bytes=16 << 20
        ),
    )(blocks)
    return received.reshape(packet.shape)


def spread_kernel(
    levels, packet, observed, weights_out, cells_out, turned, other, weights, cells, sems
):
    total, lanes = packet.shape
    per_row = lanes // PAD
    tiles = total // lanes
    lane8 = lane_ids((8, lanes))
    for tile in range(tiles):
        flipped = packet[pl.ds(tile * lanes, lanes), :].T
        turned[pl.ds(tile * lanes, lanes), :] = flipped
        for q in range(per_row):
            last = flipped[PAD * (q + 1) - 8 : PAD * (q + 1)]
            weights_out[tile * per_row + q] = last
            cells_out[tile * per_row + q] = last.astype(jnp.int32)
    copies = (
        pltpu.make_async_copy(weights_out, weights, sems.at[0]),
        pltpu.make_async_copy(cells_out, cells, sems.at[1]),
    )
    for copy in copies:
        copy.start()
    is_level = lax.broadcasted_iota(jnp.int32, (PAD, lanes), 0) < levels
    parts = (observed, other)
    for part in parts:
        part[...] = jnp.zeros_like(part)
    for copy in copies:
        copy.wait()

    def spread_block(block, carry):
        values = jnp.where(is_level, turned[pl.ds(pl.multiple_of(block * PAD, PAD), PAD), :], 0.0)

        def spread_group(group, carry):
            moved = pltpu.roll(values, lax.rem(lanes - group * UNROLL, lanes), 1)
            for u in range(UNROLL):
                spot = group * UNROLL + u
                row, lower, upper = corner_masks(weights, cells, block, spot, lane8)
                value = jnp.broadcast_to(moved[:, u : u + 1], (PAD, lanes)).reshape(
                    PAD // 8, 8, lanes
                )
                added = jnp.concatenate(
                    [(value * lower).reshape(PAD, lanes), (value * upper).reshape(PAD, lanes)], axis=0
                )
                where = pl.ds(pl.multiple_of(row * PAD, PAD), 2 * PAD)
                part = parts[u % len(parts)]
                part[where, :] = part[where, :] + added
            return carry

        lax.fori_loop(0, lanes // UNROLL, spread_group, 0)
        return carry

    lax.fori_loop(0, tiles * per_row, spread_block, 0)
    observed[...] = observed[...] + other[...]


def spread(packet, levels, rows):
    total, lanes = packet.shape
    whole = pl.BlockSpec(memory_space=pltpu.VMEM)
    blocks = total // PAD
    return pl.pallas_call(
        functools.partial(spread_kernel, levels),
        out_shape=(
            jax.ShapeDtypeStruct((rows * PAD, lanes), jnp.float32),
            jax.ShapeDtypeStruct((blocks, 8, lanes), jnp.float32),
            jax.ShapeDtypeStruct((blocks, 8, lanes), jnp.int32),
        ),
        in_specs=[whole],
        out_specs=(whole, whole, whole),
        scratch_shapes=[
            pltpu.VMEM(packet.shape, jnp.float32),
            pltpu.VMEM((rows * PAD, lanes), jnp.float32),
            pltpu.SMEM((blocks, 8, lanes), jnp.float32),
            pltpu.SMEM((blocks, 8, lanes), jnp.int32),
            pltpu.SemaphoreType.DMA((2,)),
        ],
        compiler_params=pltpu.CompilerParams(vmem_limit_bytes=40 << 20),
    )(packet)


def combine_kernel(cells, observed, tiles, norm, field):
    slots, levels, depth, lanes = tiles.shape
    n_lon = lax.axis_size("lon")
    per_device = slots // n_lon
    per_row = lanes // PAD
    row_group = CAPACITY * PAD // lanes
    base = lax.axis_index("lat") * n_lon

    def one_tile(slot, carry):
        at = (base + slot // per_device) * row_group
        block = (at // lanes) * per_row + lax.rem(slot, per_device)
        row = pl.multiple_of(cells[block, 7, lax.rem(at, lanes)] * depth, depth)
        rows = pl.ds(row, depth)
        for level in range(levels):
            seen = observed[pl.ds(row * PAD + level, depth, stride=PAD), :]
            field[level, rows, :] = norm[level, rows, :] * (seen + tiles[slot, level])
        return carry

    lax.fori_loop(0, slots, one_tile, 0)


def combine(cells, observed, tiles, norm):
    whole = pl.BlockSpec(memory_space=pltpu.VMEM)
    return pl.pallas_call(
        combine_kernel,
        out_shape=jax.ShapeDtypeStruct(norm.shape, jnp.float32),
        in_specs=[pl.BlockSpec(memory_space=pltpu.SMEM)] + [whole] * 3,
        out_specs=whole,
        compiler_params=pltpu.CompilerParams(vmem_limit_bytes=40 << 20),
    )(cells, observed, tiles, norm)


def collect_kernel(levels, returned, slots, out):
    total, lanes = returned.shape
    flipped = jnp.concatenate(
        [returned[pl.ds(start, lanes), :].T for start in range(0, total, lanes)], axis=1
    )
    values = jnp.zeros((PAD, slots.shape[1]), jnp.float32)
    for q in range(lanes // PAD):
        values += jnp.dot(
            flipped[PAD * q : PAD * (q + 1)],
            one_hot_slots(slots[...], q, total),
            precision=lax.Precision.HIGHEST,
            preferred_element_type=jnp.float32,
        )
    out[...] = values[:levels]


def collect(returned, slots, levels):
    whole = pl.BlockSpec(memory_space=pltpu.VMEM)
    return pl.pallas_call(
        functools.partial(collect_kernel, levels),
        out_shape=jax.ShapeDtypeStruct((levels, slots.shape[1]), jnp.float32),
        in_specs=[whole] * 2,
        out_specs=whole,
        compiler_params=pltpu.CompilerParams(vmem_limit_bytes=32 << 20),
    )(returned, slots)


def on_device(
    innovations,
    owners,
    prof_row,
    prof_col,
    interp_weights,
    model_tiles,
    model_ids,
    face_x,
    face_y,
    cross_term,
    wet_mask,
    norm_factor,
):
    levels, rows, lanes = norm_factor.shape
    n_lat = lax.axis_size("lat")
    n_lon = lax.axis_size("lon")
    tiles = lax.all_to_all(model_tiles, "lon", split_axis=1, concat_axis=1, tiled=True)
    tiles = jnp.transpose(tiles, (1, 0, 2, 3))
    place = jnp.stack([prof_row, prof_col])
    packet, slots = route(innovations, interp_weights, place, owners, model_ids, n_lat * n_lon)
    packet = post(packet, n_lat, n_lon, 1)
    observed, corner_weights, corner_cells = spread(packet, levels, rows)
    field = combine(corner_cells, observed, tiles, norm_factor)
    coef = jnp.stack([face_x, face_y, cross_term, wet_mask.astype(jnp.float32)])
    halos = exchange(field, coef, n_lat, n_lon)
    smoothed, sampled = diffuse(
        field, coef, norm_factor, halos, corner_weights, corner_cells, n_lat
    )
    returned = post(sampled, n_lat, n_lon, 2)
    profile_values = collect(returned, slots, levels)
    return (smoothed, profile_values)


def solution(mesh):
    in_specs = (
        P(None, ("lat", "lon")),
        P(("lat", "lon"), None),
        P(("lat", "lon")),
        P(("lat", "lon")),
        P(None, ("lat", "lon")),
        P(None, ("lat", "lon"), None, None),
        P(None, ("lat", "lon")),
        P("lat", "lon"),
        P("lat", "lon"),
        P("lat", "lon"),
        P("lat", "lon"),
        P(None, "lat", "lon"),
    )
    out_specs = (P(None, "lat", "lon"), P(None, ("lat", "lon")))
    return jax.shard_map(
        on_device, mesh=mesh, in_specs=in_specs, out_specs=out_specs, check_vma=False
    )
```

```python
import functools

import jax
import jax.numpy as jnp
from jax import lax
from jax.experimental import pallas as pl
from jax.experimental.pallas import tpu as pltpu
from jax.sharding import PartitionSpec as P

STEPS = 10
CAPACITY = 8
PAD = 32
UNROLL = 32
HALO = 16
LANES = 128
COLS = 12
PAIRS = 5
CHUNK = 40
EDGE = 4
MESH = pl.DeviceIdType.MESH


def lane_ids(shape):
    return lax.broadcasted_iota(jnp.int32, shape, len(shape) - 1)


def exchange_kernel(
    n_lat,
    n_lon,
    field,
    coef,
    west_cols,
    east_cols,
    south_field,
    north_field,
    south_coef,
    north_coef,
    pack_first,
    pack_last,
    send_sem,
    recv_sem,
):
    lat = lax.axis_index("lat")
    lon = lax.axis_index("lon")
    up = lax.rem(lat + 1, n_lat)
    down = lax.rem(lat + n_lat - 1, n_lat)
    right = lax.rem(lon + 1, n_lon)
    left = lax.rem(lon + n_lon - 1, n_lon)
    rows = field.shape[1]

    barrier = pltpu.get_barrier_semaphore()
    for there in (
        (lat, right),
        (lat, left),
        (up, lon),
        (down, lon),
        (up, right),
        (up, left),
        (down, right),
        (down, left),
    ):
        pl.semaphore_signal(barrier, inc=1, device_id=there, device_id_type=MESH)
    pl.semaphore_wait(barrier, 8)

    copies = []

    def send(source, target, there):
        number = len(copies)
        copy = pltpu.make_async_remote_copy(
            src_ref=source,
            dst_ref=target,
            send_sem=send_sem.at[number],
            recv_sem=recv_sem.at[number],
            device_id=there,
            device_id_type=MESH,
        )
        copy.start()
        copies.append(copy)

    first = pl.ds(0, HALO)
    last = pl.ds(rows - HALO, HALO)
    send(field.at[:, last, :], south_field, (up, lon))
    send(field.at[:, first, :], north_field, (down, lon))
    send(coef.at[:, last, :], south_coef, (up, lon))
    send(coef.at[:, first, :], north_coef, (down, lon))

    levels = field.shape[0]
    planes = levels + (levels % 2) + coef.shape[0]
    lane = lane_ids((rows, LANES))

    def within(start):
        start = start % LANES
        return jnp.logical_and(lane >= start, lane < start + COLS)

    for tile in range(pack_first.shape[0]):
        low = jnp.zeros((rows, LANES), jnp.float32)
        high = jnp.zeros((rows, LANES), jnp.float32)
        for k in range(PAIRS):
            for half in range(2):
                plane = 2 * (tile * PAIRS + k) + half
                if plane >= planes or levels <= plane < levels + (levels % 2):
                    continue
                values = field[plane] if plane < levels else coef[plane - planes + coef.shape[0]]
                shift = COLS * k + (LANES // 2) * half
                if shift:
                    values = pltpu.roll(values, shift, 1)
                low = jnp.where(within(shift), values, low)
                high = jnp.where(within(LANES - COLS + shift), values, high)
        pack_first[tile] = low
        pack_last[tile] = high

    own = pl.ds(HALO, rows)
    above = pl.ds(HALO + rows, HALO)
    send(pack_last, west_cols.at[:, own, :], (lat, right))
    send(pack_first, east_cols.at[:, own, :], (lat, left))
    send(pack_last.at[:, last, :], west_cols.at[:, first, :], (up, right))
    send(pack_first.at[:, last, :], east_cols.at[:, first, :], (up, left))
    send(pack_last.at[:, first, :], west_cols.at[:, above, :], (down, right))
    send(pack_first.at[:, first, :], east_cols.at[:, above, :], (down, left))
    for copy in copies:
        copy.wait()


def exchange(field, coef, n_lat, n_lon):
    levels, rows, lanes = field.shape
    pairs = (levels + 1) // 2 + coef.shape[0] // 2
    tiles = -(-pairs // PAIRS)
    whole = pl.BlockSpec(memory_space=pltpu.VMEM)
    packed = jax.ShapeDtypeStruct((tiles, rows + 2 * HALO, lanes), jnp.float32)
    edge_field = jax.ShapeDtypeStruct((levels, HALO, lanes), jnp.float32)
    edge_coef = jax.ShapeDtypeStruct((coef.shape[0], HALO, lanes), jnp.float32)
    return pl.pallas_call(
        functools.partial(exchange_kernel, n_lat, n_lon),
        out_shape=(packed, packed, edge_field, edge_field, edge_coef, edge_coef),
        in_specs=[whole] * 2,
        out_specs=[whole] * 6,
        scratch_shapes=[
            pltpu.VMEM((tiles, rows, lanes), jnp.float32),
            pltpu.VMEM((tiles, rows, lanes), jnp.float32),
            pltpu.SemaphoreType.DMA((10,)),
            pltpu.SemaphoreType.DMA((10,)),
        ],
        compiler_params=pltpu.CompilerParams(
            collective_id=0, has_side_effects=True, vmem_limit_bytes=8 << 20
        ),
    )(field, coef)


def diffuse_kernel(
    n_lat,
    field,
    coef,
    norm,
    west_cols,
    east_cols,
    south_field,
    north_field,
    south_coef,
    north_coef,
    lower,
    upper,
    cells,
    out,
    sampled,
    grid,
    other,
    raw,
    weights,
    turned,
    gathered,
):
    lat = lax.axis_index("lat")
    levels, rows, lanes = field.shape
    tall = rows + 2 * HALO
    half = lanes // 2
    strips = (levels + 1) // 2
    has_south = lat > 0
    has_north = lat < n_lat - 1

    lane = lane_ids((tall, lanes)) % half
    upper_half = lane_ids((tall, lanes)) >= half
    row = lax.broadcasted_iota(jnp.int32, (tall, lanes), 0)
    inside = jnp.logical_and(
        jnp.logical_or(row >= HALO, has_south), jnp.logical_or(row < HALO + rows, has_north)
    )
    west_side = lane < half // 2
    from_west = lane < COLS
    from_east = lane >= half - COLS

    def turn(values, shift):
        shift = shift % lanes
        return pltpu.roll(values, shift, 1) if shift else values

    def strip(pair, first, second):
        tile, k = divmod(pair, PAIRS)
        low = jnp.where(west_side, turn(first, COLS), turn(first, half - COLS))
        high = jnp.where(west_side, turn(second, COLS + half), turn(second, -COLS))
        own = jnp.where(upper_half, high, low)
        east = turn(east_cols[tile], half - COLS - COLS * k)
        west = turn(west_cols[tile], COLS - COLS * k)
        halo = jnp.where(inside, jnp.where(from_east, east, west), 0.0)
        return jnp.where(jnp.logical_or(from_east, from_west), halo, own)

    for level in range(levels):
        grid[level, pl.ds(0, HALO), :] = jnp.where(has_south, south_field[level], 0.0)
        grid[level, pl.ds(HALO, rows), :] = field[level]
        grid[level, pl.ds(HALO + rows, HALO), :] = jnp.where(has_north, north_field[level], 0.0)
    for number in range(coef.shape[0]):
        raw[0, number, pl.ds(0, HALO), :] = jnp.where(has_south, south_coef[number], 0.0)
        raw[0, number, pl.ds(HALO, rows), :] = coef[number]
        raw[0, number, pl.ds(HALO + rows, HALO), :] = jnp.where(
            has_north, north_coef[number], 0.0
        )
    for pair in range(strips):
        first = grid[2 * pair]
        second = grid[min(2 * pair + 1, levels - 1)]
        grid[levels + pair] = strip(pair, first, second)
    for number in range(0, coef.shape[0], 2):
        pair = strips + number // 2
        for offset in range(2):
            plane = raw[0, number + offset]
            both = strip(pair, plane, plane)
            mirrored = turn(both, half)
            raw[1, number + offset] = jnp.where(
                upper_half, mirrored if offset == 0 else both, both if offset == 0 else mirrored
            )

    count = (tall - 2 * EDGE) // CHUNK

    def make_weights(step, carry):
        start = EDGE + step * CHUNK
        here = pl.ds(start, CHUNK)
        below = pl.ds(start - 1, CHUNK)
        above = pl.ds(start + 1, CHUNK)
        for kind in range(2):
            wet = raw[kind, 3, here, :]
            east = raw[kind, 0, here, :] * wet * turn(wet, -1)
            west = turn(east, 1)
            twist = 0.25 * raw[kind, 2, here, :] * wet
            north = raw[kind, 1, here, :] * wet * raw[kind, 3, above, :]
            south = raw[kind, 1, below, :] * raw[kind, 3, below, :] * wet
            keep = 1.0 - (east + west + north + south)
            for number, value in enumerate(
                (keep, north, south, west, turn(twist, 1), east, -turn(twist, -1))
            ):
                weights[kind, number, pl.ds(step * CHUNK, CHUNK), :] = value
        return carry

    lax.fori_loop(0, count, make_weights, 0)

    def sweep(source, target):
        def one_chunk(step, carry):
            start = EDGE + step * CHUNK
            here = pl.ds(start, CHUNK)
            below = pl.ds(start - 1, CHUNK)
            above = pl.ds(start + 1, CHUNK)
            own = pl.ds(step * CHUNK, CHUNK)
            for kind, planes in enumerate((range(levels), range(levels, levels + strips))):
                keep, north, south, to_left, twist_left, to_right, twist_right = (
                    weights[kind, number, own, :] for number in range(7)
                )
                for plane in planes:
                    centre = source[plane, here, :]
                    upper = source[plane, above, :]
                    lower = source[plane, below, :]
                    tilt = upper - lower
                    target[plane, here, :] = (
                        keep * centre
                        + (north * upper + south * lower)
                        + turn(to_left * centre + twist_left * tilt, -1)
                        + turn(to_right * centre + twist_right * tilt, 1)
                    )
            return carry

        lax.fori_loop(0, count, one_chunk, 0)

    def two_steps(number, carry):
        sweep(grid, other)
        sweep(other, grid)
        return carry

    lax.fori_loop(0, STEPS // 2, two_steps, 0)

    column = lane_ids((rows, lanes))
    inner = pl.ds(HALO, rows)
    for level in range(levels):
        edges = grid[levels + level // 2, inner, :]
        move = half * (level % 2)
        result = jnp.where(
            column < STEPS,
            turn(edges, -COLS - move),
            jnp.where(column >= lanes - STEPS, turn(edges, half + COLS - move), grid[level, inner, :]),
        )
        result = norm[level] * result
        out[level] = result
        turned[pl.ds(level, rows, stride=PAD), :] = result
    for level in range(levels, PAD):
        turned[pl.ds(level, rows, stride=PAD), :] = jnp.zeros((rows, lanes), jnp.float32)

    even = lane_ids((PAD, lanes)) % 2 == 0
    per_row = lanes // PAD

    def sample_tile(tile, carry):
        for q in range(per_row):
            block = tile * per_row + q

            def sample_group(group, found):
                found = list(found)
                for u in range(UNROLL):
                    spot = group * UNROLL + u
                    start = pl.multiple_of(cells[block, 5, spot], PAD)
                    low = turned[pl.ds(start, PAD), :].reshape(PAD // 8, 8, lanes)
                    high = turned[pl.ds(start + PAD, PAD), :].reshape(PAD // 8, 8, lanes)
                    mixed = low * row_of(lower, block * lanes + spot) + high * row_of(
                        upper, block * lanes + spot
                    )
                    move = (cells[block, 6, spot] + spot) & (lanes - 1)
                    found[u % 2] = found[u % 2] + pltpu.roll(mixed.reshape(PAD, lanes), move, 1)
                return tuple(found)

            zeros = jnp.zeros((PAD, lanes), jnp.float32)
            on_even, on_odd = lax.fori_loop(0, lanes // UNROLL, sample_group, (zeros, zeros))
            gathered[pl.ds(PAD * q, PAD), :] = jnp.where(
                even, on_even + turn(on_even, -1), on_odd + turn(on_odd, -1)
            )
        sampled[pl.ds(pl.multiple_of(tile * lanes, lanes), lanes), :] = gathered[...].T
        return carry

    lax.fori_loop(0, sampled.shape[0] // lanes, sample_tile, 0)


def row_of(table, number):
    return table[pl.ds(number, 8, stride=0), :]


def diffuse(field, coef, norm, halos, lower, upper, cells, n_lat):
    levels, rows, lanes = field.shape
    tall = rows + 2 * HALO
    whole = pl.BlockSpec(memory_space=pltpu.VMEM)
    scalars = pl.BlockSpec(memory_space=pltpu.SMEM)
    planes = levels + (levels + 1) // 2
    return pl.pallas_call(
        functools.partial(diffuse_kernel, n_lat),
        out_shape=(
            jax.ShapeDtypeStruct(field.shape, jnp.float32),
            jax.ShapeDtypeStruct((cells.shape[0] * PAD, lanes), jnp.float32),
        ),
        in_specs=[whole] * (5 + len(halos)) + [scalars],
        out_specs=(whole, whole),
        scratch_shapes=[
            pltpu.VMEM((planes, tall, lanes), jnp.float32),
            pltpu.VMEM((planes, tall, lanes), jnp.float32),
            pltpu.VMEM((2, coef.shape[0], tall, lanes), jnp.float32),
            pltpu.VMEM((2, 7, tall - 2 * EDGE, lanes), jnp.float32),
            pltpu.VMEM((rows * PAD, lanes), jnp.float32),
            pltpu.VMEM((lanes, lanes), jnp.float32),
        ],
        compiler_params=pltpu.CompilerParams(vmem_limit_bytes=30 << 20),
    )(field, coef, norm, *halos, lower, upper, cells)


def one_hot_slots(slots, q, rows):
    shape = (rows, slots.shape[1])
    number = lax.broadcasted_iota(jnp.int32, shape, 0) * (LANES // PAD) + q
    return jnp.where(number == slots, 1.0, 0.0)


def route_kernel(innovations, weights, place, owner_column, owner_row, ids, packet, slots, table):
    levels, count = innovations.shape
    total = packet.shape[0]
    same = owner_column[...] == owner_row[...]
    earlier = lax.broadcasted_iota(jnp.int32, (count, count), 0) < lax.broadcasted_iota(
        jnp.int32, (count, count), 1
    )
    rank = jnp.sum(jnp.where(jnp.logical_and(same, earlier), 1, 0), axis=0, keepdims=True)
    slot = owner_row[...] * CAPACITY + rank
    slots[...] = slot

    table[...] = jnp.zeros_like(table)
    table[pl.ds(0, levels), :] = innovations[...]
    table[pl.ds(levels, 4), :] = weights[...]
    table[pl.ds(levels + 4, 2), :] = place[...].astype(jnp.float32)
    flipped = jnp.concatenate(
        [table[:, pl.ds(start, LANES)].T for start in range(0, count, LANES)], axis=0
    )
    sent = jnp.zeros((total, LANES), jnp.float32)
    for q in range(LANES // PAD):
        moved = pltpu.roll(flipped, PAD * q, 1) if q else flipped
        sent += jnp.dot(
            one_hot_slots(slot, q, total),
            moved,
            precision=lax.Precision.HIGHEST,
            preferred_element_type=jnp.float32,
        )
    lane = lane_ids((total, LANES))
    row = lax.broadcasted_iota(jnp.int32, (total, LANES), 0)
    per_device = 2
    row_group = CAPACITY * PAD // LANES
    group = lax.rem(row // row_group, ids.shape[1] // per_device) * per_device
    first_row = lax.rem(row, row_group) == 0
    numbers = jnp.concatenate(
        [ids[...].astype(jnp.float32), jnp.zeros((1, LANES - ids.shape[1]), jnp.float32)], axis=1
    )
    for t in range(per_device):
        number = jnp.sum(jnp.where(lane == group + t, numbers, 0.0), axis=1, keepdims=True)
        spare = jnp.logical_and(first_row, lane == PAD * (t + 1) - 1)
        sent = jnp.where(spare, number, sent)
    packet[...] = sent


def route(innovations, weights, place, owners, ids, devices):
    whole = pl.BlockSpec(memory_space=pltpu.VMEM)
    count = innovations.shape[1]
    return pl.pallas_call(
        route_kernel,
        out_shape=(
            jax.ShapeDtypeStruct((devices * CAPACITY * PAD // LANES, LANES), jnp.float32),
            jax.ShapeDtypeStruct((1, count), jnp.int32),
        ),
        in_specs=[whole] * 6,
        out_specs=(whole, whole),
        scratch_shapes=[pltpu.VMEM((LANES, count), jnp.float32)],
        compiler_params=pltpu.CompilerParams(vmem_limit_bytes=16 << 20),
    )(innovations, weights, place, owners, owners.reshape(1, count), ids)


def post_kernel(source, target, held, send_sem, recv_sem, local_sem):
    n_lat, n_lon = source.shape[:2]
    lat = lax.axis_index("lat")
    lon = lax.axis_index("lon")
    across = [lax.rem(lon + step, n_lon) for step in range(1, n_lon)]
    along = [lax.rem(lat + step, n_lat) for step in range(1, n_lat)]

    barrier = pltpu.get_barrier_semaphore()
    for other in across:
        pl.semaphore_signal(barrier, inc=1, device_id=(lat, other), device_id_type=MESH)
    for other in along:
        pl.semaphore_signal(barrier, inc=1, device_id=(other, lon), device_id_type=MESH)
    own = pltpu.make_async_copy(source.at[:, lon], held.at[:, lon], local_sem)
    own.start()
    pl.semaphore_wait(barrier, n_lon + n_lat - 2)

    def push(here, there, number, device):
        copy = pltpu.make_async_remote_copy(
            src_ref=here,
            dst_ref=there,
            send_sem=send_sem.at[number],
            recv_sem=recv_sem.at[number],
            device_id=device,
            device_id_type=MESH,
        )
        copy.start()
        return copy

    copies = [
        push(source.at[:, other], held.at[:, lon], number, (lat, other))
        for number, other in enumerate(across)
    ]
    own.wait()
    for copy in copies:
        copy.wait()
    copies = [
        push(held.at[other], target.at[lat], n_lon + number, (other, lon))
        for number, other in enumerate(along)
    ]
    own = pltpu.make_async_copy(held.at[lat], target.at[lat], local_sem)
    own.start()
    own.wait()
    for copy in copies:
        copy.wait()


def post(packet, n_lat, n_lon, collective_id):
    whole = pl.BlockSpec(memory_space=pltpu.VMEM)
    blocks = packet.reshape(n_lat, n_lon, -1, LANES)
    received = pl.pallas_call(
        post_kernel,
        out_shape=jax.ShapeDtypeStruct(blocks.shape, jnp.float32),
        in_specs=[whole],
        out_specs=whole,
        scratch_shapes=[
            pltpu.VMEM(blocks.shape, jnp.float32),
            pltpu.SemaphoreType.DMA((n_lon + n_lat,)),
            pltpu.SemaphoreType.DMA((n_lon + n_lat,)),
            pltpu.SemaphoreType.DMA,
        ],
        compiler_params=pltpu.CompilerParams(
            collective_id=collective_id, has_side_effects=True, vmem_limit_bytes=4 << 20
        ),
    )(blocks)
    return received.reshape(packet.shape)


def spread_kernel(
    levels, packet, observed, lower, upper, cells_out, turned, other, cells, sem
):
    total, lanes = packet.shape
    per_row = lanes // PAD
    tiles = total // lanes
    level_lane = PAD - 8
    sublane = lax.broadcasted_iota(jnp.int32, (8, lanes), 0)
    for tile in range(tiles):
        flipped = packet[pl.ds(tile * lanes, lanes), :].T
        turned[pl.ds(tile * lanes, lanes), :] = flipped
        for q in range(per_row):
            last = flipped[PAD * q + level_lane : PAD * (q + 1)].astype(jnp.int32)
            last = jnp.where(sublane == 5, last * PAD, jnp.where(sublane == 6, lanes - last, last))
            cells_out[tile * per_row + q] = last
    copy = pltpu.make_async_copy(cells_out, cells, sem)
    copy.start()

    lane = lane_ids((lanes, lanes)).astype(jnp.float32)
    for tile in range(tiles):
        rows = packet[pl.ds(tile * lanes, lanes), :]
        for q in range(per_row):
            first, second, third, fourth, row, column = (
                jnp.broadcast_to(rows[:, n : n + 1], (lanes, lanes))
                for n in range(PAD * q + level_lane + 1, PAD * q + level_lane + 7)
            )
            here = lane == column
            beside = lane == column + 1.0
            block = pl.ds((tile * per_row + q) * lanes, lanes)
            lower[block, :] = jnp.where(here, first, jnp.where(beside, second, 0.0))
            upper[block, :] = jnp.where(here, third, jnp.where(beside, fourth, 0.0))

    is_level = lax.broadcasted_iota(jnp.int32, (PAD, lanes), 0) < levels
    parts = (observed, other)
    for part in parts:
        part[...] = jnp.zeros_like(part)
    copy.wait()

    def spread_block(block, carry):
        values = jnp.where(is_level, turned[pl.ds(pl.multiple_of(block * PAD, PAD), PAD), :], 0.0)

        def spread_group(group, carry):
            moved = pltpu.roll(values, lax.rem(lanes - group * UNROLL, lanes), 1)
            for u in range(UNROLL):
                spot = group * UNROLL + u
                value = jnp.broadcast_to(moved[:, u : u + 1], (PAD, lanes)).reshape(
                    PAD // 8, 8, lanes
                )
                added = jnp.concatenate(
                    [
                        (value * row_of(table, block * lanes + spot)).reshape(PAD, lanes)
                        for table in (lower, upper)
                    ],
                    axis=0,
                )
                where = pl.ds(pl.multiple_of(cells[block, 5, spot], PAD), 2 * PAD)
                part = parts[u % len(parts)]
                part[where, :] = part[where, :] + added
            return carry

        lax.fori_loop(0, lanes // UNROLL, spread_group, 0)
        return carry

    lax.fori_loop(0, tiles * per_row, spread_block, 0)
    observed[...] = observed[...] + other[...]


def spread(packet, levels, rows):
    total, lanes = packet.shape
    whole = pl.BlockSpec(memory_space=pltpu.VMEM)
    blocks = total // PAD
    masks = jax.ShapeDtypeStruct((blocks * lanes, lanes), jnp.float32)
    return pl.pallas_call(
        functools.partial(spread_kernel, levels),
        out_shape=(
            jax.ShapeDtypeStruct((rows * PAD, lanes), jnp.float32),
            masks,
            masks,
            jax.ShapeDtypeStruct((blocks, 8, lanes), jnp.int32),
        ),
        in_specs=[whole],
        out_specs=(whole,) * 4,
        scratch_shapes=[
            pltpu.VMEM(packet.shape, jnp.float32),
            pltpu.VMEM((rows * PAD, lanes), jnp.float32),
            pltpu.SMEM((blocks, 8, lanes), jnp.int32),
            pltpu.SemaphoreType.DMA,
        ],
        compiler_params=pltpu.CompilerParams(vmem_limit_bytes=12 << 20),
    )(packet)


def combine_kernel(cells, observed, tiles, norm, field):
    slots, levels, depth, lanes = tiles.shape
    n_lon = lax.axis_size("lon")
    per_device = slots // n_lon
    per_row = lanes // PAD
    row_group = CAPACITY * PAD // lanes
    base = lax.axis_index("lat") * n_lon

    def one_tile(slot, carry):
        at = (base + slot // per_device) * row_group
        block = (at // lanes) * per_row + lax.rem(slot, per_device)
        row = pl.multiple_of(cells[block, 7, lax.rem(at, lanes)] * depth, depth)
        rows = pl.ds(row, depth)
        for level in range(levels):
            seen = observed[pl.ds(row * PAD + level, depth, stride=PAD), :]
            field[level, rows, :] = norm[level, rows, :] * (seen + tiles[slot, level])
        return carry

    lax.fori_loop(0, slots, one_tile, 0)


def combine(cells, observed, tiles, norm):
    whole = pl.BlockSpec(memory_space=pltpu.VMEM)
    return pl.pallas_call(
        combine_kernel,
        out_shape=jax.ShapeDtypeStruct(norm.shape, jnp.float32),
        in_specs=[pl.BlockSpec(memory_space=pltpu.SMEM)] + [whole] * 3,
        out_specs=whole,
        compiler_params=pltpu.CompilerParams(vmem_limit_bytes=8 << 20),
    )(cells, observed, tiles, norm)


def collect_kernel(levels, returned, slots, out):
    total, lanes = returned.shape
    flipped = jnp.concatenate(
        [returned[pl.ds(start, lanes), :].T for start in range(0, total, lanes)], axis=1
    )
    values = jnp.zeros((PAD, slots.shape[1]), jnp.float32)
    for q in range(lanes // PAD):
        values += jnp.dot(
            flipped[PAD * q : PAD * (q + 1)],
            one_hot_slots(slots[...], q, total),
            precision=lax.Precision.HIGHEST,
            preferred_element_type=jnp.float32,
        )
    out[...] = values[:levels]


def collect(returned, slots, levels):
    whole = pl.BlockSpec(memory_space=pltpu.VMEM)
    return pl.pallas_call(
        functools.partial(collect_kernel, levels),
        out_shape=jax.ShapeDtypeStruct((levels, slots.shape[1]), jnp.float32),
        in_specs=[whole] * 2,
        out_specs=whole,
        compiler_params=pltpu.CompilerParams(vmem_limit_bytes=16 << 20),
    )(returned, slots)


def on_device(
    innovations,
    owners,
    prof_row,
    prof_col,
    interp_weights,
    model_tiles,
    model_ids,
    face_x,
    face_y,
    cross_term,
    wet_mask,
    norm_factor,
):
    levels, rows, lanes = norm_factor.shape
    n_lat = lax.axis_size("lat")
    n_lon = lax.axis_size("lon")
    place = jnp.stack([prof_row, prof_col])
    packet, slots = route(innovations, interp_weights, place, owners, model_ids, n_lat * n_lon)
    packet = post(packet, n_lat, n_lon, 1)
    tiles, packet = lax.optimization_barrier((jnp.transpose(model_tiles, (1, 0, 2, 3)), packet))
    tiles = lax.all_to_all(tiles, "lon", split_axis=0, concat_axis=0, tiled=True)
    observed, lower, upper, cells = spread(packet, levels, rows)
    field = combine(cells, observed, tiles, norm_factor)
    coef = jnp.stack([face_x, face_y, cross_term, wet_mask.astype(jnp.float32)])
    halos = exchange(field, coef, n_lat, n_lon)
    smoothed, sampled = diffuse(
        field, coef, norm_factor, halos, lower, upper, cells, n_lat
    )
    returned = post(sampled, n_lat, n_lon, 2)
    profile_values = collect(returned, slots, levels)
    return (smoothed, profile_values)


def solution(mesh):
    in_specs = (
        P(None, ("lat", "lon")),
        P(("lat", "lon"), None),
        P(("lat", "lon")),
        P(("lat", "lon")),
        P(None, ("lat", "lon")),
        P(None, ("lat", "lon"), None, None),
        P(None, ("lat", "lon")),
        P("lat", "lon"),
        P("lat", "lon"),
        P("lat", "lon"),
        P("lat", "lon"),
        P(None, "lat", "lon"),
    )
    out_specs = (P(None, "lat", "lon"), P(None, ("lat", "lon")))
    return jax.shard_map(
        on_device, mesh=mesh, in_specs=in_specs, out_specs=out_specs, check_vma=False
    )
```

```python
import functools

import jax
import jax.numpy as jnp
from jax import lax
from jax.experimental import pallas as pl
from jax.experimental.pallas import tpu as pltpu
from jax.sharding import PartitionSpec as P

STEPS = 10
CAPACITY = 8
PAD = 32
UNROLL = 32
HALO = 16
LANES = 128
COLS = 12
PAIRS = 6
COEF_PAIRS = 5
EARLY = 10
CHUNK = 40
EDGE = 4
MESH = pl.DeviceIdType.MESH


def lane_ids(shape):
    return lax.broadcasted_iota(jnp.int32, shape, len(shape) - 1)


def within(lane, start, width):
    start = start % LANES
    return jnp.logical_and(lane >= start, lane < start + width)


def turn(values, shift):
    shift = shift % LANES
    return pltpu.roll(values, shift, 1) if shift else values


def packed_columns(plane_of, planes, rows, cols, first_pair, pairs):
    lane = lane_ids((rows, LANES))
    low = jnp.zeros((rows, LANES), jnp.float32)
    high = jnp.zeros((rows, LANES), jnp.float32)
    for k in range(pairs):
        for half in range(2):
            plane = 2 * (first_pair + k) + half
            if plane >= planes:
                continue
            shift = cols * k + (LANES // 2) * half
            values = turn(plane_of(plane), shift)
            low = jnp.where(within(lane, shift, cols), values, low)
            high = jnp.where(within(lane, LANES - cols + shift, cols), values, high)
    return low, high


def strip_plane(first, second, east, west, k, cols, inside):
    half = LANES // 2
    lane = lane_ids(first.shape)
    upper_half = lane >= half
    lane = lane % half
    west_side = lane < half // 2
    low = jnp.where(west_side, turn(first, COLS), turn(first, half - COLS))
    high = jnp.where(west_side, turn(second, COLS + half), turn(second, -COLS))
    own = jnp.where(upper_half, high, low)
    east = jnp.where(
        jnp.logical_and(inside, within(lane, half - COLS, cols)),
        turn(east, half - COLS - cols * k),
        0.0,
    )
    west = jnp.where(
        jnp.logical_and(inside, within(lane, COLS - cols, cols)), turn(west, COLS - cols * k), east
    )
    return jnp.where(jnp.logical_and(lane >= COLS, lane < half - COLS), own, west)


def inside_domain(shape, rows, has_south, has_north):
    row = lax.broadcasted_iota(jnp.int32, shape, 0)
    return jnp.logical_and(
        jnp.logical_or(row >= HALO, has_south), jnp.logical_or(row < HALO + rows, has_north)
    )


def neighbours(n_lat, n_lon):
    lat = lax.axis_index("lat")
    lon = lax.axis_index("lon")
    up = lax.rem(lat + 1, n_lat)
    down = lax.rem(lat + n_lat - 1, n_lat)
    right = lax.rem(lon + 1, n_lon)
    left = lax.rem(lon + n_lon - 1, n_lon)
    return lat, lon, up, down, right, left


def exchange_kernel(
    n_lat,
    n_lon,
    field,
    west_cols,
    east_cols,
    south_rows,
    north_rows,
    pack_first,
    pack_last,
    pack_low,
    pack_high,
    send_sem,
    recv_sem,
):
    lat, lon, up, down, right, left = neighbours(n_lat, n_lon)
    levels, rows = field.shape[:2]

    barrier = pltpu.get_barrier_semaphore()
    for there in (
        (lat, right),
        (lat, left),
        (up, lon),
        (down, lon),
        (up, right),
        (up, left),
        (down, right),
        (down, left),
    ):
        pl.semaphore_signal(barrier, inc=1, device_id=there, device_id_type=MESH)

    copies = []

    def send(source, target, there):
        number = len(copies)
        copy = pltpu.make_async_remote_copy(
            src_ref=source,
            dst_ref=target,
            send_sem=send_sem.at[number],
            recv_sem=recv_sem.at[number],
            device_id=there,
            device_id_type=MESH,
        )
        copy.start()
        copies.append(copy)

    for level in range(levels):
        at = pl.ds(STEPS * level, STEPS)
        pack_high[at, :] = field[level, pl.ds(rows - STEPS, STEPS), :]
        pack_low[at, :] = field[level, pl.ds(0, STEPS), :]
    pl.semaphore_wait(barrier, 8)
    send(pack_high, south_rows, (up, lon))
    send(pack_low, north_rows, (down, lon))
    for tile in range(pack_first.shape[0]):
        low, high = packed_columns(
            lambda plane: field[plane], levels, rows, STEPS, tile * PAIRS, PAIRS
        )
        pack_first[tile] = low
        pack_last[tile] = high

    first = pl.ds(0, HALO)
    last = pl.ds(rows - HALO, HALO)
    own = pl.ds(HALO, rows)
    above = pl.ds(HALO + rows, HALO)
    send(pack_last, west_cols.at[:, own, :], (lat, right))
    send(pack_first, east_cols.at[:, own, :], (lat, left))
    send(pack_last.at[:, last, :], west_cols.at[:, first, :], (up, right))
    send(pack_first.at[:, last, :], east_cols.at[:, first, :], (up, left))
    send(pack_last.at[:, first, :], west_cols.at[:, above, :], (down, right))
    send(pack_first.at[:, first, :], east_cols.at[:, above, :], (down, left))
    for copy in copies:
        copy.wait()


def exchange(field, n_lat, n_lon):
    levels, rows, lanes = field.shape
    tiles = -(-((levels + 1) // 2) // PAIRS)
    edge = -(-levels * STEPS // 8) * 8
    whole = pl.BlockSpec(memory_space=pltpu.VMEM)
    packed = jax.ShapeDtypeStruct((tiles, rows + 2 * HALO, lanes), jnp.float32)
    edges = jax.ShapeDtypeStruct((edge, lanes), jnp.float32)
    return pl.pallas_call(
        functools.partial(exchange_kernel, n_lat, n_lon),
        out_shape=(packed, packed, edges, edges),
        in_specs=[whole],
        out_specs=[whole] * 4,
        scratch_shapes=[
            pltpu.VMEM((tiles, rows, lanes), jnp.float32),
            pltpu.VMEM((tiles, rows, lanes), jnp.float32),
            pltpu.VMEM((edge, lanes), jnp.float32),
            pltpu.VMEM((edge, lanes), jnp.float32),
            pltpu.SemaphoreType.DMA((8,)),
            pltpu.SemaphoreType.DMA((8,)),
        ],
        compiler_params=pltpu.CompilerParams(
            collective_id=0, has_side_effects=True, vmem_limit_bytes=8 << 20
        ),
    )(field)


def prepare_kernel(
    n_lat, coef, west_cols, east_cols, south_coef, north_coef, weights, raw
):
    rows, lanes = coef.shape[1:]
    tall = rows + 2 * HALO
    half = lanes // 2
    has_south = lax.axis_index("lat") > 0
    has_north = lax.axis_index("lat") < n_lat - 1
    inside = inside_domain((tall, lanes), rows, has_south, has_north)
    upper_half = lane_ids((tall, lanes)) >= half
    for n in range(coef.shape[0]):
        plane = jnp.concatenate(
            [
                jnp.where(has_south, south_coef[n], 0.0),
                coef[n],
                jnp.where(has_north, north_coef[n], 0.0),
            ],
            axis=0,
        )
        raw[0, n] = plane
        both = strip_plane(plane, plane, east_cols[...], west_cols[...], n // 2, COLS, inside)
        mirrored = turn(both, half)
        raw[1, n] = jnp.where(upper_half, *((mirrored, both) if n % 2 == 0 else (both, mirrored)))

    def make_weights(step, carry):
        start = EDGE + step * CHUNK
        here = pl.ds(start, CHUNK)
        below = pl.ds(start - 1, CHUNK)
        above = pl.ds(start + 1, CHUNK)
        for kind in range(2):
            wet = raw[kind, 3, here, :]
            east = raw[kind, 0, here, :] * wet * turn(wet, -1)
            west = turn(east, 1)
            twist = 0.25 * raw[kind, 2, here, :] * wet
            north = raw[kind, 1, here, :] * wet * raw[kind, 3, above, :]
            south = raw[kind, 1, below, :] * raw[kind, 3, below, :] * wet
            keep = 1.0 - (east + west + north + south)
            for number, value in enumerate(
                (keep, north, south, west, turn(twist, 1), east, -turn(twist, -1))
            ):
                weights[kind, number, pl.ds(step * CHUNK, CHUNK), :] = value
        return carry

    lax.fori_loop(0, (tall - 2 * EDGE) // CHUNK, make_weights, 0)


def prepare(coef, halos, n_lat):
    count, rows, lanes = coef.shape
    tall = rows + 2 * HALO
    whole = pl.BlockSpec(memory_space=pltpu.VMEM)
    return pl.pallas_call(
        functools.partial(prepare_kernel, n_lat),
        out_shape=jax.ShapeDtypeStruct((2, 7, tall - 2 * EDGE, lanes), jnp.float32),
        in_specs=[whole] * 5,
        out_specs=whole,
        scratch_shapes=[pltpu.VMEM((2, count, tall, lanes), jnp.float32)],
        compiler_params=pltpu.CompilerParams(vmem_limit_bytes=8 << 20),
    )(coef, *halos)


def diffuse_kernel(
    n_lat,
    field,
    norm,
    west_cols,
    east_cols,
    south_rows,
    north_rows,
    weights,
    lower,
    upper,
    cells,
    out,
    sampled,
    grid,
    other,
    turned,
    gathered,
):
    levels, rows, lanes = field.shape
    tall = rows + 2 * HALO
    half = lanes // 2
    strips = (levels + 1) // 2
    has_south = lax.axis_index("lat") > 0
    has_north = lax.axis_index("lat") < n_lat - 1
    inside = inside_domain((tall, lanes), rows, has_south, has_north)

    for level in range(levels):
        at = pl.ds(STEPS * level, STEPS)
        grid[level, pl.ds(0, HALO), :] = jnp.zeros((HALO, lanes), jnp.float32)
        grid[level, pl.ds(HALO + rows, HALO), :] = jnp.zeros((HALO, lanes), jnp.float32)
        grid[level, pl.ds(HALO - STEPS, STEPS), :] = jnp.where(has_south, south_rows[at, :], 0.0)
        grid[level, pl.ds(HALO, rows), :] = field[level]
        grid[level, pl.ds(HALO + rows, STEPS), :] = jnp.where(has_north, north_rows[at, :], 0.0)
    for pair in range(strips):
        tile, k = divmod(pair, PAIRS)
        grid[levels + pair] = strip_plane(
            grid[2 * pair],
            grid[min(2 * pair + 1, levels - 1)],
            east_cols[tile],
            west_cols[tile],
            k,
            STEPS,
            inside,
        )

    count = (tall - 2 * EDGE) // CHUNK

    def sweep(source, target):
        def one_chunk(step, carry):
            start = EDGE + step * CHUNK
            here = pl.ds(start, CHUNK)
            below = pl.ds(start - 1, CHUNK)
            above = pl.ds(start + 1, CHUNK)
            own = pl.ds(step * CHUNK, CHUNK)
            for kind, planes in enumerate((range(levels), range(levels, levels + strips))):
                keep, north, south, to_left, twist_left, to_right, twist_right = (
                    weights[kind, number, own, :] for number in range(7)
                )
                for plane in planes:
                    centre = source[plane, here, :]
                    upper = source[plane, above, :]
                    lower = source[plane, below, :]
                    tilt = upper - lower
                    target[plane, here, :] = (
                        keep * centre
                        + (north * upper + south * lower)
                        + turn(to_left * centre + twist_left * tilt, -1)
                        + turn(to_right * centre + twist_right * tilt, 1)
                    )
            return carry

        lax.fori_loop(0, count, one_chunk, 0)

    def two_steps(number, carry):
        sweep(grid, other)
        sweep(other, grid)
        return carry

    lax.fori_loop(0, STEPS // 2, two_steps, 0)

    column = lane_ids((rows, lanes))
    inner = pl.ds(HALO, rows)
    for level in range(levels):
        edges = grid[levels + level // 2, inner, :]
        move = half * (level % 2)
        result = jnp.where(
            column < STEPS,
            turn(edges, -COLS - move),
            jnp.where(column >= lanes - STEPS, turn(edges, half + COLS - move), grid[level, inner, :]),
        )
        result = norm[level] * result
        out[level] = result
        turned[pl.ds(level, rows, stride=PAD), :] = result
    for level in range(levels, PAD):
        turned[pl.ds(level, rows, stride=PAD), :] = jnp.zeros((rows, lanes), jnp.float32)

    even = lane_ids((PAD, lanes)) % 2 == 0
    per_row = lanes // PAD

    def sample_tile(tile, carry):
        for q in range(per_row):
            block = tile * per_row + q

            def sample_group(group, found):
                found = list(found)
                for u in range(UNROLL):
                    spot = group * UNROLL + u
                    start = pl.multiple_of(cells[block, 5, spot], PAD)
                    low = turned[pl.ds(start, PAD), :].reshape(PAD // 8, 8, lanes)
                    high = turned[pl.ds(start + PAD, PAD), :].reshape(PAD // 8, 8, lanes)
                    mixed = low * row_of(lower, block * lanes + spot) + high * row_of(
                        upper, block * lanes + spot
                    )
                    move = (cells[block, 6, spot] + spot) & (lanes - 1)
                    found[u % 2] = found[u % 2] + pltpu.roll(mixed.reshape(PAD, lanes), move, 1)
                return tuple(found)

            zeros = jnp.zeros((PAD, lanes), jnp.float32)
            on_even, on_odd = lax.fori_loop(0, lanes // UNROLL, sample_group, (zeros, zeros))
            gathered[pl.ds(PAD * q, PAD), :] = jnp.where(
                even, on_even + turn(on_even, -1), on_odd + turn(on_odd, -1)
            )
        sampled[pl.ds(pl.multiple_of(tile * lanes, lanes), lanes), :] = gathered[...].T
        return carry

    lax.fori_loop(0, sampled.shape[0] // lanes, sample_tile, 0)


def row_of(table, number):
    return table[pl.ds(number, 8, stride=0), :]


def diffuse(field, norm, halos, weights, lower, upper, cells, n_lat):
    levels, rows, lanes = field.shape
    tall = rows + 2 * HALO
    whole = pl.BlockSpec(memory_space=pltpu.VMEM)
    scalars = pl.BlockSpec(memory_space=pltpu.SMEM)
    planes = levels + (levels + 1) // 2
    return pl.pallas_call(
        functools.partial(diffuse_kernel, n_lat),
        out_shape=(
            jax.ShapeDtypeStruct(field.shape, jnp.float32),
            jax.ShapeDtypeStruct((cells.shape[0] * PAD, lanes), jnp.float32),
        ),
        in_specs=[whole] * 9 + [scalars],
        out_specs=(whole, whole),
        scratch_shapes=[
            pltpu.VMEM((planes, tall, lanes), jnp.float32),
            pltpu.VMEM((planes, tall, lanes), jnp.float32),
            pltpu.VMEM((rows * PAD, lanes), jnp.float32),
            pltpu.VMEM((lanes, lanes), jnp.float32),
        ],
        compiler_params=pltpu.CompilerParams(vmem_limit_bytes=24 << 20),
    )(field, norm, *halos, weights, lower, upper, cells)


def one_hot_slots(slots, q, rows):
    shape = (rows, slots.shape[1])
    number = lax.broadcasted_iota(jnp.int32, shape, 0) * (LANES // PAD) + q
    return jnp.where(number == slots, 1.0, 0.0)


def route_kernel(innovations, weights, place, owner_column, owner_row, ids, packet, slots, table):
    levels, count = innovations.shape
    total = packet.shape[0]
    same = owner_column[...] == owner_row[...]
    earlier = lax.broadcasted_iota(jnp.int32, (count, count), 0) < lax.broadcasted_iota(
        jnp.int32, (count, count), 1
    )
    rank = jnp.sum(jnp.where(jnp.logical_and(same, earlier), 1, 0), axis=0, keepdims=True)
    slot = owner_row[...] * CAPACITY + rank
    slots[...] = slot

    table[...] = jnp.zeros_like(table)
    table[pl.ds(0, levels), :] = innovations[...]
    table[pl.ds(levels, 4), :] = weights[...]
    table[pl.ds(levels + 4, 2), :] = place[...].astype(jnp.float32)
    flipped = jnp.concatenate(
        [table[:, pl.ds(start, LANES)].T for start in range(0, count, LANES)], axis=0
    )
    sent = jnp.zeros((total, LANES), jnp.float32)
    for q in range(LANES // PAD):
        moved = pltpu.roll(flipped, PAD * q, 1) if q else flipped
        sent += jnp.dot(
            one_hot_slots(slot, q, total),
            moved,
            precision=lax.Precision.HIGHEST,
            preferred_element_type=jnp.float32,
        )
    lane = lane_ids((total, LANES))
    row = lax.broadcasted_iota(jnp.int32, (total, LANES), 0)
    per_device = 2
    row_group = CAPACITY * PAD // LANES
    group = lax.rem(row // row_group, ids.shape[1] // per_device) * per_device
    first_row = lax.rem(row, row_group) == 0
    numbers = jnp.concatenate(
        [ids[...].astype(jnp.float32), jnp.zeros((1, LANES - ids.shape[1]), jnp.float32)], axis=1
    )
    for t in range(per_device):
        number = jnp.sum(jnp.where(lane == group + t, numbers, 0.0), axis=1, keepdims=True)
        spare = jnp.logical_and(first_row, lane == PAD * (t + 1) - 1)
        sent = jnp.where(spare, number, sent)
    packet[...] = sent


def route(innovations, weights, place, owners, ids, devices):
    whole = pl.BlockSpec(memory_space=pltpu.VMEM)
    count = innovations.shape[1]
    return pl.pallas_call(
        route_kernel,
        out_shape=(
            jax.ShapeDtypeStruct((devices * CAPACITY * PAD // LANES, LANES), jnp.float32),
            jax.ShapeDtypeStruct((1, count), jnp.int32),
        ),
        in_specs=[whole] * 6,
        out_specs=(whole, whole),
        scratch_shapes=[pltpu.VMEM((LANES, count), jnp.float32)],
        compiler_params=pltpu.CompilerParams(vmem_limit_bytes=16 << 20),
    )(innovations, weights, place, owners, owners.reshape(1, count), ids)


def post_kernel(has_coef, source, *refs):
    if has_coef:
        coef, tiles, target, west_cols, east_cols, south_coef, north_coef, late = refs[:8]
        held, send_sem, recv_sem, local_sem, pack_first, pack_last, late_sem = refs[8:]
    else:
        target, held, send_sem, recv_sem, local_sem = refs
    n_lat, n_lon = source.shape[:2]
    lat, lon, up, down, right, left = neighbours(n_lat, n_lon)
    across = [lax.rem(lon + step, n_lon) for step in range(1, n_lon)]
    along = [lax.rem(lat + step, n_lat) for step in range(1, n_lat)]
    corners = [(up, right), (up, left), (down, right), (down, left)] if has_coef else []

    barrier = pltpu.get_barrier_semaphore()
    for other in across:
        pl.semaphore_signal(barrier, inc=1, device_id=(lat, other), device_id_type=MESH)
    for other in along:
        pl.semaphore_signal(barrier, inc=1, device_id=(other, lon), device_id_type=MESH)
    for there in corners:
        pl.semaphore_signal(barrier, inc=1, device_id=there, device_id_type=MESH)
    own = pltpu.make_async_copy(source.at[:, lon], held.at[:, lon], local_sem)
    own.start()
    moves = []
    if has_coef:
        for level in range(late.shape[1]):
            move = pltpu.make_async_copy(
                tiles.at[EARLY + level], late.at[:, level], late_sem.at[level]
            )
            move.start()
            moves.append(move)
        rows = coef.shape[1]
        low, high = packed_columns(
            lambda plane: coef[plane], coef.shape[0], rows, COLS, 0, COEF_PAIRS
        )
        pack_first[...] = low
        pack_last[...] = high
    pl.semaphore_wait(barrier, n_lon + n_lat - 2 + len(corners))

    def push(here, there, number, device):
        copy = pltpu.make_async_remote_copy(
            src_ref=here,
            dst_ref=there,
            send_sem=send_sem.at[number],
            recv_sem=recv_sem.at[number],
            device_id=device,
            device_id_type=MESH,
        )
        copy.start()
        return copy

    copies = [
        push(source.at[:, other], held.at[:, lon], number, (lat, other))
        for number, other in enumerate(across)
    ]
    edges = []
    if has_coef:
        first = pl.ds(0, HALO)
        last = pl.ds(rows - HALO, HALO)
        middle = pl.ds(HALO, rows)
        above = pl.ds(HALO + rows, HALO)
        for here, there, device in (
            (coef.at[:, last, :], south_coef, (up, lon)),
            (coef.at[:, first, :], north_coef, (down, lon)),
            (pack_last, west_cols.at[middle, :], (lat, right)),
            (pack_first, east_cols.at[middle, :], (lat, left)),
            (pack_last.at[last, :], west_cols.at[first, :], (up, right)),
            (pack_first.at[last, :], east_cols.at[first, :], (up, left)),
            (pack_last.at[first, :], west_cols.at[above, :], (down, right)),
            (pack_first.at[first, :], east_cols.at[above, :], (down, left)),
        ):
            edges.append(push(here, there, n_lon + n_lat + len(edges), device))
    own.wait()
    for copy in copies:
        copy.wait()
    copies = [
        push(held.at[other], target.at[lat], n_lon + number, (other, lon))
        for number, other in enumerate(along)
    ]
    own = pltpu.make_async_copy(held.at[lat], target.at[lat], local_sem)
    own.start()
    own.wait()
    for copy in copies + edges + moves:
        copy.wait()


def post(packet, n_lat, n_lon, collective_id, coef=None, tiles=None):
    whole = pl.BlockSpec(memory_space=pltpu.VMEM)
    anywhere = pl.BlockSpec(memory_space=pl.ANY)
    blocks = packet.reshape(n_lat, n_lon, -1, LANES)
    has_coef = coef is not None
    sems = n_lon + n_lat + 8 * has_coef
    out_shape = [jax.ShapeDtypeStruct(blocks.shape, jnp.float32)]
    scratch = [
        pltpu.VMEM(blocks.shape, jnp.float32),
        pltpu.SemaphoreType.DMA((sems,)),
        pltpu.SemaphoreType.DMA((sems,)),
        pltpu.SemaphoreType.DMA,
    ]
    operands, in_specs, out_specs = [blocks], [whole], [whole]
    if has_coef:
        count, rows, lanes = coef.shape
        levels, slots, depth, _ = tiles.shape
        packed = jax.ShapeDtypeStruct((rows + 2 * HALO, lanes), jnp.float32)
        edge = jax.ShapeDtypeStruct((count, HALO, lanes), jnp.float32)
        late = jax.ShapeDtypeStruct((slots, levels - EARLY, depth, lanes), jnp.float32)
        out_shape += [packed, packed, edge, edge, late]
        scratch += [
            pltpu.VMEM((rows, lanes), jnp.float32),
            pltpu.VMEM((rows, lanes), jnp.float32),
            pltpu.SemaphoreType.DMA((levels - EARLY,)),
        ]
        operands += [coef, tiles]
        in_specs += [whole, anywhere]
        out_specs += [whole] * 4 + [anywhere]
    received, *rest = pl.pallas_call(
        functools.partial(post_kernel, has_coef),
        out_shape=out_shape,
        in_specs=in_specs,
        out_specs=out_specs,
        scratch_shapes=scratch,
        compiler_params=pltpu.CompilerParams(
            collective_id=collective_id, has_side_effects=True, vmem_limit_bytes=4 << 20
        ),
    )(*operands)
    return (received.reshape(packet.shape), *rest)


def spread_kernel(
    levels, packet, seen, lower, upper, cells_out, turned, observed, other, cells, sem
):
    total, lanes = packet.shape
    per_row = lanes // PAD
    tiles = total // lanes
    level_lane = PAD - 8
    sublane = lax.broadcasted_iota(jnp.int32, (8, lanes), 0)
    for tile in range(tiles):
        flipped = packet[pl.ds(tile * lanes, lanes), :].T
        turned[pl.ds(tile * lanes, lanes), :] = flipped
        for q in range(per_row):
            last = flipped[PAD * q + level_lane : PAD * (q + 1)].astype(jnp.int32)
            last = jnp.where(sublane == 5, last * PAD, jnp.where(sublane == 6, lanes - last, last))
            cells_out[tile * per_row + q] = last
    copy = pltpu.make_async_copy(cells_out, cells, sem)
    copy.start()

    lane = lane_ids((lanes, lanes)).astype(jnp.float32)
    for tile in range(tiles):
        rows = packet[pl.ds(tile * lanes, lanes), :]
        for q in range(per_row):
            first, second, third, fourth, row, column = (
                jnp.broadcast_to(rows[:, n : n + 1], (lanes, lanes))
                for n in range(PAD * q + level_lane + 1, PAD * q + level_lane + 7)
            )
            here = lane == column
            beside = lane == column + 1.0
            block = pl.ds((tile * per_row + q) * lanes, lanes)
            lower[block, :] = jnp.where(here, first, jnp.where(beside, second, 0.0))
            upper[block, :] = jnp.where(here, third, jnp.where(beside, fourth, 0.0))

    is_level = lax.broadcasted_iota(jnp.int32, (PAD, lanes), 0) < levels
    parts = (observed, other)
    for part in parts:
        part[...] = jnp.zeros_like(part)
    copy.wait()

    def spread_block(block, carry):
        values = jnp.where(is_level, turned[pl.ds(pl.multiple_of(block * PAD, PAD), PAD), :], 0.0)

        def spread_group(group, carry):
            moved = pltpu.roll(values, lax.rem(lanes - group * UNROLL, lanes), 1)
            for u in range(UNROLL):
                spot = group * UNROLL + u
                value = jnp.broadcast_to(moved[:, u : u + 1], (PAD, lanes)).reshape(
                    PAD // 8, 8, lanes
                )
                added = jnp.concatenate(
                    [
                        (value * row_of(table, block * lanes + spot)).reshape(PAD, lanes)
                        for table in (lower, upper)
                    ],
                    axis=0,
                )
                where = pl.ds(pl.multiple_of(cells[block, 5, spot], PAD), 2 * PAD)
                part = parts[u % len(parts)]
                part[where, :] = part[where, :] + added
            return carry

        lax.fori_loop(0, lanes // UNROLL, spread_group, 0)
        return carry

    lax.fori_loop(0, tiles * per_row, spread_block, 0)
    rows = seen.shape[1]
    for level in range(levels):
        at = pl.ds(level, rows, stride=PAD)
        seen[level] = observed[at, :] + other[at, :]


def spread(packet, levels, rows):
    total, lanes = packet.shape
    whole = pl.BlockSpec(memory_space=pltpu.VMEM)
    blocks = total // PAD
    masks = jax.ShapeDtypeStruct((blocks * lanes, lanes), jnp.float32)
    return pl.pallas_call(
        functools.partial(spread_kernel, levels),
        out_shape=(
            jax.ShapeDtypeStruct((levels, rows, lanes), jnp.float32),
            masks,
            masks,
            jax.ShapeDtypeStruct((blocks, 8, lanes), jnp.int32),
        ),
        in_specs=[whole],
        out_specs=(whole,) * 4,
        scratch_shapes=[
            pltpu.VMEM(packet.shape, jnp.float32),
            pltpu.VMEM((rows * PAD, lanes), jnp.float32),
            pltpu.VMEM((rows * PAD, lanes), jnp.float32),
            pltpu.SMEM((blocks, 8, lanes), jnp.int32),
            pltpu.SemaphoreType.DMA,
        ],
        compiler_params=pltpu.CompilerParams(vmem_limit_bytes=12 << 20),
    )(packet)


def combine_kernel(cells, seen, early, late, norm, field):
    slots, _, depth, lanes = early.shape
    n_lon = lax.axis_size("lon")
    per_device = slots // n_lon
    per_row = lanes // PAD
    row_group = CAPACITY * PAD // lanes
    base = lax.axis_index("lat") * n_lon

    def one_tile(slot, carry):
        at = (base + slot // per_device) * row_group
        block = (at // lanes) * per_row + lax.rem(slot, per_device)
        rows = pl.ds(pl.multiple_of(cells[block, 7, lax.rem(at, lanes)] * depth, depth), depth)
        for part, tiles in ((pl.ds(0, early.shape[1]), early), (pl.ds(early.shape[1], late.shape[1]), late)):
            field[part, rows, :] = norm[part, rows, :] * (seen[part, rows, :] + tiles[slot])
        return carry

    lax.fori_loop(0, slots, one_tile, 0)


def combine(cells, seen, early, late, norm):
    whole = pl.BlockSpec(memory_space=pltpu.VMEM)
    return pl.pallas_call(
        combine_kernel,
        out_shape=jax.ShapeDtypeStruct(norm.shape, jnp.float32),
        in_specs=[pl.BlockSpec(memory_space=pltpu.SMEM)] + [whole] * 4,
        out_specs=whole,
        compiler_params=pltpu.CompilerParams(vmem_limit_bytes=8 << 20),
    )(cells, seen, early, late, norm)


def collect_kernel(levels, returned, slots, out):
    total, lanes = returned.shape
    flipped = jnp.concatenate(
        [returned[pl.ds(start, lanes), :].T for start in range(0, total, lanes)], axis=1
    )
    values = jnp.zeros((PAD, slots.shape[1]), jnp.float32)
    for q in range(lanes // PAD):
        values += jnp.dot(
            flipped[PAD * q : PAD * (q + 1)],
            one_hot_slots(slots[...], q, total),
            precision=lax.Precision.HIGHEST,
            preferred_element_type=jnp.float32,
        )
    out[...] = values[:levels]


def collect(returned, slots, levels):
    whole = pl.BlockSpec(memory_space=pltpu.VMEM)
    return pl.pallas_call(
        functools.partial(collect_kernel, levels),
        out_shape=jax.ShapeDtypeStruct((levels, slots.shape[1]), jnp.float32),
        in_specs=[whole] * 2,
        out_specs=whole,
        compiler_params=pltpu.CompilerParams(vmem_limit_bytes=16 << 20),
    )(returned, slots)


def on_device(
    innovations,
    owners,
    prof_row,
    prof_col,
    interp_weights,
    model_tiles,
    model_ids,
    face_x,
    face_y,
    cross_term,
    wet_mask,
    norm_factor,
):
    levels, rows, lanes = norm_factor.shape
    n_lat = lax.axis_size("lat")
    n_lon = lax.axis_size("lon")
    early = lax.all_to_all(
        jnp.transpose(model_tiles[:EARLY], (1, 0, 2, 3)), "lon", split_axis=0, concat_axis=0, tiled=True
    )
    coef = jnp.stack([face_x, face_y, cross_term, wet_mask.astype(jnp.float32)])
    place = jnp.stack([prof_row, prof_col])
    packet, slots = route(innovations, interp_weights, place, owners, model_ids, n_lat * n_lon)
    packet, *coef_halos, late = post(packet, n_lat, n_lon, 1, coef, model_tiles)
    late = lax.all_to_all(late, "lon", split_axis=0, concat_axis=0, tiled=True)
    seen, lower, upper, cells = spread(packet, levels, rows)
    weights = prepare(coef, coef_halos, n_lat)
    field = combine(cells, seen, early, late, norm_factor)
    halos = exchange(field, n_lat, n_lon)
    smoothed, sampled = diffuse(field, norm_factor, halos, weights, lower, upper, cells, n_lat)
    (returned,) = post(sampled, n_lat, n_lon, 2)
    profile_values = collect(returned, slots, levels)
    return (smoothed, profile_values)


def solution(mesh):
    in_specs = (
        P(None, ("lat", "lon")),
        P(("lat", "lon"), None),
        P(("lat", "lon")),
        P(("lat", "lon")),
        P(None, ("lat", "lon")),
        P(None, ("lat", "lon"), None, None),
        P(None, ("lat", "lon")),
        P("lat", "lon"),
        P("lat", "lon"),
        P("lat", "lon"),
        P("lat", "lon"),
        P(None, "lat", "lon"),
    )
    out_specs = (P(None, "lat", "lon"), P(None, ("lat", "lon")))
    return jax.shard_map(
        on_device, mesh=mesh, in_specs=in_specs, out_specs=out_specs, check_vma=False
    )
```

```python
import functools

import jax
import jax.numpy as jnp
from jax import lax
from jax.experimental import pallas as pl
from jax.experimental.pallas import tpu as pltpu
from jax.sharding import PartitionSpec as P

STEPS = 10
CAPACITY = 8
PAD = 32
DEEP = 40
UNROLL = 32
BIG = 62 << 20
PARTS = 2
HALO = 16
LANES = 128
COLS = 12
PAIRS = 6
COEF_PAIRS = 5
EARLY = 10
BATCH = 5
CHUNK = 40
EDGE = 4
MESH = pl.DeviceIdType.MESH


def lane_ids(shape):
    return lax.broadcasted_iota(jnp.int32, shape, len(shape) - 1)


def within(lane, start, width):
    start = start % LANES
    return jnp.logical_and(lane >= start, lane < start + width)


def turn(values, shift):
    shift = shift % LANES
    return pltpu.roll(values, shift, 1) if shift else values


def packed_columns(plane_of, planes, rows, cols, first_pair, pairs):
    lane = lane_ids((rows, LANES))
    low = jnp.zeros((rows, LANES), jnp.float32)
    high = jnp.zeros((rows, LANES), jnp.float32)
    for k in range(pairs):
        for half in range(2):
            plane = 2 * (first_pair + k) + half
            if plane >= planes:
                continue
            shift = cols * k + (LANES // 2) * half
            values = turn(plane_of(plane), shift)
            low = jnp.where(within(lane, shift, cols), values, low)
            high = jnp.where(within(lane, LANES - cols + shift, cols), values, high)
    return low, high


def strip_plane(first, second, east, west, k, cols, inside):
    half = LANES // 2
    lane = lane_ids(first.shape)
    upper_half = lane >= half
    lane = lane % half
    west_side = lane < half // 2
    low = jnp.where(west_side, turn(first, COLS), turn(first, half - COLS))
    high = jnp.where(west_side, turn(second, COLS + half), turn(second, -COLS))
    own = jnp.where(upper_half, high, low)
    east = jnp.where(
        jnp.logical_and(inside, within(lane, half - COLS, cols)),
        turn(east, half - COLS - cols * k),
        0.0,
    )
    west = jnp.where(
        jnp.logical_and(inside, within(lane, COLS - cols, cols)), turn(west, COLS - cols * k), east
    )
    return jnp.where(jnp.logical_and(lane >= COLS, lane < half - COLS), own, west)


def inside_domain(shape, rows, has_south, has_north):
    row = lax.broadcasted_iota(jnp.int32, shape, 0)
    return jnp.logical_and(
        jnp.logical_or(row >= HALO, has_south), jnp.logical_or(row < HALO + rows, has_north)
    )


def neighbours(n_lat, n_lon):
    lat = lax.axis_index("lat")
    lon = lax.axis_index("lon")
    up = lax.rem(lat + 1, n_lat)
    down = lax.rem(lat + n_lat - 1, n_lat)
    right = lax.rem(lon + 1, n_lon)
    left = lax.rem(lon + n_lon - 1, n_lon)
    return lat, lon, up, down, right, left


def exchange_kernel(
    n_lat,
    n_lon,
    packs,
    west_cols,
    east_cols,
    south_rows,
    north_rows,
    send_sem,
    recv_sem,
):
    lat, lon, up, down, right, left = neighbours(n_lat, n_lon)
    tiles, rows = packs.shape[0] // 2 - 1, packs.shape[1]
    pack_first, pack_last = packs.at[pl.ds(0, tiles)], packs.at[pl.ds(tiles, tiles)]
    pack_low, pack_high = packs.at[2 * tiles], packs.at[2 * tiles + 1]
    first = pl.ds(0, HALO)
    last = pl.ds(rows - HALO, HALO)
    own = pl.ds(HALO, rows)
    above = pl.ds(HALO + rows, HALO)
    sends = (
        (pack_high, south_rows, (up, lon)),
        (pack_low, north_rows, (down, lon)),
        (pack_last, west_cols.at[:, own, :], (lat, right)),
        (pack_first, east_cols.at[:, own, :], (lat, left)),
        (pack_last.at[:, last, :], west_cols.at[:, first, :], (up, right)),
        (pack_first.at[:, last, :], east_cols.at[:, first, :], (up, left)),
        (pack_last.at[:, first, :], west_cols.at[:, above, :], (down, right)),
        (pack_first.at[:, first, :], east_cols.at[:, above, :], (down, left)),
    )
    barrier = pltpu.get_barrier_semaphore()
    for _, _, there in sends:
        pl.semaphore_signal(barrier, inc=1, device_id=there, device_id_type=MESH)
    pl.semaphore_wait(barrier, len(sends))
    copies = []
    for number, (source, target, there) in enumerate(sends):
        copy = pltpu.make_async_remote_copy(
            src_ref=source,
            dst_ref=target,
            send_sem=send_sem.at[number],
            recv_sem=recv_sem.at[number],
            device_id=there,
            device_id_type=MESH,
        )
        copy.start()
        copies.append(copy)
    for copy in copies:
        copy.wait()


def exchange(packs, n_lat, n_lon):
    count, rows, lanes = packs.shape
    anywhere = pl.BlockSpec(memory_space=pl.ANY)
    packed = jax.ShapeDtypeStruct((count // 2 - 1, rows + 2 * HALO, lanes), jnp.float32)
    edges = jax.ShapeDtypeStruct((rows, lanes), jnp.float32)
    return pl.pallas_call(
        functools.partial(exchange_kernel, n_lat, n_lon),
        out_shape=(packed, packed, edges, edges),
        in_specs=[anywhere],
        out_specs=[anywhere] * 4,
        scratch_shapes=[pltpu.SemaphoreType.DMA((8,)), pltpu.SemaphoreType.DMA((8,))],
        compiler_params=pltpu.CompilerParams(
            collective_id=0, has_side_effects=True, vmem_limit_bytes=BIG
        ),
    )(packs)


def prepare_kernel(
    n_lat, coef, west_cols, east_cols, south_coef, north_coef, weights_out, weights, raw, sem
):
    rows, lanes = coef.shape[1:]
    tall = rows + 2 * HALO
    half = lanes // 2
    has_south = lax.axis_index("lat") > 0
    has_north = lax.axis_index("lat") < n_lat - 1
    inside = inside_domain((tall, lanes), rows, has_south, has_north)
    upper_half = lane_ids((tall, lanes)) >= half
    for n in range(coef.shape[0]):
        plane = jnp.concatenate(
            [
                jnp.where(has_south, south_coef[n], 0.0),
                coef[n],
                jnp.where(has_north, north_coef[n], 0.0),
            ],
            axis=0,
        )
        raw[0, n] = plane
        both = strip_plane(plane, plane, east_cols[...], west_cols[...], n // 2, COLS, inside)
        mirrored = turn(both, half)
        raw[1, n] = jnp.where(upper_half, *((mirrored, both) if n % 2 == 0 else (both, mirrored)))

    def make_weights(step, carry):
        start = EDGE + step * CHUNK
        here = pl.ds(start, CHUNK)
        below = pl.ds(start - 1, CHUNK)
        above = pl.ds(start + 1, CHUNK)
        for kind in range(2):
            wet = raw[kind, 3, here, :]
            east = raw[kind, 0, here, :] * wet * turn(wet, -1)
            west = turn(east, 1)
            twist = 0.25 * raw[kind, 2, here, :] * wet
            north = raw[kind, 1, here, :] * wet * raw[kind, 3, above, :]
            south = raw[kind, 1, below, :] * raw[kind, 3, below, :] * wet
            keep = 1.0 - (east + west + north + south)
            for number, value in enumerate(
                (keep, north, south, west, turn(twist, 1), east, -turn(twist, -1))
            ):
                weights[kind, number, pl.ds(step * CHUNK, CHUNK), :] = value
        return carry

    lax.fori_loop(0, (tall - 2 * EDGE) // CHUNK, make_weights, 0)
    copy = pltpu.make_async_copy(weights, weights_out, sem)
    copy.start()
    copy.wait()


def prepare(coef, halos, n_lat):
    count, rows, lanes = coef.shape
    tall = rows + 2 * HALO
    whole = pl.BlockSpec(memory_space=pltpu.VMEM)
    return pl.pallas_call(
        functools.partial(prepare_kernel, n_lat),
        out_shape=jax.ShapeDtypeStruct((2, 7, tall - 2 * EDGE, lanes), jnp.float32),
        in_specs=[whole] * 5,
        out_specs=pl.BlockSpec(memory_space=pltpu.HBM),
        scratch_shapes=[
            pltpu.VMEM((2, 7, tall - 2 * EDGE, lanes), jnp.float32),
            pltpu.VMEM((2, count, tall, lanes), jnp.float32),
            pltpu.SemaphoreType.DMA,
        ],
        compiler_params=pltpu.CompilerParams(vmem_limit_bytes=BIG),
    )(coef, *halos)


def diffuse_kernel(
    n_lat,
    field,
    norm_far,
    weights_far,
    lower_far,
    upper_far,
    west_cols,
    east_cols,
    south_rows,
    north_rows,
    cells,
    out,
    sampled,
    grid,
    other,
    turned,
    gathered,
    norm,
    weights,
    lower,
    upper,
    sems,
    out_sems,
):
    levels, rows, lanes = field.shape
    tall = rows + 2 * HALO
    half = lanes // 2
    strips = (levels + 1) // 2
    has_south = lax.axis_index("lat") > 0
    has_north = lax.axis_index("lat") < n_lat - 1
    inside = inside_domain((tall, lanes), rows, has_south, has_north)

    near = grid.at[pl.ds(0, levels), pl.ds(HALO, rows), :]
    copies = [
        pltpu.make_async_copy(far, here, sems.at[number])
        for number, (far, here) in enumerate(
            (
                (field, near),
                (weights_far, weights),
                (norm_far, norm),
                (lower_far, lower),
                (upper_far, upper),
            )
        )
    ]
    for copy in copies:
        copy.start()
    for level in range(levels):
        at = pl.ds(STEPS * level, STEPS)
        grid[level, pl.ds(0, HALO), :] = jnp.zeros((HALO, lanes), jnp.float32)
        grid[level, pl.ds(HALO + rows, HALO), :] = jnp.zeros((HALO, lanes), jnp.float32)
        grid[level, pl.ds(HALO - STEPS, STEPS), :] = jnp.where(has_south, south_rows[at, :], 0.0)
        grid[level, pl.ds(HALO + rows, STEPS), :] = jnp.where(has_north, north_rows[at, :], 0.0)
    copies[0].wait()
    for pair in range(strips):
        tile, k = divmod(pair, PAIRS)
        grid[levels + pair] = strip_plane(
            grid[2 * pair],
            grid[min(2 * pair + 1, levels - 1)],
            east_cols[tile],
            west_cols[tile],
            k,
            STEPS,
            inside,
        )

    count = (tall - 2 * EDGE) // CHUNK

    def sweep(source, target):
        def one_chunk(step, carry):
            start = EDGE + step * CHUNK
            here = pl.ds(start, CHUNK)
            below = pl.ds(start - 1, CHUNK)
            above = pl.ds(start + 1, CHUNK)
            own = pl.ds(step * CHUNK, CHUNK)
            for kind, planes in enumerate((range(levels), range(levels, levels + strips))):
                keep, north, south, to_left, twist_left, to_right, twist_right = (
                    weights[kind, number, own, :] for number in range(7)
                )
                for plane in planes:
                    centre = source[plane, here, :]
                    upper = source[plane, above, :]
                    lower = source[plane, below, :]
                    tilt = upper - lower
                    target[plane, here, :] = (
                        keep * centre
                        + (north * upper + south * lower)
                        + turn(to_left * centre + twist_left * tilt, -1)
                        + turn(to_right * centre + twist_right * tilt, 1)
                    )
            return carry

        lax.fori_loop(0, count, one_chunk, 0)

    copies[1].wait()

    def two_steps(number, carry):
        sweep(grid, other)
        sweep(other, grid)
        return carry

    lax.fori_loop(0, STEPS // 2, two_steps, 0)

    for copy in copies[2:]:
        copy.wait()
    moves = []
    column = lane_ids((rows, lanes))
    inner = pl.ds(HALO, rows)
    for level in range(levels):
        edges = grid[levels + level // 2, inner, :]
        move = half * (level % 2)
        result = jnp.where(
            column < STEPS,
            turn(edges, -COLS - move),
            jnp.where(column >= lanes - STEPS, turn(edges, half + COLS - move), grid[level, inner, :]),
        )
        result = norm[level] * result
        norm[level] = result
        move = pltpu.make_async_copy(norm.at[level], out.at[level], out_sems.at[level])
        move.start()
        moves.append(move)
        turned[pl.ds(level, rows, stride=DEEP), :] = result
    for level in range(levels, PAD):
        turned[pl.ds(level, rows, stride=DEEP), :] = jnp.zeros((rows, lanes), jnp.float32)

    even = lane_ids((PAD, lanes)) % 2 == 0
    per_row = lanes // PAD

    def sample_tile(tile, carry):
        for q in range(per_row):
            block = tile * per_row + q

            def sample_group(group, found):
                found = list(found)
                for u in range(UNROLL):
                    spot = group * UNROLL + u
                    start = pl.multiple_of(cells[block, 5, spot], 8)
                    low = turned[pl.ds(start, PAD), :].reshape(PAD // 8, 8, lanes)
                    high = turned[pl.ds(start + DEEP, PAD), :].reshape(PAD // 8, 8, lanes)
                    mixed = low * row_of(lower, block * lanes + spot) + high * row_of(
                        upper, block * lanes + spot
                    )
                    move = (cells[block, 6, spot] + spot) & (lanes - 1)
                    found[u % 2] = found[u % 2] + pltpu.roll(mixed.reshape(PAD, lanes), move, 1)
                return tuple(found)

            zeros = jnp.zeros((PAD, lanes), jnp.float32)
            on_even, on_odd = lax.fori_loop(0, lanes // UNROLL, sample_group, (zeros, zeros))
            gathered[pl.ds(PAD * q, PAD), :] = jnp.where(
                even, on_even + turn(on_even, -1), on_odd + turn(on_odd, -1)
            )
        sampled[pl.ds(pl.multiple_of(tile * lanes, lanes), lanes), :] = gathered[...].T
        return carry

    lax.fori_loop(0, sampled.shape[0] // lanes, sample_tile, 0)
    for move in moves:
        move.wait()


def row_of(table, number):
    return table[pl.ds(number, 8, stride=0), :]


def diffuse(field, norm, halos, weights, lower, upper, cells, n_lat):
    levels, rows, lanes = field.shape
    tall = rows + 2 * HALO
    whole = pl.BlockSpec(memory_space=pltpu.VMEM)
    scalars = pl.BlockSpec(memory_space=pltpu.SMEM)
    planes = levels + (levels + 1) // 2
    anywhere = pl.BlockSpec(memory_space=pl.ANY)
    return pl.pallas_call(
        functools.partial(diffuse_kernel, n_lat),
        out_shape=(
            jax.ShapeDtypeStruct(field.shape, jnp.float32),
            jax.ShapeDtypeStruct((cells.shape[0] * PAD, lanes), jnp.float32),
        ),
        in_specs=[anywhere] * 5 + [whole] * 4 + [scalars],
        out_specs=(anywhere, whole),
        scratch_shapes=[
            pltpu.VMEM((planes, tall, lanes), jnp.float32),
            pltpu.VMEM((planes, tall, lanes), jnp.float32),
            pltpu.VMEM((rows * DEEP, lanes), jnp.float32),
            pltpu.VMEM((lanes, lanes), jnp.float32),
            pltpu.VMEM(norm.shape, jnp.float32),
            pltpu.VMEM(weights.shape, jnp.float32),
            pltpu.VMEM(lower.shape, jnp.float32),
            pltpu.VMEM(upper.shape, jnp.float32),
            pltpu.SemaphoreType.DMA((5,)),
            pltpu.SemaphoreType.DMA((levels,)),
        ],
        compiler_params=pltpu.CompilerParams(vmem_limit_bytes=BIG),
    )(field, norm, weights, lower, upper, *halos, cells)


def one_hot_slots(slots, q, rows):
    shape = (rows, slots.shape[1])
    number = lax.broadcasted_iota(jnp.int32, shape, 0) * (LANES // PAD) + q
    return jnp.where(number == slots, 1.0, 0.0)


def route_kernel(innovations, weights, place, owner_column, owner_row, ids, packet, slots, table):
    levels, count = innovations.shape
    total = packet.shape[0]
    same = owner_column[...] == owner_row[...]
    earlier = lax.broadcasted_iota(jnp.int32, (count, count), 0) < lax.broadcasted_iota(
        jnp.int32, (count, count), 1
    )
    rank = jnp.sum(jnp.where(jnp.logical_and(same, earlier), 1, 0), axis=0, keepdims=True)
    slot = owner_row[...] * CAPACITY + rank
    slots[...] = slot

    table[...] = jnp.zeros_like(table)
    table[pl.ds(0, levels), :] = innovations[...]
    table[pl.ds(levels, 4), :] = weights[...]
    table[pl.ds(levels + 4, 2), :] = place[...].astype(jnp.float32)
    flipped = jnp.concatenate(
        [table[:, pl.ds(start, LANES)].T for start in range(0, count, LANES)], axis=0
    )
    sent = jnp.zeros((total, LANES), jnp.float32)
    for q in range(LANES // PAD):
        moved = pltpu.roll(flipped, PAD * q, 1) if q else flipped
        sent += jnp.dot(
            one_hot_slots(slot, q, total),
            moved,
            precision=lax.Precision.HIGHEST,
            preferred_element_type=jnp.float32,
        )
    lane = lane_ids((total, LANES))
    row = lax.broadcasted_iota(jnp.int32, (total, LANES), 0)
    per_device = 2
    row_group = CAPACITY * PAD // LANES
    group = lax.rem(row // row_group, ids.shape[1] // per_device) * per_device
    first_row = lax.rem(row, row_group) == 0
    numbers = jnp.concatenate(
        [ids[...].astype(jnp.float32), jnp.zeros((1, LANES - ids.shape[1]), jnp.float32)], axis=1
    )
    for t in range(per_device):
        number = jnp.sum(jnp.where(lane == group + t, numbers, 0.0), axis=1, keepdims=True)
        spare = jnp.logical_and(first_row, lane == PAD * (t + 1) - 1)
        sent = jnp.where(spare, number, sent)
    packet[...] = sent


def route(innovations, weights, place, owners, ids, devices):
    whole = pl.BlockSpec(memory_space=pltpu.VMEM)
    count = innovations.shape[1]
    return pl.pallas_call(
        route_kernel,
        out_shape=(
            jax.ShapeDtypeStruct((devices * CAPACITY * PAD // LANES, LANES), jnp.float32),
            jax.ShapeDtypeStruct((1, count), jnp.int32),
        ),
        in_specs=[whole] * 6,
        out_specs=(whole, whole),
        scratch_shapes=[pltpu.VMEM((LANES, count), jnp.float32)],
        compiler_params=pltpu.CompilerParams(vmem_limit_bytes=BIG),
    )(innovations, weights, place, owners, owners.reshape(1, count), ids)


def post_kernel(has_coef, source, *refs):
    if has_coef:
        coef, tiles, target, west_cols, east_cols, south_coef, north_coef, late = refs[:8]
        held, send_sem, recv_sem, local_sem, pack_first, pack_last, late_sem = refs[8:]
    else:
        target, held, send_sem, recv_sem, local_sem = refs
    n_lat, n_lon = source.shape[:2]
    lat, lon, up, down, right, left = neighbours(n_lat, n_lon)
    across = [lax.rem(lon + step, n_lon) for step in range(1, n_lon)]
    along = [lax.rem(lat + step, n_lat) for step in range(1, n_lat)]
    corners = [(up, right), (up, left), (down, right), (down, left)] if has_coef else []

    barrier = pltpu.get_barrier_semaphore()
    for other in across:
        pl.semaphore_signal(barrier, inc=1, device_id=(lat, other), device_id_type=MESH)
    for other in along:
        pl.semaphore_signal(barrier, inc=1, device_id=(other, lon), device_id_type=MESH)
    for there in corners:
        pl.semaphore_signal(barrier, inc=1, device_id=there, device_id_type=MESH)
    own = pltpu.make_async_copy(source.at[:, lon], held.at[:, lon], local_sem)
    own.start()
    moves = []
    if has_coef:
        for level in range(late.shape[1]):
            move = pltpu.make_async_copy(
                tiles.at[EARLY + level], late.at[:, level], late_sem.at[level]
            )
            move.start()
            moves.append(move)
        rows = coef.shape[1]
        low, high = packed_columns(
            lambda plane: coef[plane], coef.shape[0], rows, COLS, 0, COEF_PAIRS
        )
        pack_first[...] = low
        pack_last[...] = high
    pl.semaphore_wait(barrier, n_lon + n_lat - 2 + len(corners))

    def push(here, there, number, device):
        copy = pltpu.make_async_remote_copy(
            src_ref=here,
            dst_ref=there,
            send_sem=send_sem.at[number],
            recv_sem=recv_sem.at[number],
            device_id=device,
            device_id_type=MESH,
        )
        copy.start()
        return copy

    copies = [
        push(source.at[:, other], held.at[:, lon], number, (lat, other))
        for number, other in enumerate(across)
    ]
    edges = []
    if has_coef:
        first = pl.ds(0, HALO)
        last = pl.ds(rows - HALO, HALO)
        middle = pl.ds(HALO, rows)
        above = pl.ds(HALO + rows, HALO)
        for here, there, device in (
            (coef.at[:, last, :], south_coef, (up, lon)),
            (coef.at[:, first, :], north_coef, (down, lon)),
            (pack_last, west_cols.at[middle, :], (lat, right)),
            (pack_first, east_cols.at[middle, :], (lat, left)),
            (pack_last.at[last, :], west_cols.at[first, :], (up, right)),
            (pack_first.at[last, :], east_cols.at[first, :], (up, left)),
            (pack_last.at[first, :], west_cols.at[above, :], (down, right)),
            (pack_first.at[first, :], east_cols.at[above, :], (down, left)),
        ):
            edges.append(push(here, there, n_lon + n_lat + len(edges), device))
    own.wait()
    for copy in copies:
        copy.wait()
    copies = [
        push(held.at[other], target.at[lat], n_lon + number, (other, lon))
        for number, other in enumerate(along)
    ]
    own = pltpu.make_async_copy(held.at[lat], target.at[lat], local_sem)
    own.start()
    own.wait()
    for copy in copies + edges + moves:
        copy.wait()


def post(packet, n_lat, n_lon, collective_id, coef=None, tiles=None):
    whole = pl.BlockSpec(memory_space=pltpu.VMEM)
    anywhere = pl.BlockSpec(memory_space=pl.ANY)
    outside = pl.BlockSpec(memory_space=pltpu.HBM)
    blocks = packet.reshape(n_lat, n_lon, -1, LANES)
    has_coef = coef is not None
    sems = n_lon + n_lat + 8 * has_coef
    out_shape = [jax.ShapeDtypeStruct(blocks.shape, jnp.float32)]
    scratch = [
        pltpu.VMEM(blocks.shape, jnp.float32),
        pltpu.SemaphoreType.DMA((sems,)),
        pltpu.SemaphoreType.DMA((sems,)),
        pltpu.SemaphoreType.DMA,
    ]
    operands, in_specs, out_specs = [blocks], [whole], [outside if has_coef else whole]
    if has_coef:
        count, rows, lanes = coef.shape
        levels, slots, depth, _ = tiles.shape
        packed = jax.ShapeDtypeStruct((rows + 2 * HALO, lanes), jnp.float32)
        edge = jax.ShapeDtypeStruct((count, HALO, lanes), jnp.float32)
        late = jax.ShapeDtypeStruct((slots, levels - EARLY, depth, lanes), jnp.float32)
        out_shape += [packed, packed, edge, edge, late]
        scratch += [
            pltpu.VMEM((rows, lanes), jnp.float32),
            pltpu.VMEM((rows, lanes), jnp.float32),
            pltpu.SemaphoreType.DMA((levels - EARLY,)),
        ]
        operands += [coef, tiles]
        in_specs += [whole, anywhere]
        out_specs += [outside] * 5
    received, *rest = pl.pallas_call(
        functools.partial(post_kernel, has_coef),
        out_shape=out_shape,
        in_specs=in_specs,
        out_specs=out_specs,
        scratch_shapes=scratch,
        compiler_params=pltpu.CompilerParams(
            collective_id=collective_id, has_side_effects=True, vmem_limit_bytes=BIG if has_coef else 4 << 20
        ),
    )(*operands)
    return (received.reshape(packet.shape), *rest)


def spread_kernel(
    levels,
    packet,
    seen_out,
    lower_out,
    upper_out,
    cells_out,
    seen,
    lower,
    upper,
    turned,
    cells,
    sem,
    *parts,
):
    total, lanes = packet.shape
    per_row = lanes // PAD
    tiles = total // lanes
    level_lane = PAD - 8
    sublane = lax.broadcasted_iota(jnp.int32, (8, lanes), 0)
    for tile in range(tiles):
        flipped = packet[pl.ds(tile * lanes, lanes), :].T
        turned[pl.ds(tile * lanes, lanes), :] = flipped
        for q in range(per_row):
            last = flipped[PAD * q + level_lane : PAD * (q + 1)].astype(jnp.int32)
            last = jnp.where(sublane == 5, last * DEEP, jnp.where(sublane == 6, lanes - last, last))
            cells_out[tile * per_row + q] = last
    copy = pltpu.make_async_copy(cells_out, cells, sem.at[0])
    copy.start()

    lane = lane_ids((lanes, lanes)).astype(jnp.float32)
    for tile in range(tiles):
        rows = packet[pl.ds(tile * lanes, lanes), :]
        for q in range(per_row):
            first, second, third, fourth, row, column = (
                jnp.broadcast_to(rows[:, n : n + 1], (lanes, lanes))
                for n in range(PAD * q + level_lane + 1, PAD * q + level_lane + 7)
            )
            here = lane == column
            beside = lane == column + 1.0
            block = pl.ds((tile * per_row + q) * lanes, lanes)
            lower[block, :] = jnp.where(here, first, jnp.where(beside, second, 0.0))
            upper[block, :] = jnp.where(here, third, jnp.where(beside, fourth, 0.0))

    is_level = lax.broadcasted_iota(jnp.int32, (PAD, lanes), 0) < levels
    tables = (
        pltpu.make_async_copy(lower, lower_out, sem.at[1]),
        pltpu.make_async_copy(upper, upper_out, sem.at[2]),
    )
    for table in tables:
        table.start()
    for part in parts:
        part[...] = jnp.zeros_like(part)
    copy.wait()

    def spread_block(block, carry):
        values = jnp.where(is_level, turned[pl.ds(pl.multiple_of(block * PAD, PAD), PAD), :], 0.0)

        def spread_group(group, carry):
            moved = pltpu.roll(values, lax.rem(lanes - group * UNROLL, lanes), 1)
            for u in range(UNROLL):
                spot = group * UNROLL + u
                value = jnp.broadcast_to(moved[:, u : u + 1], (PAD, lanes)).reshape(
                    PAD // 8, 8, lanes
                )
                part = parts[u % len(parts)]
                for table, offset in ((lower, 0), (upper, DEEP)):
                    start = pl.multiple_of(cells[block, 5, spot] + offset, 8)
                    added = (value * row_of(table, block * lanes + spot)).reshape(PAD, lanes)
                    part[pl.ds(start, PAD), :] = part[pl.ds(start, PAD), :] + added
            return carry

        lax.fori_loop(0, lanes // UNROLL, spread_group, 0)
        return carry

    lax.fori_loop(0, tiles * per_row, spread_block, 0)
    rows = seen.shape[1]
    moves = list(tables)
    for level in range(levels):
        at = pl.ds(level, rows, stride=DEEP)
        total = parts[0][at, :]
        for part in parts[1:]:
            total = total + part[at, :]
        seen[level] = total
        move = pltpu.make_async_copy(seen.at[level], seen_out.at[level], sem.at[3 + level])
        move.start()
        moves.append(move)
    for move in moves:
        move.wait()


def spread(packet, levels, rows):
    total, lanes = packet.shape
    whole = pl.BlockSpec(memory_space=pltpu.VMEM)
    blocks = total // PAD
    outside = pl.BlockSpec(memory_space=pltpu.HBM)
    masks = jax.ShapeDtypeStruct((blocks * lanes, lanes), jnp.float32)
    return pl.pallas_call(
        functools.partial(spread_kernel, levels),
        out_shape=(
            jax.ShapeDtypeStruct((levels, rows, lanes), jnp.float32),
            masks,
            masks,
            jax.ShapeDtypeStruct((blocks, 8, lanes), jnp.int32),
        ),
        in_specs=[whole],
        out_specs=(outside,) * 3 + (whole,),
        scratch_shapes=[
            pltpu.VMEM((levels, rows, lanes), jnp.float32),
            pltpu.VMEM(masks.shape, jnp.float32),
            pltpu.VMEM(masks.shape, jnp.float32),
            pltpu.VMEM(packet.shape, jnp.float32),
            pltpu.SMEM((blocks, 8, lanes), jnp.int32),
            pltpu.SemaphoreType.DMA((3 + levels,)),
        ]
        + [pltpu.VMEM((rows * DEEP, lanes), jnp.float32)] * PARTS,
        compiler_params=pltpu.CompilerParams(vmem_limit_bytes=BIG),
    )(packet)


def combine_kernel(
    cells,
    seen,
    early,
    late,
    norm,
    field_out,
    packs_out,
    field,
    packs,
    seen_in,
    tiles_in,
    norm_in,
    sems,
    out_sems,
):
    slots, _, depth, lanes = early.shape
    levels = norm.shape[0]
    n_lon = lax.axis_size("lon")
    per_device = slots // n_lon
    per_row = lanes // PAD
    row_group = CAPACITY * PAD // lanes
    base = lax.axis_index("lat") * n_lon
    batches = []
    for number, start in enumerate(range(0, levels, BATCH)):
        part = pl.ds(start, BATCH)
        tiles = early.at[:, part] if start < EARLY else late.at[:, pl.ds(start - EARLY, BATCH)]
        copies = (
            pltpu.make_async_copy(seen.at[part], seen_in.at[part], sems.at[number, 0]),
            pltpu.make_async_copy(tiles, tiles_in.at[:, part], sems.at[number, 1]),
            pltpu.make_async_copy(norm.at[part], norm_in.at[part], sems.at[number, 2]),
        )
        for copy in copies:
            copy.start()
        batches.append((part, copies))

    moves = []

    def send_out(here, there):
        move = pltpu.make_async_copy(here, there, out_sems.at[len(moves)])
        move.start()
        moves.append(move)

    for part, copies in batches:
        for copy in copies:
            copy.wait()

        def one_tile(slot, carry):
            at = (base + slot // per_device) * row_group
            block = (at // lanes) * per_row + lax.rem(slot, per_device)
            rows = pl.ds(pl.multiple_of(cells[block, 7, lax.rem(at, lanes)] * depth, depth), depth)
            field[part, rows, :] = norm_in[part, rows, :] * (
                seen_in[part, rows, :] + tiles_in[slot, part]
            )
            return carry

        lax.fori_loop(0, slots, one_tile, 0, unroll=4)
        send_out(field.at[part], field_out.at[part])

    rows = field.shape[1]
    tiles = packs.shape[0] // 2 - 1
    for level in range(levels):
        at = pl.ds(STEPS * level, STEPS)
        packs[2 * tiles, at, :] = field[level, pl.ds(0, STEPS), :]
        packs[2 * tiles + 1, at, :] = field[level, pl.ds(rows - STEPS, STEPS), :]
    for tile in range(tiles):
        packs[tile], packs[tiles + tile] = packed_columns(
            lambda plane: field[plane], levels, rows, STEPS, tile * PAIRS, PAIRS
        )
    send_out(packs, packs_out)
    for move in moves:
        move.wait()


def combine(cells, seen, early, late, norm):
    anywhere = pl.BlockSpec(memory_space=pl.ANY)
    levels, rows, lanes = norm.shape
    tiles = (early.shape[0], levels) + early.shape[2:]
    packs = -(-((levels + 1) // 2) // PAIRS)
    outs = [norm.shape, (2 * packs + 2, rows, lanes)]
    return pl.pallas_call(
        combine_kernel,
        out_shape=[jax.ShapeDtypeStruct(shape, jnp.float32) for shape in outs],
        in_specs=[pl.BlockSpec(memory_space=pltpu.SMEM)] + [anywhere] * 4,
        out_specs=[anywhere] * 2,
        scratch_shapes=[pltpu.VMEM(shape, jnp.float32) for shape in outs]
        + [
            pltpu.VMEM(seen.shape, jnp.float32),
            pltpu.VMEM(tiles, jnp.float32),
            pltpu.VMEM(norm.shape, jnp.float32),
            pltpu.SemaphoreType.DMA((levels // BATCH, 3)),
            pltpu.SemaphoreType.DMA((levels // BATCH + 1,)),
        ],
        compiler_params=pltpu.CompilerParams(vmem_limit_bytes=59 << 20),
    )(cells, seen, early, late, norm)


def collect_kernel(levels, returned, slots, out):
    total, lanes = returned.shape
    flipped = jnp.concatenate(
        [returned[pl.ds(start, lanes), :].T for start in range(0, total, lanes)], axis=1
    )
    values = jnp.zeros((PAD, slots.shape[1]), jnp.float32)
    for q in range(lanes // PAD):
        values += jnp.dot(
            flipped[PAD * q : PAD * (q + 1)],
            one_hot_slots(slots[...], q, total),
            precision=lax.Precision.HIGHEST,
            preferred_element_type=jnp.float32,
        )
    out[...] = values[:levels]


def collect(returned, slots, levels):
    whole = pl.BlockSpec(memory_space=pltpu.VMEM)
    return pl.pallas_call(
        functools.partial(collect_kernel, levels),
        out_shape=jax.ShapeDtypeStruct((levels, slots.shape[1]), jnp.float32),
        in_specs=[whole] * 2,
        out_specs=whole,
        compiler_params=pltpu.CompilerParams(vmem_limit_bytes=8 << 20),
    )(returned, slots)


def on_device(
    innovations,
    owners,
    prof_row,
    prof_col,
    interp_weights,
    model_tiles,
    model_ids,
    face_x,
    face_y,
    cross_term,
    wet_mask,
    norm_factor,
):
    levels, rows, lanes = norm_factor.shape
    n_lat = lax.axis_size("lat")
    n_lon = lax.axis_size("lon")
    early = lax.all_to_all(
        jnp.transpose(model_tiles[:EARLY], (1, 0, 2, 3)), "lon", split_axis=0, concat_axis=0, tiled=True
    )
    coef = jnp.stack([face_x, face_y, cross_term, wet_mask.astype(jnp.float32)])
    place = jnp.stack([prof_row, prof_col])
    packet, slots = route(innovations, interp_weights, place, owners, model_ids, n_lat * n_lon)
    packet, *coef_halos, late = post(packet, n_lat, n_lon, 1, coef, model_tiles)
    late = lax.all_to_all(late, "lon", split_axis=0, concat_axis=0, tiled=True)
    seen, lower, upper, cells = spread(packet, levels, rows)
    weights = prepare(coef, coef_halos, n_lat)
    field, packs = combine(cells, seen, early, late, norm_factor)
    halos = exchange(packs, n_lat, n_lon)
    smoothed, sampled = diffuse(field, norm_factor, halos, weights, lower, upper, cells, n_lat)
    (returned,) = post(sampled, n_lat, n_lon, 2)
    profile_values = collect(returned, slots, levels)
    return (smoothed, profile_values)


def solution(mesh):
    in_specs = (
        P(None, ("lat", "lon")),
        P(("lat", "lon"), None),
        P(("lat", "lon")),
        P(("lat", "lon")),
        P(None, ("lat", "lon")),
        P(None, ("lat", "lon"), None, None),
        P(None, ("lat", "lon")),
        P("lat", "lon"),
        P("lat", "lon"),
        P("lat", "lon"),
        P("lat", "lon"),
        P(None, "lat", "lon"),
    )
    out_specs = (P(None, "lat", "lon"), P(None, ("lat", "lon")))
    return jax.shard_map(
        on_device, mesh=mesh, in_specs=in_specs, out_specs=out_specs, check_vma=False
    )
```

```python
import functools

import jax
import jax.numpy as jnp
from jax import lax
from jax.experimental import pallas as pl
from jax.experimental.pallas import tpu as pltpu
from jax.sharding import PartitionSpec as P

STEPS = 10
CAPACITY = 8
PAD = 32
DEEP = 40
UNROLL = 32
BIG = 62 << 20
HALO = 16
LANES = 128
COLS = 12
PAIRS = 6
COEF_PAIRS = 5
EARLY = 10
CHUNK = 40
EDGE = 4
MESH = pl.DeviceIdType.MESH


def lane_ids(shape):
    return lax.broadcasted_iota(jnp.int32, shape, len(shape) - 1)


def within(lane, start, width):
    start = start % LANES
    return jnp.logical_and(lane >= start, lane < start + width)


def turn(values, shift):
    shift = shift % LANES
    return pltpu.roll(values, shift, 1) if shift else values


def packed_columns(plane_of, planes, rows, cols, first_pair, pairs):
    lane = lane_ids((rows, LANES))
    low = jnp.zeros((rows, LANES), jnp.float32)
    high = jnp.zeros((rows, LANES), jnp.float32)
    for k in range(pairs):
        for half in range(2):
            plane = 2 * (first_pair + k) + half
            if plane >= planes:
                continue
            shift = cols * k + (LANES // 2) * half
            values = turn(plane_of(plane), shift)
            low = jnp.where(within(lane, shift, cols), values, low)
            high = jnp.where(within(lane, LANES - cols + shift, cols), values, high)
    return low, high


def strip_plane(first, second, east, west, k, cols, inside):
    half = LANES // 2
    lane = lane_ids(first.shape)
    upper_half = lane >= half
    lane = lane % half
    west_side = lane < half // 2
    low = jnp.where(west_side, turn(first, COLS), turn(first, half - COLS))
    high = jnp.where(west_side, turn(second, COLS + half), turn(second, -COLS))
    own = jnp.where(upper_half, high, low)
    east = jnp.where(
        jnp.logical_and(inside, within(lane, half - COLS, cols)),
        turn(east, half - COLS - cols * k),
        0.0,
    )
    west = jnp.where(
        jnp.logical_and(inside, within(lane, COLS - cols, cols)), turn(west, COLS - cols * k), east
    )
    return jnp.where(jnp.logical_and(lane >= COLS, lane < half - COLS), own, west)


def inside_domain(shape, rows, has_south, has_north):
    row = lax.broadcasted_iota(jnp.int32, shape, 0)
    return jnp.logical_and(
        jnp.logical_or(row >= HALO, has_south), jnp.logical_or(row < HALO + rows, has_north)
    )


def neighbours(n_lat, n_lon):
    lat = lax.axis_index("lat")
    lon = lax.axis_index("lon")
    up = lax.rem(lat + 1, n_lat)
    down = lax.rem(lat + n_lat - 1, n_lat)
    right = lax.rem(lon + 1, n_lon)
    left = lax.rem(lon + n_lon - 1, n_lon)
    return lat, lon, up, down, right, left


def exchange_kernel(
    n_lat,
    n_lon,
    field,
    west_cols,
    east_cols,
    south_rows,
    north_rows,
    pack_first,
    pack_last,
    pack_low,
    pack_high,
    send_sem,
    recv_sem,
):
    lat, lon, up, down, right, left = neighbours(n_lat, n_lon)
    levels, rows = field.shape[:2]

    barrier = pltpu.get_barrier_semaphore()
    for there in (
        (lat, right),
        (lat, left),
        (up, lon),
        (down, lon),
        (up, right),
        (up, left),
        (down, right),
        (down, left),
    ):
        pl.semaphore_signal(barrier, inc=1, device_id=there, device_id_type=MESH)

    copies = []

    def send(source, target, there):
        number = len(copies)
        copy = pltpu.make_async_remote_copy(
            src_ref=source,
            dst_ref=target,
            send_sem=send_sem.at[number],
            recv_sem=recv_sem.at[number],
            device_id=there,
            device_id_type=MESH,
        )
        copy.start()
        copies.append(copy)

    for level in range(levels):
        at = pl.ds(STEPS * level, STEPS)
        pack_high[at, :] = field[level, pl.ds(rows - STEPS, STEPS), :]
        pack_low[at, :] = field[level, pl.ds(0, STEPS), :]
    pl.semaphore_wait(barrier, 8)
    send(pack_high, south_rows, (up, lon))
    send(pack_low, north_rows, (down, lon))
    for tile in range(pack_first.shape[0]):
        low, high = packed_columns(
            lambda plane: field[plane], levels, rows, STEPS, tile * PAIRS, PAIRS
        )
        pack_first[tile] = low
        pack_last[tile] = high

    first = pl.ds(0, HALO)
    last = pl.ds(rows - HALO, HALO)
    own = pl.ds(HALO, rows)
    above = pl.ds(HALO + rows, HALO)
    send(pack_last, west_cols.at[:, own, :], (lat, right))
    send(pack_first, east_cols.at[:, own, :], (lat, left))
    send(pack_last.at[:, last, :], west_cols.at[:, first, :], (up, right))
    send(pack_first.at[:, last, :], east_cols.at[:, first, :], (up, left))
    send(pack_last.at[:, first, :], west_cols.at[:, above, :], (down, right))
    send(pack_first.at[:, first, :], east_cols.at[:, above, :], (down, left))
    for copy in copies:
        copy.wait()


def exchange(field, n_lat, n_lon):
    levels, rows, lanes = field.shape
    tiles = -(-((levels + 1) // 2) // PAIRS)
    edge = -(-levels * STEPS // 8) * 8
    whole = pl.BlockSpec(memory_space=pltpu.VMEM)
    packed = jax.ShapeDtypeStruct((tiles, rows + 2 * HALO, lanes), jnp.float32)
    edges = jax.ShapeDtypeStruct((edge, lanes), jnp.float32)
    return pl.pallas_call(
        functools.partial(exchange_kernel, n_lat, n_lon),
        out_shape=(packed, packed, edges, edges),
        in_specs=[whole],
        out_specs=[whole] * 4,
        scratch_shapes=[
            pltpu.VMEM((tiles, rows, lanes), jnp.float32),
            pltpu.VMEM((tiles, rows, lanes), jnp.float32),
            pltpu.VMEM((edge, lanes), jnp.float32),
            pltpu.VMEM((edge, lanes), jnp.float32),
            pltpu.SemaphoreType.DMA((8,)),
            pltpu.SemaphoreType.DMA((8,)),
        ],
        compiler_params=pltpu.CompilerParams(
            collective_id=0, has_side_effects=True, vmem_limit_bytes=8 << 20
        ),
    )(field)


def prepare_kernel(
    n_lat, coef, west_cols, east_cols, south_coef, north_coef, weights, raw
):
    rows, lanes = coef.shape[1:]
    tall = rows + 2 * HALO
    half = lanes // 2
    has_south = lax.axis_index("lat") > 0
    has_north = lax.axis_index("lat") < n_lat - 1
    inside = inside_domain((tall, lanes), rows, has_south, has_north)
    upper_half = lane_ids((tall, lanes)) >= half
    for n in range(coef.shape[0]):
        plane = jnp.concatenate(
            [
                jnp.where(has_south, south_coef[n], 0.0),
                coef[n],
                jnp.where(has_north, north_coef[n], 0.0),
            ],
            axis=0,
        )
        raw[0, n] = plane
        both = strip_plane(plane, plane, east_cols[...], west_cols[...], n // 2, COLS, inside)
        mirrored = turn(both, half)
        raw[1, n] = jnp.where(upper_half, *((mirrored, both) if n % 2 == 0 else (both, mirrored)))

    def make_weights(step, carry):
        start = EDGE + step * CHUNK
        here = pl.ds(start, CHUNK)
        below = pl.ds(start - 1, CHUNK)
        above = pl.ds(start + 1, CHUNK)
        for kind in range(2):
            wet = raw[kind, 3, here, :]
            east = raw[kind, 0, here, :] * wet * turn(wet, -1)
            west = turn(east, 1)
            twist = 0.25 * raw[kind, 2, here, :] * wet
            north = raw[kind, 1, here, :] * wet * raw[kind, 3, above, :]
            south = raw[kind, 1, below, :] * raw[kind, 3, below, :] * wet
            keep = 1.0 - (east + west + north + south)
            for number, value in enumerate(
                (keep, north, south, west, turn(twist, 1), east, -turn(twist, -1))
            ):
                weights[kind, number, pl.ds(step * CHUNK, CHUNK), :] = value
        return carry

    lax.fori_loop(0, (tall - 2 * EDGE) // CHUNK, make_weights, 0)


def prepare(coef, halos, n_lat):
    count, rows, lanes = coef.shape
    tall = rows + 2 * HALO
    whole = pl.BlockSpec(memory_space=pltpu.VMEM)
    return pl.pallas_call(
        functools.partial(prepare_kernel, n_lat),
        out_shape=jax.ShapeDtypeStruct((2, 7, tall - 2 * EDGE, lanes), jnp.float32),
        in_specs=[whole] * 5,
        out_specs=whole,
        scratch_shapes=[pltpu.VMEM((2, count, tall, lanes), jnp.float32)],
        compiler_params=pltpu.CompilerParams(vmem_limit_bytes=4 << 20),
    )(coef, *halos)


def diffuse_kernel(
    n_lat,
    field,
    norm,
    west_cols,
    east_cols,
    south_rows,
    north_rows,
    weights,
    lower,
    upper,
    cells,
    out,
    sampled,
    grid,
    other,
    turned,
    gathered,
):
    levels, rows, lanes = field.shape
    tall = rows + 2 * HALO
    half = lanes // 2
    strips = (levels + 1) // 2
    has_south = lax.axis_index("lat") > 0
    has_north = lax.axis_index("lat") < n_lat - 1
    inside = inside_domain((tall, lanes), rows, has_south, has_north)

    for level in range(levels):
        at = pl.ds(STEPS * level, STEPS)
        grid[level, pl.ds(0, HALO), :] = jnp.zeros((HALO, lanes), jnp.float32)
        grid[level, pl.ds(HALO + rows, HALO), :] = jnp.zeros((HALO, lanes), jnp.float32)
        grid[level, pl.ds(HALO - STEPS, STEPS), :] = jnp.where(has_south, south_rows[at, :], 0.0)
        grid[level, pl.ds(HALO, rows), :] = field[level]
        grid[level, pl.ds(HALO + rows, STEPS), :] = jnp.where(has_north, north_rows[at, :], 0.0)
    for pair in range(strips):
        tile, k = divmod(pair, PAIRS)
        grid[levels + pair] = strip_plane(
            grid[2 * pair],
            grid[min(2 * pair + 1, levels - 1)],
            east_cols[tile],
            west_cols[tile],
            k,
            STEPS,
            inside,
        )

    count = (tall - 2 * EDGE) // CHUNK

    def sweep(source, target):
        def one_chunk(step, carry):
            start = EDGE + step * CHUNK
            here = pl.ds(start, CHUNK)
            below = pl.ds(start - 1, CHUNK)
            above = pl.ds(start + 1, CHUNK)
            own = pl.ds(step * CHUNK, CHUNK)
            for kind, planes in enumerate((range(levels), range(levels, levels + strips))):
                keep, north, south, to_left, twist_left, to_right, twist_right = (
                    weights[kind, number, own, :] for number in range(7)
                )
                for plane in planes:
                    centre = source[plane, here, :]
                    upper = source[plane, above, :]
                    lower = source[plane, below, :]
                    tilt = upper - lower
                    target[plane, here, :] = (
                        keep * centre
                        + (north * upper + south * lower)
                        + turn(to_left * centre + twist_left * tilt, -1)
                        + turn(to_right * centre + twist_right * tilt, 1)
                    )
            return carry

        lax.fori_loop(0, count, one_chunk, 0)

    def two_steps(number, carry):
        sweep(grid, other)
        sweep(other, grid)
        return carry

    lax.fori_loop(0, STEPS // 2, two_steps, 0)

    column = lane_ids((rows, lanes))
    inner = pl.ds(HALO, rows)
    for level in range(levels):
        edges = grid[levels + level // 2, inner, :]
        move = half * (level % 2)
        result = jnp.where(
            column < STEPS,
            turn(edges, -COLS - move),
            jnp.where(column >= lanes - STEPS, turn(edges, half + COLS - move), grid[level, inner, :]),
        )
        result = norm[level] * result
        out[level] = result
        turned[pl.ds(level, rows, stride=DEEP), :] = result
    for level in range(levels, PAD):
        turned[pl.ds(level, rows, stride=DEEP), :] = jnp.zeros((rows, lanes), jnp.float32)

    even = lane_ids((PAD, lanes)) % 2 == 0
    per_row = lanes // PAD

    def sample_tile(tile, carry):
        for q in range(per_row):
            block = tile * per_row + q

            def sample_group(group, found):
                found = list(found)
                for u in range(UNROLL):
                    spot = group * UNROLL + u
                    start = pl.multiple_of(cells[block, 5, spot], 8)
                    low = turned[pl.ds(start, PAD), :].reshape(PAD // 8, 8, lanes)
                    high = turned[pl.ds(start + DEEP, PAD), :].reshape(PAD // 8, 8, lanes)
                    mixed = low * row_of(lower, block * lanes + spot) + high * row_of(
                        upper, block * lanes + spot
                    )
                    move = (cells[block, 6, spot] + spot) & (lanes - 1)
                    found[u % 2] = found[u % 2] + pltpu.roll(mixed.reshape(PAD, lanes), move, 1)
                return tuple(found)

            zeros = jnp.zeros((PAD, lanes), jnp.float32)
            on_even, on_odd = lax.fori_loop(0, lanes // UNROLL, sample_group, (zeros, zeros))
            gathered[pl.ds(PAD * q, PAD), :] = jnp.where(
                even, on_even + turn(on_even, -1), on_odd + turn(on_odd, -1)
            )
        sampled[pl.ds(pl.multiple_of(tile * lanes, lanes), lanes), :] = gathered[...].T
        return carry

    lax.fori_loop(0, sampled.shape[0] // lanes, sample_tile, 0)


def row_of(table, number):
    return table[pl.ds(number, 8, stride=0), :]


def diffuse(field, norm, halos, weights, lower, upper, cells, n_lat):
    levels, rows, lanes = field.shape
    tall = rows + 2 * HALO
    whole = pl.BlockSpec(memory_space=pltpu.VMEM)
    scalars = pl.BlockSpec(memory_space=pltpu.SMEM)
    planes = levels + (levels + 1) // 2
    return pl.pallas_call(
        functools.partial(diffuse_kernel, n_lat),
        out_shape=(
            jax.ShapeDtypeStruct(field.shape, jnp.float32),
            jax.ShapeDtypeStruct((cells.shape[0] * PAD, lanes), jnp.float32),
        ),
        in_specs=[whole] * 9 + [scalars],
        out_specs=(whole, whole),
        scratch_shapes=[
            pltpu.VMEM((planes, tall, lanes), jnp.float32),
            pltpu.VMEM((planes, tall, lanes), jnp.float32),
            pltpu.VMEM((rows * DEEP, lanes), jnp.float32),
            pltpu.VMEM((lanes, lanes), jnp.float32),
        ],
        compiler_params=pltpu.CompilerParams(vmem_limit_bytes=24 << 20),
    )(field, norm, *halos, weights, lower, upper, cells)


def one_hot_slots(slots, q, rows):
    shape = (rows, slots.shape[1])
    number = lax.broadcasted_iota(jnp.int32, shape, 0) * (LANES // PAD) + q
    return jnp.where(number == slots, 1.0, 0.0)


def route_kernel(innovations, weights, place, owner_column, owner_row, ids, packet, slots, table):
    levels, count = innovations.shape
    total = packet.shape[0]
    same = owner_column[...] == owner_row[...]
    earlier = lax.broadcasted_iota(jnp.int32, (count, count), 0) < lax.broadcasted_iota(
        jnp.int32, (count, count), 1
    )
    rank = jnp.sum(jnp.where(jnp.logical_and(same, earlier), 1, 0), axis=0, keepdims=True)
    slot = owner_row[...] * CAPACITY + rank
    slots[...] = slot

    table[...] = jnp.zeros_like(table)
    table[pl.ds(0, levels), :] = innovations[...]
    table[pl.ds(levels, 4), :] = weights[...]
    table[pl.ds(levels + 4, 2), :] = place[...].astype(jnp.float32)
    flipped = jnp.concatenate(
        [table[:, pl.ds(start, LANES)].T for start in range(0, count, LANES)], axis=0
    )
    sent = jnp.zeros((total, LANES), jnp.float32)
    for q in range(LANES // PAD):
        moved = pltpu.roll(flipped, PAD * q, 1) if q else flipped
        sent += jnp.dot(
            one_hot_slots(slot, q, total),
            moved,
            precision=lax.Precision.HIGHEST,
            preferred_element_type=jnp.float32,
        )
    lane = lane_ids((total, LANES))
    row = lax.broadcasted_iota(jnp.int32, (total, LANES), 0)
    per_device = 2
    row_group = CAPACITY * PAD // LANES
    group = lax.rem(row // row_group, ids.shape[1] // per_device) * per_device
    first_row = lax.rem(row, row_group) == 0
    numbers = jnp.concatenate(
        [ids[...].astype(jnp.float32), jnp.zeros((1, LANES - ids.shape[1]), jnp.float32)], axis=1
    )
    for t in range(per_device):
        number = jnp.sum(jnp.where(lane == group + t, numbers, 0.0), axis=1, keepdims=True)
        spare = jnp.logical_and(first_row, lane == PAD * (t + 1) - 1)
        sent = jnp.where(spare, number, sent)
    packet[...] = sent


def route(innovations, weights, place, owners, ids, devices):
    whole = pl.BlockSpec(memory_space=pltpu.VMEM)
    count = innovations.shape[1]
    return pl.pallas_call(
        route_kernel,
        out_shape=(
            jax.ShapeDtypeStruct((devices * CAPACITY * PAD // LANES, LANES), jnp.float32),
            jax.ShapeDtypeStruct((1, count), jnp.int32),
        ),
        in_specs=[whole] * 6,
        out_specs=(whole, whole),
        scratch_shapes=[pltpu.VMEM((LANES, count), jnp.float32)],
        compiler_params=pltpu.CompilerParams(vmem_limit_bytes=BIG),
    )(innovations, weights, place, owners, owners.reshape(1, count), ids)


def post_kernel(has_coef, source, *refs):
    if has_coef:
        coef, tiles, target, west_cols, east_cols, south_coef, north_coef, late = refs[:8]
        held, send_sem, recv_sem, local_sem, pack_first, pack_last, staged, late_sem = refs[8:]
    else:
        target, held, send_sem, recv_sem, local_sem = refs
    n_lat, n_lon = source.shape[:2]
    lat, lon, up, down, right, left = neighbours(n_lat, n_lon)
    across = [lax.rem(lon + step, n_lon) for step in range(1, n_lon)]
    along = [lax.rem(lat + step, n_lat) for step in range(1, n_lat)]
    corners = [(up, right), (up, left), (down, right), (down, left)] if has_coef else []

    barrier = pltpu.get_barrier_semaphore()
    for other in across:
        pl.semaphore_signal(barrier, inc=1, device_id=(lat, other), device_id_type=MESH)
    for other in along:
        pl.semaphore_signal(barrier, inc=1, device_id=(other, lon), device_id_type=MESH)
    for there in corners:
        pl.semaphore_signal(barrier, inc=1, device_id=there, device_id_type=MESH)
    own = pltpu.make_async_copy(source.at[:, lon], held.at[:, lon], local_sem)
    own.start()
    moves = []
    if has_coef:
        count = late.shape[1]
        stage = pltpu.make_async_copy(tiles.at[pl.ds(EARLY, count)], staged, late_sem.at[count])
        stage.start()
        rows = coef.shape[1]
        low, high = packed_columns(
            lambda plane: coef[plane], coef.shape[0], rows, COLS, 0, COEF_PAIRS
        )
        pack_first[...] = low
        pack_last[...] = high
    pl.semaphore_wait(barrier, n_lon + n_lat - 2 + len(corners))

    def push(here, there, number, device):
        copy = pltpu.make_async_remote_copy(
            src_ref=here,
            dst_ref=there,
            send_sem=send_sem.at[number],
            recv_sem=recv_sem.at[number],
            device_id=device,
            device_id_type=MESH,
        )
        copy.start()
        return copy

    copies = [
        push(source.at[:, other], held.at[:, lon], number, (lat, other))
        for number, other in enumerate(across)
    ]
    edges = []
    if has_coef:
        first = pl.ds(0, HALO)
        last = pl.ds(rows - HALO, HALO)
        middle = pl.ds(HALO, rows)
        above = pl.ds(HALO + rows, HALO)
        for here, there, device in (
            (coef.at[:, last, :], south_coef, (up, lon)),
            (coef.at[:, first, :], north_coef, (down, lon)),
            (pack_last, west_cols.at[middle, :], (lat, right)),
            (pack_first, east_cols.at[middle, :], (lat, left)),
            (pack_last.at[last, :], west_cols.at[first, :], (up, right)),
            (pack_first.at[last, :], east_cols.at[first, :], (up, left)),
            (pack_last.at[first, :], west_cols.at[above, :], (down, right)),
            (pack_first.at[first, :], east_cols.at[above, :], (down, left)),
        ):
            edges.append(push(here, there, n_lon + n_lat + len(edges), device))
    if has_coef:
        stage.wait()
        for level in range(count):
            move = pltpu.make_async_copy(staged.at[level], late.at[:, level], late_sem.at[level])
            move.start()
            moves.append(move)
    own.wait()
    for copy in copies:
        copy.wait()
    copies = [
        push(held.at[other], target.at[lat], n_lon + number, (other, lon))
        for number, other in enumerate(along)
    ]
    own = pltpu.make_async_copy(held.at[lat], target.at[lat], local_sem)
    own.start()
    own.wait()
    for copy in copies + edges + moves:
        copy.wait()


def post(packet, n_lat, n_lon, collective_id, coef=None, tiles=None):
    whole = pl.BlockSpec(memory_space=pltpu.VMEM)
    anywhere = pl.BlockSpec(memory_space=pl.ANY)
    outside = pl.BlockSpec(memory_space=pltpu.HBM)
    blocks = packet.reshape(n_lat, n_lon, -1, LANES)
    has_coef = coef is not None
    sems = n_lon + n_lat + 8 * has_coef
    out_shape = [jax.ShapeDtypeStruct(blocks.shape, jnp.float32)]
    scratch = [
        pltpu.VMEM(blocks.shape, jnp.float32),
        pltpu.SemaphoreType.DMA((sems,)),
        pltpu.SemaphoreType.DMA((sems,)),
        pltpu.SemaphoreType.DMA,
    ]
    operands, in_specs, out_specs = [blocks], [whole], [outside if has_coef else whole]
    if has_coef:
        count, rows, lanes = coef.shape
        levels, slots, depth, _ = tiles.shape
        packed = jax.ShapeDtypeStruct((rows + 2 * HALO, lanes), jnp.float32)
        edge = jax.ShapeDtypeStruct((count, HALO, lanes), jnp.float32)
        late = jax.ShapeDtypeStruct((slots, levels - EARLY, depth, lanes), jnp.float32)
        out_shape += [packed, packed, edge, edge, late]
        scratch += [
            pltpu.VMEM((rows, lanes), jnp.float32),
            pltpu.VMEM((rows, lanes), jnp.float32),
            pltpu.VMEM((levels - EARLY, slots, depth, lanes), jnp.float32),
            pltpu.SemaphoreType.DMA((levels - EARLY + 1,)),
        ]
        operands += [coef, tiles]
        in_specs += [whole, anywhere]
        out_specs += [outside] * 5
    received, *rest = pl.pallas_call(
        functools.partial(post_kernel, has_coef),
        out_shape=out_shape,
        in_specs=in_specs,
        out_specs=out_specs,
        scratch_shapes=scratch,
        compiler_params=pltpu.CompilerParams(
            collective_id=collective_id, has_side_effects=True, vmem_limit_bytes=BIG if has_coef else 4 << 20
        ),
    )(*operands)
    return (received.reshape(packet.shape), *rest)


def spread_kernel(
    levels, packet, seen, lower, upper, cells_out, turned, observed, other, cells, sem
):
    total, lanes = packet.shape
    per_row = lanes // PAD
    tiles = total // lanes
    level_lane = PAD - 8
    sublane = lax.broadcasted_iota(jnp.int32, (8, lanes), 0)
    for tile in range(tiles):
        flipped = packet[pl.ds(tile * lanes, lanes), :].T
        turned[pl.ds(tile * lanes, lanes), :] = flipped
        for q in range(per_row):
            last = flipped[PAD * q + level_lane : PAD * (q + 1)].astype(jnp.int32)
            last = jnp.where(sublane == 5, last * DEEP, jnp.where(sublane == 6, lanes - last, last))
            cells_out[tile * per_row + q] = last
    copy = pltpu.make_async_copy(cells_out, cells, sem)
    copy.start()

    lane = lane_ids((lanes, lanes)).astype(jnp.float32)
    for tile in range(tiles):
        rows = packet[pl.ds(tile * lanes, lanes), :]
        for q in range(per_row):
            first, second, third, fourth, row, column = (
                jnp.broadcast_to(rows[:, n : n + 1], (lanes, lanes))
                for n in range(PAD * q + level_lane + 1, PAD * q + level_lane + 7)
            )
            here = lane == column
            beside = lane == column + 1.0
            block = pl.ds((tile * per_row + q) * lanes, lanes)
            lower[block, :] = jnp.where(here, first, jnp.where(beside, second, 0.0))
            upper[block, :] = jnp.where(here, third, jnp.where(beside, fourth, 0.0))

    is_level = lax.broadcasted_iota(jnp.int32, (PAD, lanes), 0) < levels
    parts = (observed, other)
    for part in parts:
        part[...] = jnp.zeros_like(part)
    copy.wait()

    def spread_block(block, carry):
        values = jnp.where(is_level, turned[pl.ds(pl.multiple_of(block * PAD, PAD), PAD), :], 0.0)

        def spread_group(group, carry):
            moved = pltpu.roll(values, lax.rem(lanes - group * UNROLL, lanes), 1)
            for u in range(UNROLL):
                spot = group * UNROLL + u
                value = jnp.broadcast_to(moved[:, u : u + 1], (PAD, lanes)).reshape(
                    PAD // 8, 8, lanes
                )
                part = parts[u % len(parts)]
                for table, offset in ((lower, 0), (upper, DEEP)):
                    start = pl.multiple_of(cells[block, 5, spot] + offset, 8)
                    added = (value * row_of(table, block * lanes + spot)).reshape(PAD, lanes)
                    part[pl.ds(start, PAD), :] = part[pl.ds(start, PAD), :] + added
            return carry

        lax.fori_loop(0, lanes // UNROLL, spread_group, 0)
        return carry

    lax.fori_loop(0, tiles * per_row, spread_block, 0)
    rows = seen.shape[1]
    for level in range(levels):
        at = pl.ds(level, rows, stride=DEEP)
        seen[level] = observed[at, :] + other[at, :]


def spread(packet, levels, rows):
    total, lanes = packet.shape
    whole = pl.BlockSpec(memory_space=pltpu.VMEM)
    blocks = total // PAD
    masks = jax.ShapeDtypeStruct((blocks * lanes, lanes), jnp.float32)
    return pl.pallas_call(
        functools.partial(spread_kernel, levels),
        out_shape=(
            jax.ShapeDtypeStruct((levels, rows, lanes), jnp.float32),
            masks,
            masks,
            jax.ShapeDtypeStruct((blocks, 8, lanes), jnp.int32),
        ),
        in_specs=[whole],
        out_specs=(whole,) * 4,
        scratch_shapes=[
            pltpu.VMEM(packet.shape, jnp.float32),
            pltpu.VMEM((rows * DEEP, lanes), jnp.float32),
            pltpu.VMEM((rows * DEEP, lanes), jnp.float32),
            pltpu.SMEM((blocks, 8, lanes), jnp.int32),
            pltpu.SemaphoreType.DMA,
        ],
        compiler_params=pltpu.CompilerParams(vmem_limit_bytes=20 << 20),
    )(packet)


def combine_kernel(cells, seen, early, late, norm, field):
    slots, _, depth, lanes = early.shape
    n_lon = lax.axis_size("lon")
    per_device = slots // n_lon
    per_row = lanes // PAD
    row_group = CAPACITY * PAD // lanes
    base = lax.axis_index("lat") * n_lon

    def one_tile(slot, carry):
        at = (base + slot // per_device) * row_group
        block = (at // lanes) * per_row + lax.rem(slot, per_device)
        rows = pl.ds(pl.multiple_of(cells[block, 7, lax.rem(at, lanes)] * depth, depth), depth)
        for part, tiles in ((pl.ds(0, early.shape[1]), early), (pl.ds(early.shape[1], late.shape[1]), late)):
            field[part, rows, :] = norm[part, rows, :] * (seen[part, rows, :] + tiles[slot])
        return carry

    lax.fori_loop(0, slots, one_tile, 0)


def combine(cells, seen, early, late, norm):
    whole = pl.BlockSpec(memory_space=pltpu.VMEM)
    return pl.pallas_call(
        combine_kernel,
        out_shape=jax.ShapeDtypeStruct(norm.shape, jnp.float32),
        in_specs=[pl.BlockSpec(memory_space=pltpu.SMEM)] + [whole] * 4,
        out_specs=whole,
        compiler_params=pltpu.CompilerParams(vmem_limit_bytes=8 << 20),
    )(cells, seen, early, late, norm)


def collect_kernel(levels, returned, slots, out):
    total, lanes = returned.shape
    flipped = jnp.concatenate(
        [returned[pl.ds(start, lanes), :].T for start in range(0, total, lanes)], axis=1
    )
    values = jnp.zeros((PAD, slots.shape[1]), jnp.float32)
    for q in range(lanes // PAD):
        values += jnp.dot(
            flipped[PAD * q : PAD * (q + 1)],
            one_hot_slots(slots[...], q, total),
            precision=lax.Precision.HIGHEST,
            preferred_element_type=jnp.float32,
        )
    out[...] = values[:levels]


def collect(returned, slots, levels):
    whole = pl.BlockSpec(memory_space=pltpu.VMEM)
    return pl.pallas_call(
        functools.partial(collect_kernel, levels),
        out_shape=jax.ShapeDtypeStruct((levels, slots.shape[1]), jnp.float32),
        in_specs=[whole] * 2,
        out_specs=whole,
        compiler_params=pltpu.CompilerParams(vmem_limit_bytes=8 << 20),
    )(returned, slots)


def on_device(
    innovations,
    owners,
    prof_row,
    prof_col,
    interp_weights,
    model_tiles,
    model_ids,
    face_x,
    face_y,
    cross_term,
    wet_mask,
    norm_factor,
):
    levels, rows, lanes = norm_factor.shape
    n_lat = lax.axis_size("lat")
    n_lon = lax.axis_size("lon")
    early = lax.all_to_all(
        jnp.transpose(model_tiles[:EARLY], (1, 0, 2, 3)), "lon", split_axis=0, concat_axis=0, tiled=True
    )
    coef = jnp.stack([face_x, face_y, cross_term, wet_mask.astype(jnp.float32)])
    place = jnp.stack([prof_row, prof_col])
    packet, slots = route(innovations, interp_weights, place, owners, model_ids, n_lat * n_lon)
    packet, *coef_halos, late = post(packet, n_lat, n_lon, 1, coef, model_tiles)
    late = lax.all_to_all(late, "lon", split_axis=0, concat_axis=0, tiled=True)
    seen, lower, upper, cells = spread(packet, levels, rows)
    weights = prepare(coef, coef_halos, n_lat)
    field = combine(cells, seen, early, late, norm_factor)
    halos = exchange(field, n_lat, n_lon)
    smoothed, sampled = diffuse(field, norm_factor, halos, weights, lower, upper, cells, n_lat)
    (returned,) = post(sampled, n_lat, n_lon, 2)
    profile_values = collect(returned, slots, levels)
    return (smoothed, profile_values)


def solution(mesh):
    in_specs = (
        P(None, ("lat", "lon")),
        P(("lat", "lon"), None),
        P(("lat", "lon")),
        P(("lat", "lon")),
        P(None, ("lat", "lon")),
        P(None, ("lat", "lon"), None, None),
        P(None, ("lat", "lon")),
        P("lat", "lon"),
        P("lat", "lon"),
        P("lat", "lon"),
        P("lat", "lon"),
        P(None, "lat", "lon"),
    )
    out_specs = (P(None, "lat", "lon"), P(None, ("lat", "lon")))
    return jax.shard_map(
        on_device, mesh=mesh, in_specs=in_specs, out_specs=out_specs, check_vma=False
    )
```

```python
import functools

import jax
import jax.numpy as jnp
from jax import lax
from jax.experimental import pallas as pl
from jax.experimental.pallas import tpu as pltpu
from jax.sharding import PartitionSpec as P

STEPS = 10
CAPACITY = 8
PAD = 32
DEEP = 40
UNROLL = 32
BIG = 62 << 20
HALO = 16
LANES = 128
COLS = 12
PAIRS = 6
COEF_PAIRS = 5
EARLY = 10
MIDDLE = 5
CHUNK = 40
EDGE = 4
MESH = pl.DeviceIdType.MESH


def lane_ids(shape):
    return lax.broadcasted_iota(jnp.int32, shape, len(shape) - 1)


def within(lane, start, width):
    start = start % LANES
    return jnp.logical_and(lane >= start, lane < start + width)


def turn(values, shift):
    shift = shift % LANES
    return pltpu.roll(values, shift, 1) if shift else values


def packed_columns(plane_of, planes, rows, cols, first_pair, pairs):
    lane = lane_ids((rows, LANES))
    low = jnp.zeros((rows, LANES), jnp.float32)
    high = jnp.zeros((rows, LANES), jnp.float32)
    for k in range(pairs):
        for half in range(2):
            plane = 2 * (first_pair + k) + half
            if plane >= planes:
                continue
            shift = cols * k + (LANES // 2) * half
            values = turn(plane_of(plane), shift)
            low = jnp.where(within(lane, shift, cols), values, low)
            high = jnp.where(within(lane, LANES - cols + shift, cols), values, high)
    return low, high


def strip_plane(first, second, east, west, k, cols, inside):
    half = LANES // 2
    lane = lane_ids(first.shape)
    upper_half = lane >= half
    lane = lane % half
    west_side = lane < half // 2
    low = jnp.where(west_side, turn(first, COLS), turn(first, half - COLS))
    high = jnp.where(west_side, turn(second, COLS + half), turn(second, -COLS))
    own = jnp.where(upper_half, high, low)
    east = jnp.where(
        jnp.logical_and(inside, within(lane, half - COLS, cols)),
        turn(east, half - COLS - cols * k),
        0.0,
    )
    west = jnp.where(
        jnp.logical_and(inside, within(lane, COLS - cols, cols)), turn(west, COLS - cols * k), east
    )
    return jnp.where(jnp.logical_and(lane >= COLS, lane < half - COLS), own, west)


def inside_domain(shape, rows, has_south, has_north):
    row = lax.broadcasted_iota(jnp.int32, shape, 0)
    return jnp.logical_and(
        jnp.logical_or(row >= HALO, has_south), jnp.logical_or(row < HALO + rows, has_north)
    )


def neighbours(n_lat, n_lon):
    lat = lax.axis_index("lat")
    lon = lax.axis_index("lon")
    up = lax.rem(lat + 1, n_lat)
    down = lax.rem(lat + n_lat - 1, n_lat)
    right = lax.rem(lon + 1, n_lon)
    left = lax.rem(lon + n_lon - 1, n_lon)
    return lat, lon, up, down, right, left


def exchange_kernel(
    n_lat,
    n_lon,
    field,
    west_cols,
    east_cols,
    south_rows,
    north_rows,
    pack_first,
    pack_last,
    pack_low,
    pack_high,
    send_sem,
    recv_sem,
):
    lat, lon, up, down, right, left = neighbours(n_lat, n_lon)
    levels, rows = field.shape[:2]

    barrier = pltpu.get_barrier_semaphore()
    for there in (
        (lat, right),
        (lat, left),
        (up, lon),
        (down, lon),
        (up, right),
        (up, left),
        (down, right),
        (down, left),
    ):
        pl.semaphore_signal(barrier, inc=1, device_id=there, device_id_type=MESH)

    copies = []

    def send(source, target, there):
        number = len(copies)
        copy = pltpu.make_async_remote_copy(
            src_ref=source,
            dst_ref=target,
            send_sem=send_sem.at[number],
            recv_sem=recv_sem.at[number],
            device_id=there,
            device_id_type=MESH,
        )
        copy.start()
        copies.append(copy)

    for level in range(levels):
        at = pl.ds(STEPS * level, STEPS)
        pack_high[at, :] = field[level, pl.ds(rows - STEPS, STEPS), :]
        pack_low[at, :] = field[level, pl.ds(0, STEPS), :]
    pl.semaphore_wait(barrier, 8)
    send(pack_high, south_rows, (up, lon))
    send(pack_low, north_rows, (down, lon))
    for tile in range(pack_first.shape[0]):
        low, high = packed_columns(
            lambda plane: field[plane], levels, rows, STEPS, tile * PAIRS, PAIRS
        )
        pack_first[tile] = low
        pack_last[tile] = high

    first = pl.ds(0, HALO)
    last = pl.ds(rows - HALO, HALO)
    own = pl.ds(HALO, rows)
    above = pl.ds(HALO + rows, HALO)
    send(pack_last, west_cols.at[:, own, :], (lat, right))
    send(pack_first, east_cols.at[:, own, :], (lat, left))
    send(pack_last.at[:, last, :], west_cols.at[:, first, :], (up, right))
    send(pack_first.at[:, last, :], east_cols.at[:, first, :], (up, left))
    send(pack_last.at[:, first, :], west_cols.at[:, above, :], (down, right))
    send(pack_first.at[:, first, :], east_cols.at[:, above, :], (down, left))
    for copy in copies:
        copy.wait()


def exchange(field, n_lat, n_lon):
    levels, rows, lanes = field.shape
    tiles = -(-((levels + 1) // 2) // PAIRS)
    edge = -(-levels * STEPS // 8) * 8
    whole = pl.BlockSpec(memory_space=pltpu.VMEM)
    packed = jax.ShapeDtypeStruct((tiles, rows + 2 * HALO, lanes), jnp.float32)
    edges = jax.ShapeDtypeStruct((edge, lanes), jnp.float32)
    return pl.pallas_call(
        functools.partial(exchange_kernel, n_lat, n_lon),
        out_shape=(packed, packed, edges, edges),
        in_specs=[whole],
        out_specs=[whole] * 4,
        scratch_shapes=[
            pltpu.VMEM((tiles, rows, lanes), jnp.float32),
            pltpu.VMEM((tiles, rows, lanes), jnp.float32),
            pltpu.VMEM((edge, lanes), jnp.float32),
            pltpu.VMEM((edge, lanes), jnp.float32),
            pltpu.SemaphoreType.DMA((8,)),
            pltpu.SemaphoreType.DMA((8,)),
        ],
        compiler_params=pltpu.CompilerParams(
            collective_id=0, has_side_effects=True, vmem_limit_bytes=8 << 20
        ),
    )(field)


def step_coefficients(
    n_lat, coef, west_cols, east_cols, south_coef, north_coef, weights, raw
):
    rows, lanes = coef.shape[1:]
    tall = rows + 2 * HALO
    half = lanes // 2
    has_south = lax.axis_index("lat") > 0
    has_north = lax.axis_index("lat") < n_lat - 1
    inside = inside_domain((tall, lanes), rows, has_south, has_north)
    upper_half = lane_ids((tall, lanes)) >= half
    for n in range(coef.shape[0]):
        plane = jnp.concatenate(
            [
                jnp.where(has_south, south_coef[n], 0.0),
                coef[n],
                jnp.where(has_north, north_coef[n], 0.0),
            ],
            axis=0,
        )
        raw[0, n] = plane
        both = strip_plane(plane, plane, east_cols[...], west_cols[...], n // 2, COLS, inside)
        mirrored = turn(both, half)
        raw[1, n] = jnp.where(upper_half, *((mirrored, both) if n % 2 == 0 else (both, mirrored)))

    def make_weights(step, carry):
        start = EDGE + step * CHUNK
        here = pl.ds(start, CHUNK)
        below = pl.ds(start - 1, CHUNK)
        above = pl.ds(start + 1, CHUNK)
        for kind in range(2):
            wet = raw[kind, 3, here, :]
            east = raw[kind, 0, here, :] * wet * turn(wet, -1)
            west = turn(east, 1)
            twist = 0.25 * raw[kind, 2, here, :] * wet
            north = raw[kind, 1, here, :] * wet * raw[kind, 3, above, :]
            south = raw[kind, 1, below, :] * raw[kind, 3, below, :] * wet
            keep = 1.0 - (east + west + north + south)
            for number, value in enumerate(
                (keep, north, south, west, turn(twist, 1), east, -turn(twist, -1))
            ):
                weights[kind, number, pl.ds(step * CHUNK, CHUNK), :] = value
        return carry

    lax.fori_loop(0, (tall - 2 * EDGE) // CHUNK, make_weights, 0)


def diffuse_kernel(
    n_lat,
    field,
    norm,
    west_cols,
    east_cols,
    south_rows,
    north_rows,
    weights,
    lower,
    upper,
    cells,
    out,
    sampled,
    grid,
    other,
    turned,
    gathered,
):
    levels, rows, lanes = field.shape
    tall = rows + 2 * HALO
    half = lanes // 2
    strips = (levels + 1) // 2
    has_south = lax.axis_index("lat") > 0
    has_north = lax.axis_index("lat") < n_lat - 1
    inside = inside_domain((tall, lanes), rows, has_south, has_north)

    for level in range(levels):
        at = pl.ds(STEPS * level, STEPS)
        grid[level, pl.ds(0, HALO), :] = jnp.zeros((HALO, lanes), jnp.float32)
        grid[level, pl.ds(HALO + rows, HALO), :] = jnp.zeros((HALO, lanes), jnp.float32)
        grid[level, pl.ds(HALO - STEPS, STEPS), :] = jnp.where(has_south, south_rows[at, :], 0.0)
        grid[level, pl.ds(HALO, rows), :] = field[level]
        grid[level, pl.ds(HALO + rows, STEPS), :] = jnp.where(has_north, north_rows[at, :], 0.0)
    for pair in range(strips):
        tile, k = divmod(pair, PAIRS)
        grid[levels + pair] = strip_plane(
            grid[2 * pair],
            grid[min(2 * pair + 1, levels - 1)],
            east_cols[tile],
            west_cols[tile],
            k,
            STEPS,
            inside,
        )

    count = (tall - 2 * EDGE) // CHUNK

    def sweep(source, target):
        def one_chunk(step, carry):
            start = EDGE + step * CHUNK
            here = pl.ds(start, CHUNK)
            below = pl.ds(start - 1, CHUNK)
            above = pl.ds(start + 1, CHUNK)
            own = pl.ds(step * CHUNK, CHUNK)
            for kind, planes in enumerate((range(levels), range(levels, levels + strips))):
                keep, north, south, to_left, twist_left, to_right, twist_right = (
                    weights[kind, number, own, :] for number in range(7)
                )
                for plane in planes:
                    centre = source[plane, here, :]
                    upper = source[plane, above, :]
                    lower = source[plane, below, :]
                    tilt = upper - lower
                    target[plane, here, :] = (
                        keep * centre
                        + (north * upper + south * lower)
                        + turn(to_left * centre + twist_left * tilt, -1)
                        + turn(to_right * centre + twist_right * tilt, 1)
                    )
            return carry

        lax.fori_loop(0, count, one_chunk, 0)

    def two_steps(number, carry):
        sweep(grid, other)
        sweep(other, grid)
        return carry

    lax.fori_loop(0, STEPS // 2, two_steps, 0)

    column = lane_ids((rows, lanes))
    inner = pl.ds(HALO, rows)
    for level in range(levels):
        edges = grid[levels + level // 2, inner, :]
        move = half * (level % 2)
        result = jnp.where(
            column < STEPS,
            turn(edges, -COLS - move),
            jnp.where(column >= lanes - STEPS, turn(edges, half + COLS - move), grid[level, inner, :]),
        )
        result = norm[level] * result
        out[level] = result
        turned[pl.ds(level, rows, stride=DEEP), :] = result
    for level in range(levels, PAD):
        turned[pl.ds(level, rows, stride=DEEP), :] = jnp.zeros((rows, lanes), jnp.float32)

    even = lane_ids((PAD, lanes)) % 2 == 0
    per_row = lanes // PAD

    def sample_tile(tile, carry):
        for q in range(per_row):
            block = tile * per_row + q

            def sample_group(group, found):
                found = list(found)
                for u in range(UNROLL):
                    spot = group * UNROLL + u
                    start = pl.multiple_of(cells[block, 5, spot], 8)
                    low = turned[pl.ds(start, PAD), :].reshape(PAD // 8, 8, lanes)
                    high = turned[pl.ds(start + DEEP, PAD), :].reshape(PAD // 8, 8, lanes)
                    mixed = low * row_of(lower, block * lanes + spot) + high * row_of(
                        upper, block * lanes + spot
                    )
                    move = (cells[block, 6, spot] + spot) & (lanes - 1)
                    found[u % 2] = found[u % 2] + pltpu.roll(mixed.reshape(PAD, lanes), move, 1)
                return tuple(found)

            zeros = jnp.zeros((PAD, lanes), jnp.float32)
            on_even, on_odd = lax.fori_loop(0, lanes // UNROLL, sample_group, (zeros, zeros))
            gathered[pl.ds(PAD * q, PAD), :] = jnp.where(
                even, on_even + turn(on_even, -1), on_odd + turn(on_odd, -1)
            )
        sampled[pl.ds(pl.multiple_of(tile * lanes, lanes), lanes), :] = gathered[...].T
        return carry

    lax.fori_loop(0, sampled.shape[0] // lanes, sample_tile, 0)


def row_of(table, number):
    return table[pl.ds(number, 8, stride=0), :]


def diffuse(field, norm, halos, weights, lower, upper, cells, n_lat):
    levels, rows, lanes = field.shape
    tall = rows + 2 * HALO
    whole = pl.BlockSpec(memory_space=pltpu.VMEM)
    scalars = pl.BlockSpec(memory_space=pltpu.SMEM)
    planes = levels + (levels + 1) // 2
    return pl.pallas_call(
        functools.partial(diffuse_kernel, n_lat),
        out_shape=(
            jax.ShapeDtypeStruct(field.shape, jnp.float32),
            jax.ShapeDtypeStruct((cells.shape[0] * PAD, lanes), jnp.float32),
        ),
        in_specs=[whole] * 9 + [scalars],
        out_specs=(whole, whole),
        scratch_shapes=[
            pltpu.VMEM((planes, tall, lanes), jnp.float32),
            pltpu.VMEM((planes, tall, lanes), jnp.float32),
            pltpu.VMEM((rows * DEEP, lanes), jnp.float32),
            pltpu.VMEM((lanes, lanes), jnp.float32),
        ],
        compiler_params=pltpu.CompilerParams(vmem_limit_bytes=24 << 20),
    )(field, norm, *halos, weights, lower, upper, cells)


def one_hot_slots(slots, q, rows):
    shape = (rows, slots.shape[1])
    number = lax.broadcasted_iota(jnp.int32, shape, 0) * (LANES // PAD) + q
    return jnp.where(number == slots, 1.0, 0.0)


def route_kernel(innovations, weights, place, owner_column, owner_row, ids, packet, slots, table):
    levels, count = innovations.shape
    total = packet.shape[0]
    same = owner_column[...] == owner_row[...]
    earlier = lax.broadcasted_iota(jnp.int32, (count, count), 0) < lax.broadcasted_iota(
        jnp.int32, (count, count), 1
    )
    rank = jnp.sum(jnp.where(jnp.logical_and(same, earlier), 1, 0), axis=0, keepdims=True)
    slot = owner_row[...] * CAPACITY + rank
    slots[...] = slot

    table[...] = jnp.zeros_like(table)
    table[pl.ds(0, levels), :] = innovations[...]
    table[pl.ds(levels, 4), :] = weights[...]
    table[pl.ds(levels + 4, 2), :] = place[...].astype(jnp.float32)
    flipped = jnp.concatenate(
        [table[:, pl.ds(start, LANES)].T for start in range(0, count, LANES)], axis=0
    )
    sent = jnp.zeros((total, LANES), jnp.float32)
    for q in range(LANES // PAD):
        moved = pltpu.roll(flipped, PAD * q, 1) if q else flipped
        sent += jnp.dot(
            one_hot_slots(slot, q, total),
            moved,
            precision=lax.Precision.HIGHEST,
            preferred_element_type=jnp.float32,
        )
    lane = lane_ids((total, LANES))
    row = lax.broadcasted_iota(jnp.int32, (total, LANES), 0)
    per_device = 2
    row_group = CAPACITY * PAD // LANES
    group = lax.rem(row // row_group, ids.shape[1] // per_device) * per_device
    first_row = lax.rem(row, row_group) == 0
    numbers = jnp.concatenate(
        [ids[...].astype(jnp.float32), jnp.zeros((1, LANES - ids.shape[1]), jnp.float32)], axis=1
    )
    for t in range(per_device):
        number = jnp.sum(jnp.where(lane == group + t, numbers, 0.0), axis=1, keepdims=True)
        spare = jnp.logical_and(first_row, lane == PAD * (t + 1) - 1)
        sent = jnp.where(spare, number, sent)
    packet[...] = sent


def route(innovations, weights, place, owners, ids, devices):
    whole = pl.BlockSpec(memory_space=pltpu.VMEM)
    count = innovations.shape[1]
    return pl.pallas_call(
        route_kernel,
        out_shape=(
            jax.ShapeDtypeStruct((devices * CAPACITY * PAD // LANES, LANES), jnp.float32),
            jax.ShapeDtypeStruct((1, count), jnp.int32),
        ),
        in_specs=[whole] * 6,
        out_specs=(whole, whole),
        scratch_shapes=[pltpu.VMEM((LANES, count), jnp.float32)],
        compiler_params=pltpu.CompilerParams(vmem_limit_bytes=BIG),
    )(innovations, weights, place, owners, owners.reshape(1, count), ids)


def post_kernel(has_coef, source, *refs):
    if has_coef:
        coef, tiles, target, weights_out, middle, late = refs[:6]
        held, send_sem, recv_sem, local_sem, pack_first, pack_last, staged, late_sem = refs[6:14]
        west_cols, east_cols, south_coef, north_coef, weights, raw = refs[14:]
    else:
        target, held, send_sem, recv_sem, local_sem = refs
    n_lat, n_lon = source.shape[:2]
    lat, lon, up, down, right, left = neighbours(n_lat, n_lon)
    across = [lax.rem(lon + step, n_lon) for step in range(1, n_lon)]
    along = [lax.rem(lat + step, n_lat) for step in range(1, n_lat)]
    corners = [(up, right), (up, left), (down, right), (down, left)] if has_coef else []

    barrier = pltpu.get_barrier_semaphore()
    for other in across:
        pl.semaphore_signal(barrier, inc=1, device_id=(lat, other), device_id_type=MESH)
    for other in along:
        pl.semaphore_signal(barrier, inc=1, device_id=(other, lon), device_id_type=MESH)
    for there in corners:
        pl.semaphore_signal(barrier, inc=1, device_id=there, device_id_type=MESH)
    own = pltpu.make_async_copy(source.at[:, lon], held.at[:, lon], local_sem)
    own.start()
    moves = []
    if has_coef:
        count = late.shape[1]
        stage = pltpu.make_async_copy(
            tiles.at[pl.ds(EARLY, MIDDLE + count)], staged, late_sem.at[count]
        )
        stage.start()
        rows = coef.shape[1]
        low, high = packed_columns(
            lambda plane: coef[plane], coef.shape[0], rows, COLS, 0, COEF_PAIRS
        )
        pack_first[...] = low
        pack_last[...] = high
    pl.semaphore_wait(barrier, n_lon + n_lat - 2 + len(corners))

    def push(here, there, number, device):
        copy = pltpu.make_async_remote_copy(
            src_ref=here,
            dst_ref=there,
            send_sem=send_sem.at[number],
            recv_sem=recv_sem.at[number],
            device_id=device,
            device_id_type=MESH,
        )
        copy.start()
        return copy

    copies = [
        push(source.at[:, other], held.at[:, lon], number, (lat, other))
        for number, other in enumerate(across)
    ]
    edges = []
    if has_coef:
        first = pl.ds(0, HALO)
        last = pl.ds(rows - HALO, HALO)
        within_rows = pl.ds(HALO, rows)
        above = pl.ds(HALO + rows, HALO)
        for here, there, device in (
            (coef.at[:, last, :], south_coef, (up, lon)),
            (coef.at[:, first, :], north_coef, (down, lon)),
            (pack_last, west_cols.at[within_rows, :], (lat, right)),
            (pack_first, east_cols.at[within_rows, :], (lat, left)),
            (pack_last.at[last, :], west_cols.at[first, :], (up, right)),
            (pack_first.at[last, :], east_cols.at[first, :], (up, left)),
            (pack_last.at[first, :], west_cols.at[above, :], (down, right)),
            (pack_first.at[first, :], east_cols.at[above, :], (down, left)),
        ):
            edges.append(push(here, there, n_lon + n_lat + len(edges), device))
    if has_coef:
        stage.wait()
        for level in range(count):
            move = pltpu.make_async_copy(
                staged.at[MIDDLE + level], late.at[:, level], late_sem.at[level]
            )
            move.start()
            moves.append(move)
    own.wait()
    for copy in copies:
        copy.wait()
    copies = [
        push(held.at[other], target.at[lat], n_lon + number, (other, lon))
        for number, other in enumerate(along)
    ]
    own = pltpu.make_async_copy(held.at[lat], target.at[lat], local_sem)
    own.start()
    if has_coef:
        per_device = middle.shape[2]
        levels = pl.ds(0, MIDDLE)
        mine = pltpu.make_async_copy(
            staged.at[levels, pl.ds(per_device * lon, per_device)],
            middle.at[lon],
            late_sem.at[count + 1],
        )
        mine.start()
        moves.append(mine)
        for number, other in enumerate(across):
            copies.append(
                push(
                    staged.at[levels, pl.ds(per_device * other, per_device)],
                    middle.at[lon],
                    n_lon + n_lat + 8 + number,
                    (lat, other),
                )
            )
        for copy in edges:
            copy.wait()
        step_coefficients(n_lat, coef, west_cols, east_cols, south_coef, north_coef, weights, raw)
        move = pltpu.make_async_copy(weights, weights_out, late_sem.at[count + 2])
        move.start()
        moves.append(move)
    own.wait()
    for copy in copies + moves:
        copy.wait()


def post(packet, n_lat, n_lon, collective_id, coef=None, tiles=None):
    whole = pl.BlockSpec(memory_space=pltpu.VMEM)
    anywhere = pl.BlockSpec(memory_space=pl.ANY)
    outside = pl.BlockSpec(memory_space=pltpu.HBM)
    blocks = packet.reshape(n_lat, n_lon, -1, LANES)
    has_coef = coef is not None
    sems = n_lon + n_lat + (8 + n_lon) * has_coef
    out_shape = [jax.ShapeDtypeStruct(blocks.shape, jnp.float32)]
    scratch = [
        pltpu.VMEM(blocks.shape, jnp.float32),
        pltpu.SemaphoreType.DMA((sems,)),
        pltpu.SemaphoreType.DMA((sems,)),
        pltpu.SemaphoreType.DMA,
    ]
    operands, in_specs, out_specs = [blocks], [whole], [outside if has_coef else whole]
    if has_coef:
        count, rows, lanes = coef.shape
        levels, slots, depth, _ = tiles.shape
        tall = rows + 2 * HALO
        table = (2, 7, tall - 2 * EDGE, lanes)
        later = levels - EARLY - MIDDLE
        out_shape += [
            jax.ShapeDtypeStruct(shape, jnp.float32)
            for shape in (
                table,
                (n_lon, MIDDLE, slots // n_lon, depth, lanes),
                (slots, later, depth, lanes),
            )
        ]
        scratch += [
            pltpu.VMEM((rows, lanes), jnp.float32),
            pltpu.VMEM((rows, lanes), jnp.float32),
            pltpu.VMEM((MIDDLE + later, slots, depth, lanes), jnp.float32),
            pltpu.SemaphoreType.DMA((later + 3,)),
            pltpu.VMEM((tall, lanes), jnp.float32),
            pltpu.VMEM((tall, lanes), jnp.float32),
            pltpu.VMEM((count, HALO, lanes), jnp.float32),
            pltpu.VMEM((count, HALO, lanes), jnp.float32),
            pltpu.VMEM(table, jnp.float32),
            pltpu.VMEM((2, count, tall, lanes), jnp.float32),
        ]
        operands += [coef, tiles]
        in_specs += [whole, anywhere]
        out_specs += [outside] * 3
    received, *rest = pl.pallas_call(
        functools.partial(post_kernel, has_coef),
        out_shape=out_shape,
        in_specs=in_specs,
        out_specs=out_specs,
        scratch_shapes=scratch,
        compiler_params=pltpu.CompilerParams(
            collective_id=collective_id, has_side_effects=True, vmem_limit_bytes=BIG if has_coef else 4 << 20
        ),
    )(*operands)
    return (received.reshape(packet.shape), *rest)


def spread_kernel(
    levels, packet, seen, lower, upper, cells_out, turned, observed, other, cells, sem
):
    total, lanes = packet.shape
    per_row = lanes // PAD
    tiles = total // lanes
    level_lane = PAD - 8
    sublane = lax.broadcasted_iota(jnp.int32, (8, lanes), 0)
    for tile in range(tiles):
        flipped = packet[pl.ds(tile * lanes, lanes), :].T
        turned[pl.ds(tile * lanes, lanes), :] = flipped
        for q in range(per_row):
            last = flipped[PAD * q + level_lane : PAD * (q + 1)].astype(jnp.int32)
            last = jnp.where(sublane == 5, last * DEEP, jnp.where(sublane == 6, lanes - last, last))
            cells_out[tile * per_row + q] = last
    copy = pltpu.make_async_copy(cells_out, cells, sem)
    copy.start()

    lane = lane_ids((lanes, lanes)).astype(jnp.float32)
    for tile in range(tiles):
        rows = packet[pl.ds(tile * lanes, lanes), :]
        for q in range(per_row):
            first, second, third, fourth, row, column = (
                jnp.broadcast_to(rows[:, n : n + 1], (lanes, lanes))
                for n in range(PAD * q + level_lane + 1, PAD * q + level_lane + 7)
            )
            here = lane == column
            beside = lane == column + 1.0
            block = pl.ds((tile * per_row + q) * lanes, lanes)
            lower[block, :] = jnp.where(here, first, jnp.where(beside, second, 0.0))
            upper[block, :] = jnp.where(here, third, jnp.where(beside, fourth, 0.0))

    is_level = lax.broadcasted_iota(jnp.int32, (PAD, lanes), 0) < levels
    parts = (observed, other)
    for part in parts:
        part[...] = jnp.zeros_like(part)
    copy.wait()

    def spread_block(block, carry):
        values = jnp.where(is_level, turned[pl.ds(pl.multiple_of(block * PAD, PAD), PAD), :], 0.0)

        def spread_group(group, carry):
            moved = pltpu.roll(values, lax.rem(lanes - group * UNROLL, lanes), 1)
            for u in range(UNROLL):
                spot = group * UNROLL + u
                value = jnp.broadcast_to(moved[:, u : u + 1], (PAD, lanes)).reshape(
                    PAD // 8, 8, lanes
                )
                part = parts[u % len(parts)]
                for table, offset in ((lower, 0), (upper, DEEP)):
                    start = pl.multiple_of(cells[block, 5, spot] + offset, 8)
                    added = (value * row_of(table, block * lanes + spot)).reshape(PAD, lanes)
                    part[pl.ds(start, PAD), :] = part[pl.ds(start, PAD), :] + added
            return carry

        lax.fori_loop(0, lanes // UNROLL, spread_group, 0)
        return carry

    lax.fori_loop(0, tiles * per_row, spread_block, 0)
    rows = seen.shape[1]
    for level in range(levels):
        at = pl.ds(level, rows, stride=DEEP)
        seen[level] = observed[at, :] + other[at, :]


def spread(packet, levels, rows):
    total, lanes = packet.shape
    whole = pl.BlockSpec(memory_space=pltpu.VMEM)
    blocks = total // PAD
    masks = jax.ShapeDtypeStruct((blocks * lanes, lanes), jnp.float32)
    return pl.pallas_call(
        functools.partial(spread_kernel, levels),
        out_shape=(
            jax.ShapeDtypeStruct((levels, rows, lanes), jnp.float32),
            masks,
            masks,
            jax.ShapeDtypeStruct((blocks, 8, lanes), jnp.int32),
        ),
        in_specs=[whole],
        out_specs=(whole,) * 4,
        scratch_shapes=[
            pltpu.VMEM(packet.shape, jnp.float32),
            pltpu.VMEM((rows * DEEP, lanes), jnp.float32),
            pltpu.VMEM((rows * DEEP, lanes), jnp.float32),
            pltpu.SMEM((blocks, 8, lanes), jnp.int32),
            pltpu.SemaphoreType.DMA,
        ],
        compiler_params=pltpu.CompilerParams(vmem_limit_bytes=20 << 20),
    )(packet)


def combine_kernel(cells, seen, early, middle, late, norm, field):
    slots, _, depth, lanes = early.shape
    n_lon = lax.axis_size("lon")
    per_device = slots // n_lon
    per_row = lanes // PAD
    row_group = CAPACITY * PAD // lanes
    base = lax.axis_index("lat") * n_lon

    def one_tile(slot, carry):
        at = (base + slot // per_device) * row_group
        block = (at // lanes) * per_row + lax.rem(slot, per_device)
        rows = pl.ds(pl.multiple_of(cells[block, 7, lax.rem(at, lanes)] * depth, depth), depth)
        start = 0
        for tiles in (
            early[slot],
            middle[slot // per_device, :, lax.rem(slot, per_device)],
            late[slot],
        ):
            part = pl.ds(start, tiles.shape[0])
            start += tiles.shape[0]
            field[part, rows, :] = norm[part, rows, :] * (seen[part, rows, :] + tiles)
        return carry

    lax.fori_loop(0, slots, one_tile, 0)


def combine(cells, seen, early, middle, late, norm):
    whole = pl.BlockSpec(memory_space=pltpu.VMEM)
    return pl.pallas_call(
        combine_kernel,
        out_shape=jax.ShapeDtypeStruct(norm.shape, jnp.float32),
        in_specs=[pl.BlockSpec(memory_space=pltpu.SMEM)] + [whole] * 5,
        out_specs=whole,
        compiler_params=pltpu.CompilerParams(vmem_limit_bytes=8 << 20),
    )(cells, seen, early, middle, late, norm)


def collect_kernel(levels, returned, slots, out):
    total, lanes = returned.shape
    flipped = jnp.concatenate(
        [returned[pl.ds(start, lanes), :].T for start in range(0, total, lanes)], axis=1
    )
    values = jnp.zeros((PAD, slots.shape[1]), jnp.float32)
    for q in range(lanes // PAD):
        values += jnp.dot(
            flipped[PAD * q : PAD * (q + 1)],
            one_hot_slots(slots[...], q, total),
            precision=lax.Precision.HIGHEST,
            preferred_element_type=jnp.float32,
        )
    out[...] = values[:levels]


def collect(returned, slots, levels):
    whole = pl.BlockSpec(memory_space=pltpu.VMEM)
    return pl.pallas_call(
        functools.partial(collect_kernel, levels),
        out_shape=jax.ShapeDtypeStruct((levels, slots.shape[1]), jnp.float32),
        in_specs=[whole] * 2,
        out_specs=whole,
        compiler_params=pltpu.CompilerParams(vmem_limit_bytes=8 << 20),
    )(returned, slots)


def on_device(
    innovations,
    owners,
    prof_row,
    prof_col,
    interp_weights,
    model_tiles,
    model_ids,
    face_x,
    face_y,
    cross_term,
    wet_mask,
    norm_factor,
):
    levels, rows, lanes = norm_factor.shape
    n_lat = lax.axis_size("lat")
    n_lon = lax.axis_size("lon")
    early = lax.all_to_all(
        jnp.transpose(model_tiles[:EARLY], (1, 0, 2, 3)), "lon", split_axis=0, concat_axis=0, tiled=True
    )
    coef = jnp.stack([face_x, face_y, cross_term, wet_mask.astype(jnp.float32)])
    place = jnp.stack([prof_row, prof_col])
    packet, slots = route(innovations, interp_weights, place, owners, model_ids, n_lat * n_lon)
    packet, weights, middle, late = post(packet, n_lat, n_lon, 1, coef, model_tiles)
    late = lax.all_to_all(late, "lon", split_axis=0, concat_axis=0, tiled=True)
    seen, lower, upper, cells = spread(packet, levels, rows)
    field = combine(cells, seen, early, middle, late, norm_factor)
    halos = exchange(field, n_lat, n_lon)
    smoothed, sampled = diffuse(field, norm_factor, halos, weights, lower, upper, cells, n_lat)
    (returned,) = post(sampled, n_lat, n_lon, 2)
    profile_values = collect(returned, slots, levels)
    return (smoothed, profile_values)


def solution(mesh):
    in_specs = (
        P(None, ("lat", "lon")),
        P(("lat", "lon"), None),
        P(("lat", "lon")),
        P(("lat", "lon")),
        P(None, ("lat", "lon")),
        P(None, ("lat", "lon"), None, None),
        P(None, ("lat", "lon")),
        P("lat", "lon"),
        P("lat", "lon"),
        P("lat", "lon"),
        P("lat", "lon"),
        P(None, "lat", "lon"),
    )
    out_specs = (P(None, "lat", "lon"), P(None, ("lat", "lon")))
    return jax.shard_map(
        on_device, mesh=mesh, in_specs=in_specs, out_specs=out_specs, check_vma=False
    )
```

```python
import functools

import jax
import jax.numpy as jnp
from jax import lax
from jax.experimental import pallas as pl
from jax.experimental.pallas import tpu as pltpu
from jax.sharding import PartitionSpec as P

STEPS = 10
CAPACITY = 8
PAD = 32
DEEP = 40
UNROLL = 32
BIG = 62 << 20
HALO = 16
LANES = 128
COLS = 12
PAIRS = 6
COEF_PAIRS = 5
EARLY = 10
MIDDLE = 5
CHUNK = 40
EDGE = 4
MESH = pl.DeviceIdType.MESH


def lane_ids(shape):
    return lax.broadcasted_iota(jnp.int32, shape, len(shape) - 1)


SPARE = ((0, 60, 50, 4, 60), (0, 124, 114, 4, 120), (1, 60, 50, 2, 52))


def spare_columns(cols, last):
    values = jnp.zeros(cols.shape[1:], jnp.float32)
    lane = lane_ids(values.shape)
    place = COLS - STEPS if last else LANES // 2 - COLS
    for tile, first_lane, last_lane, width, _ in SPARE:
        moved = turn(cols[tile], place - (last_lane if last else first_lane))
        values = jnp.where(within(lane, place, width), moved, values)
        place += width
    return values


def within(lane, start, width):
    start = start % LANES
    return jnp.logical_and(lane >= start, lane < start + width)


def turn(values, shift):
    shift = shift % LANES
    return pltpu.roll(values, shift, 1) if shift else values


def packed_columns(plane_of, planes, rows, cols, first_pair, pairs):
    lane = lane_ids((rows, LANES))
    low = jnp.zeros((rows, LANES), jnp.float32)
    high = jnp.zeros((rows, LANES), jnp.float32)
    for k in range(pairs):
        for half in range(2):
            plane = 2 * (first_pair + k) + half
            if plane >= planes:
                continue
            shift = cols * k + (LANES // 2) * half
            values = turn(plane_of(plane), shift)
            low = jnp.where(within(lane, shift, cols), values, low)
            high = jnp.where(within(lane, LANES - cols + shift, cols), values, high)
    return low, high


def strip_plane(first, second, east, west, k, cols, inside):
    half = LANES // 2
    lane = lane_ids(first.shape)
    upper_half = lane >= half
    lane = lane % half
    west_side = lane < half // 2
    low = jnp.where(west_side, turn(first, COLS), turn(first, half - COLS))
    high = jnp.where(west_side, turn(second, COLS + half), turn(second, -COLS))
    own = jnp.where(upper_half, high, low)
    east = jnp.where(
        jnp.logical_and(inside, within(lane, half - COLS, cols)),
        east if k is None else turn(east, half - COLS - cols * k),
        0.0,
    )
    west = jnp.where(
        jnp.logical_and(inside, within(lane, COLS - cols, cols)),
        west if k is None else turn(west, COLS - cols * k),
        east,
    )
    return jnp.where(jnp.logical_and(lane >= COLS, lane < half - COLS), own, west)


def inside_domain(shape, rows, has_south, has_north):
    row = lax.broadcasted_iota(jnp.int32, shape, 0)
    return jnp.logical_and(
        jnp.logical_or(row >= HALO, has_south), jnp.logical_or(row < HALO + rows, has_north)
    )


def neighbours(n_lat, n_lon):
    lat = lax.axis_index("lat")
    lon = lax.axis_index("lon")
    up = lax.rem(lat + 1, n_lat)
    down = lax.rem(lat + n_lat - 1, n_lat)
    right = lax.rem(lon + 1, n_lon)
    left = lax.rem(lon + n_lon - 1, n_lon)
    return lat, lon, up, down, right, left


def exchange_kernel(
    n_lat,
    n_lon,
    field,
    west_cols,
    east_cols,
    south_rows,
    north_rows,
    pack_first,
    pack_last,
    pack_low,
    pack_high,
    send_sem,
    recv_sem,
):
    lat, lon, up, down, right, left = neighbours(n_lat, n_lon)
    levels, rows = field.shape[:2]

    barrier = pltpu.get_barrier_semaphore()
    for there in (
        (lat, right),
        (lat, left),
        (up, lon),
        (down, lon),
        (up, right),
        (up, left),
        (down, right),
        (down, left),
    ):
        pl.semaphore_signal(barrier, inc=1, device_id=there, device_id_type=MESH)

    copies = []

    def send(source, target, there):
        number = len(copies)
        copy = pltpu.make_async_remote_copy(
            src_ref=source,
            dst_ref=target,
            send_sem=send_sem.at[number],
            recv_sem=recv_sem.at[number],
            device_id=there,
            device_id_type=MESH,
        )
        copy.start()
        copies.append(copy)

    for level in range(levels):
        at = pl.ds(STEPS * level, STEPS)
        pack_high[at, :] = field[level, pl.ds(rows - STEPS, STEPS), :]
        pack_low[at, :] = field[level, pl.ds(0, STEPS), :]
    lane = lane_ids((rows, LANES))
    for tile in range(pack_first.shape[0]):
        low, high = packed_columns(
            lambda plane: field[plane], levels, rows, STEPS, tile * PAIRS, PAIRS
        )
        for at, first_lane, last_lane, width, shift in SPARE:
            if at == tile:
                values = turn(field[levels - 1], shift)
                low = jnp.where(within(lane, first_lane, width), values, low)
                high = jnp.where(within(lane, last_lane, width), values, high)
        pack_first[tile] = low
        pack_last[tile] = high
    pl.semaphore_wait(barrier, 8)
    first = pl.ds(0, HALO)
    last = pl.ds(rows - HALO, HALO)
    own = pl.ds(HALO, rows)
    above = pl.ds(HALO + rows, HALO)
    send(pack_last, west_cols.at[:, own, :], (lat, right))
    send(pack_first, east_cols.at[:, own, :], (lat, left))
    send(pack_last.at[:, last, :], west_cols.at[:, first, :], (up, right))
    send(pack_first.at[:, last, :], east_cols.at[:, first, :], (up, left))
    send(pack_last.at[:, first, :], west_cols.at[:, above, :], (down, right))
    send(pack_first.at[:, first, :], east_cols.at[:, above, :], (down, left))
    send(pack_high, south_rows, (up, lon))
    send(pack_low, north_rows, (down, lon))
    for copy in copies:
        copy.wait()


def exchange(field, n_lat, n_lon):
    levels, rows, lanes = field.shape
    tiles = levels // 2 // PAIRS
    edge = -(-levels * STEPS // 8) * 8
    whole = pl.BlockSpec(memory_space=pltpu.VMEM)
    packed = jax.ShapeDtypeStruct((tiles, rows + 2 * HALO, lanes), jnp.float32)
    edges = jax.ShapeDtypeStruct((edge, lanes), jnp.float32)
    return pl.pallas_call(
        functools.partial(exchange_kernel, n_lat, n_lon),
        out_shape=(packed, packed, edges, edges),
        in_specs=[whole],
        out_specs=[whole] * 4,
        scratch_shapes=[
            pltpu.VMEM((tiles, rows, lanes), jnp.float32),
            pltpu.VMEM((tiles, rows, lanes), jnp.float32),
            pltpu.VMEM((edge, lanes), jnp.float32),
            pltpu.VMEM((edge, lanes), jnp.float32),
            pltpu.SemaphoreType.DMA((8,)),
            pltpu.SemaphoreType.DMA((8,)),
        ],
        compiler_params=pltpu.CompilerParams(
            collective_id=0, has_side_effects=True, vmem_limit_bytes=8 << 20
        ),
    )(field)


def step_coefficients(
    n_lat, coef, west_cols, east_cols, south_coef, north_coef, weights, raw
):
    rows, lanes = coef.shape[1:]
    tall = rows + 2 * HALO
    half = lanes // 2
    has_south = lax.axis_index("lat") > 0
    has_north = lax.axis_index("lat") < n_lat - 1
    inside = inside_domain((tall, lanes), rows, has_south, has_north)
    upper_half = lane_ids((tall, lanes)) >= half
    for n in range(coef.shape[0]):
        plane = jnp.concatenate(
            [
                jnp.where(has_south, south_coef[n], 0.0),
                coef[n],
                jnp.where(has_north, north_coef[n], 0.0),
            ],
            axis=0,
        )
        raw[0, n] = plane
        both = strip_plane(plane, plane, east_cols[...], west_cols[...], n // 2, COLS, inside)
        mirrored = turn(both, half)
        raw[1, n] = jnp.where(upper_half, *((mirrored, both) if n % 2 == 0 else (both, mirrored)))

    def make_weights(step, carry):
        start = EDGE + step * CHUNK
        here = pl.ds(start, CHUNK)
        below = pl.ds(start - 1, CHUNK)
        above = pl.ds(start + 1, CHUNK)
        for kind in range(2):
            wet = raw[kind, 3, here, :]
            east = raw[kind, 0, here, :] * wet * turn(wet, -1)
            west = turn(east, 1)
            twist = 0.25 * raw[kind, 2, here, :] * wet
            north = raw[kind, 1, here, :] * wet * raw[kind, 3, above, :]
            south = raw[kind, 1, below, :] * raw[kind, 3, below, :] * wet
            keep = 1.0 - (east + west + north + south)
            for number, value in enumerate(
                (keep, north, south, west, turn(twist, 1), east, -turn(twist, -1))
            ):
                weights[kind, number, pl.ds(step * CHUNK, CHUNK), :] = value
        return carry

    lax.fori_loop(0, (tall - 2 * EDGE) // CHUNK, make_weights, 0)


def diffuse_kernel(
    n_lat,
    field,
    norm,
    west_cols,
    east_cols,
    south_rows,
    north_rows,
    weights,
    lower,
    upper,
    cells,
    out,
    sampled,
    grid,
    other,
    turned,
    gathered,
):
    levels, rows, lanes = field.shape
    tall = rows + 2 * HALO
    half = lanes // 2
    strips = (levels + 1) // 2
    has_south = lax.axis_index("lat") > 0
    has_north = lax.axis_index("lat") < n_lat - 1
    inside = inside_domain((tall, lanes), rows, has_south, has_north)

    for level in range(levels):
        at = pl.ds(STEPS * level, STEPS)
        grid[level, pl.ds(0, HALO), :] = jnp.zeros((HALO, lanes), jnp.float32)
        grid[level, pl.ds(HALO + rows, HALO), :] = jnp.zeros((HALO, lanes), jnp.float32)
        grid[level, pl.ds(HALO - STEPS, STEPS), :] = jnp.where(has_south, south_rows[at, :], 0.0)
        grid[level, pl.ds(HALO, rows), :] = field[level]
        grid[level, pl.ds(HALO + rows, STEPS), :] = jnp.where(has_north, north_rows[at, :], 0.0)
    for pair in range(strips):
        tile, k = divmod(pair, PAIRS)
        alone = 2 * pair + 1 >= levels
        grid[levels + pair] = strip_plane(
            grid[2 * pair],
            grid[min(2 * pair + 1, levels - 1)],
            spare_columns(east_cols, False) if alone else east_cols[tile],
            spare_columns(west_cols, True) if alone else west_cols[tile],
            None if alone else k,
            STEPS,
            inside,
        )

    count = (tall - 2 * EDGE) // CHUNK

    def sweep(source, target):
        def one_chunk(step, carry):
            start = EDGE + step * CHUNK
            here = pl.ds(start, CHUNK)
            below = pl.ds(start - 1, CHUNK)
            above = pl.ds(start + 1, CHUNK)
            own = pl.ds(step * CHUNK, CHUNK)
            for kind, planes in enumerate((range(levels), range(levels, levels + strips))):
                keep, north, south, to_left, twist_left, to_right, twist_right = (
                    weights[kind, number, own, :] for number in range(7)
                )
                for plane in planes:
                    centre = source[plane, here, :]
                    upper = source[plane, above, :]
                    lower = source[plane, below, :]
                    tilt = upper - lower
                    target[plane, here, :] = (
                        keep * centre
                        + (north * upper + south * lower)
                        + turn(to_left * centre + twist_left * tilt, -1)
                        + turn(to_right * centre + twist_right * tilt, 1)
                    )
            return carry

        lax.fori_loop(0, count, one_chunk, 0)

    def two_steps(number, carry):
        sweep(grid, other)
        sweep(other, grid)
        return carry

    lax.fori_loop(0, STEPS // 2, two_steps, 0)

    column = lane_ids((rows, lanes))
    inner = pl.ds(HALO, rows)
    for level in range(levels):
        edges = grid[levels + level // 2, inner, :]
        move = half * (level % 2)
        result = jnp.where(
            column < STEPS,
            turn(edges, -COLS - move),
            jnp.where(column >= lanes - STEPS, turn(edges, half + COLS - move), grid[level, inner, :]),
        )
        result = norm[level] * result
        out[level] = result
        turned[pl.ds(level, rows, stride=DEEP), :] = result
    for level in range(levels, PAD):
        turned[pl.ds(level, rows, stride=DEEP), :] = jnp.zeros((rows, lanes), jnp.float32)

    even = lane_ids((PAD, lanes)) % 2 == 0
    per_row = lanes // PAD

    def sample_tile(tile, carry):
        for q in range(per_row):
            block = tile * per_row + q

            def sample_group(group, found):
                found = list(found)
                for u in range(UNROLL):
                    spot = group * UNROLL + u
                    start = pl.multiple_of(cells[block, 5, spot], 8)
                    low = turned[pl.ds(start, PAD), :].reshape(PAD // 8, 8, lanes)
                    high = turned[pl.ds(start + DEEP, PAD), :].reshape(PAD // 8, 8, lanes)
                    mixed = low * row_of(lower, block * lanes + spot) + high * row_of(
                        upper, block * lanes + spot
                    )
                    move = (cells[block, 6, spot] + spot) & (lanes - 1)
                    found[u % 2] = found[u % 2] + pltpu.roll(mixed.reshape(PAD, lanes), move, 1)
                return tuple(found)

            zeros = jnp.zeros((PAD, lanes), jnp.float32)
            on_even, on_odd = lax.fori_loop(0, lanes // UNROLL, sample_group, (zeros, zeros))
            gathered[pl.ds(PAD * q, PAD), :] = jnp.where(
                even, on_even + turn(on_even, -1), on_odd + turn(on_odd, -1)
            )
        sampled[pl.ds(pl.multiple_of(tile * lanes, lanes), lanes), :] = gathered[...].T
        return carry

    lax.fori_loop(0, sampled.shape[0] // lanes, sample_tile, 0)


def row_of(table, number):
    return table[pl.ds(number, 8, stride=0), :]


def diffuse(field, norm, halos, weights, lower, upper, cells, n_lat):
    levels, rows, lanes = field.shape
    tall = rows + 2 * HALO
    whole = pl.BlockSpec(memory_space=pltpu.VMEM)
    scalars = pl.BlockSpec(memory_space=pltpu.SMEM)
    planes = levels + (levels + 1) // 2
    return pl.pallas_call(
        functools.partial(diffuse_kernel, n_lat),
        out_shape=(
            jax.ShapeDtypeStruct(field.shape, jnp.float32),
            jax.ShapeDtypeStruct((cells.shape[0] * PAD, lanes), jnp.float32),
        ),
        in_specs=[whole] * 9 + [scalars],
        out_specs=(whole, whole),
        scratch_shapes=[
            pltpu.VMEM((planes, tall, lanes), jnp.float32),
            pltpu.VMEM((planes, tall, lanes), jnp.float32),
            pltpu.VMEM((rows * DEEP, lanes), jnp.float32),
            pltpu.VMEM((lanes, lanes), jnp.float32),
        ],
        compiler_params=pltpu.CompilerParams(vmem_limit_bytes=24 << 20),
    )(field, norm, *halos, weights, lower, upper, cells)


def one_hot_slots(slots, q, rows):
    shape = (rows, slots.shape[1])
    number = lax.broadcasted_iota(jnp.int32, shape, 0) * (LANES // PAD) + q
    return jnp.where(number == slots, 1.0, 0.0)


def route_kernel(innovations, weights, place, owner_column, owner_row, ids, packet, slots, table):
    levels, count = innovations.shape
    total = packet.shape[0]
    same = owner_column[...] == owner_row[...]
    earlier = lax.broadcasted_iota(jnp.int32, (count, count), 0) < lax.broadcasted_iota(
        jnp.int32, (count, count), 1
    )
    rank = jnp.sum(jnp.where(jnp.logical_and(same, earlier), 1, 0), axis=0, keepdims=True)
    slot = owner_row[...] * CAPACITY + rank
    slots[...] = slot

    table[...] = jnp.zeros_like(table)
    table[pl.ds(0, levels), :] = innovations[...]
    table[pl.ds(levels, 4), :] = weights[...]
    table[pl.ds(levels + 4, 2), :] = place[...].astype(jnp.float32)
    flipped = jnp.concatenate(
        [table[:, pl.ds(start, LANES)].T for start in range(0, count, LANES)], axis=0
    )
    sent = jnp.zeros((total, LANES), jnp.float32)
    for q in range(LANES // PAD):
        moved = pltpu.roll(flipped, PAD * q, 1) if q else flipped
        sent += jnp.dot(
            one_hot_slots(slot, q, total),
            moved,
            precision=lax.Precision.HIGHEST,
            preferred_element_type=jnp.float32,
        )
    lane = lane_ids((total, LANES))
    row = lax.broadcasted_iota(jnp.int32, (total, LANES), 0)
    per_device = 2
    row_group = CAPACITY * PAD // LANES
    group = lax.rem(row // row_group, ids.shape[1] // per_device) * per_device
    first_row = lax.rem(row, row_group) == 0
    numbers = jnp.concatenate(
        [ids[...].astype(jnp.float32), jnp.zeros((1, LANES - ids.shape[1]), jnp.float32)], axis=1
    )
    for t in range(per_device):
        number = jnp.sum(jnp.where(lane == group + t, numbers, 0.0), axis=1, keepdims=True)
        spare = jnp.logical_and(first_row, lane == PAD * (t + 1) - 1)
        sent = jnp.where(spare, number, sent)
    packet[...] = sent


def route(innovations, weights, place, owners, ids, devices):
    whole = pl.BlockSpec(memory_space=pltpu.VMEM)
    count = innovations.shape[1]
    return pl.pallas_call(
        route_kernel,
        out_shape=(
            jax.ShapeDtypeStruct((devices * CAPACITY * PAD // LANES, LANES), jnp.float32),
            jax.ShapeDtypeStruct((1, count), jnp.int32),
        ),
        in_specs=[whole] * 6,
        out_specs=(whole, whole),
        scratch_shapes=[pltpu.VMEM((LANES, count), jnp.float32)],
        compiler_params=pltpu.CompilerParams(vmem_limit_bytes=BIG),
    )(innovations, weights, place, owners, owners.reshape(1, count), ids)


def post_kernel(has_coef, source, *refs):
    if has_coef:
        coef, tiles, target, weights_out, middle, late = refs[:6]
        held, send_sem, recv_sem, local_sem, pack_first, pack_last, staged, late_sem = refs[6:14]
        west_cols, east_cols, south_coef, north_coef, weights, raw = refs[14:]
    else:
        target, held, send_sem, recv_sem, local_sem = refs
    n_lat, n_lon = source.shape[:2]
    lat, lon, up, down, right, left = neighbours(n_lat, n_lon)
    across = [lax.rem(lon + step, n_lon) for step in range(1, n_lon)]
    along = [lax.rem(lat + step, n_lat) for step in range(1, n_lat)]
    corners = [(up, right), (up, left), (down, right), (down, left)] if has_coef else []

    barrier = pltpu.get_barrier_semaphore()
    for other in across:
        pl.semaphore_signal(barrier, inc=1, device_id=(lat, other), device_id_type=MESH)
    for other in along:
        pl.semaphore_signal(barrier, inc=1, device_id=(other, lon), device_id_type=MESH)
    for there in corners:
        pl.semaphore_signal(barrier, inc=1, device_id=there, device_id_type=MESH)
    own = pltpu.make_async_copy(source.at[:, lon], held.at[:, lon], local_sem)
    own.start()
    moves = []
    if has_coef:
        count = late.shape[1]
        stage = pltpu.make_async_copy(
            tiles.at[pl.ds(EARLY, MIDDLE + count)], staged, late_sem.at[count]
        )
        stage.start()
        rows = coef.shape[1]
        low, high = packed_columns(
            lambda plane: coef[plane], coef.shape[0], rows, COLS, 0, COEF_PAIRS
        )
        pack_first[...] = low
        pack_last[...] = high
    pl.semaphore_wait(barrier, n_lon + n_lat - 2 + len(corners))

    def push(here, there, number, device):
        copy = pltpu.make_async_remote_copy(
            src_ref=here,
            dst_ref=there,
            send_sem=send_sem.at[number],
            recv_sem=recv_sem.at[number],
            device_id=device,
            device_id_type=MESH,
        )
        copy.start()
        return copy

    copies = [
        push(source.at[:, other], held.at[:, lon], number, (lat, other))
        for number, other in enumerate(across)
    ]
    edges = []
    if has_coef:
        first = pl.ds(0, HALO)
        last = pl.ds(rows - HALO, HALO)
        within_rows = pl.ds(HALO, rows)
        above = pl.ds(HALO + rows, HALO)
        for here, there, device in (
            (coef.at[:, last, :], south_coef, (up, lon)),
            (coef.at[:, first, :], north_coef, (down, lon)),
            (pack_last, west_cols.at[within_rows, :], (lat, right)),
            (pack_first, east_cols.at[within_rows, :], (lat, left)),
            (pack_last.at[last, :], west_cols.at[first, :], (up, right)),
            (pack_first.at[last, :], east_cols.at[first, :], (up, left)),
            (pack_last.at[first, :], west_cols.at[above, :], (down, right)),
            (pack_first.at[first, :], east_cols.at[above, :], (down, left)),
        ):
            edges.append(push(here, there, n_lon + n_lat + len(edges), device))
    if has_coef:
        stage.wait()
        for level in range(count):
            move = pltpu.make_async_copy(
                staged.at[MIDDLE + level], late.at[:, level], late_sem.at[level]
            )
            move.start()
            moves.append(move)
    own.wait()
    for copy in copies:
        copy.wait()
    copies = [
        push(held.at[other], target.at[lat], n_lon + number, (other, lon))
        for number, other in enumerate(along)
    ]
    own = pltpu.make_async_copy(held.at[lat], target.at[lat], local_sem)
    own.start()
    if has_coef:
        per_device = middle.shape[2]
        levels = pl.ds(0, MIDDLE)
        mine = pltpu.make_async_copy(
            staged.at[levels, pl.ds(per_device * lon, per_device)],
            middle.at[lon],
            late_sem.at[count + 1],
        )
        mine.start()
        moves.append(mine)
        for number, other in enumerate(across):
            copies.append(
                push(
                    staged.at[levels, pl.ds(per_device * other, per_device)],
                    middle.at[lon],
                    n_lon + n_lat + 8 + number,
                    (lat, other),
                )
            )
        for copy in edges:
            copy.wait()
        step_coefficients(n_lat, coef, west_cols, east_cols, south_coef, north_coef, weights, raw)
        move = pltpu.make_async_copy(weights, weights_out, late_sem.at[count + 2])
        move.start()
        moves.append(move)
    own.wait()
    for copy in copies + moves:
        copy.wait()


def post(packet, n_lat, n_lon, collective_id, coef=None, tiles=None):
    whole = pl.BlockSpec(memory_space=pltpu.VMEM)
    anywhere = pl.BlockSpec(memory_space=pl.ANY)
    outside = pl.BlockSpec(memory_space=pltpu.HBM)
    blocks = packet.reshape(n_lat, n_lon, -1, LANES)
    has_coef = coef is not None
    sems = n_lon + n_lat + (8 + n_lon) * has_coef
    out_shape = [jax.ShapeDtypeStruct(blocks.shape, jnp.float32)]
    scratch = [
        pltpu.VMEM(blocks.shape, jnp.float32),
        pltpu.SemaphoreType.DMA((sems,)),
        pltpu.SemaphoreType.DMA((sems,)),
        pltpu.SemaphoreType.DMA,
    ]
    operands, in_specs, out_specs = [blocks], [whole], [outside if has_coef else whole]
    if has_coef:
        count, rows, lanes = coef.shape
        levels, slots, depth, _ = tiles.shape
        tall = rows + 2 * HALO
        table = (2, 7, tall - 2 * EDGE, lanes)
        later = levels - EARLY - MIDDLE
        out_shape += [
            jax.ShapeDtypeStruct(shape, jnp.float32)
            for shape in (
                table,
                (n_lon, MIDDLE, slots // n_lon, depth, lanes),
                (slots, later, depth, lanes),
            )
        ]
        scratch += [
            pltpu.VMEM((rows, lanes), jnp.float32),
            pltpu.VMEM((rows, lanes), jnp.float32),
            pltpu.VMEM((MIDDLE + later, slots, depth, lanes), jnp.float32),
            pltpu.SemaphoreType.DMA((later + 3,)),
            pltpu.VMEM((tall, lanes), jnp.float32),
            pltpu.VMEM((tall, lanes), jnp.float32),
            pltpu.VMEM((count, HALO, lanes), jnp.float32),
            pltpu.VMEM((count, HALO, lanes), jnp.float32),
            pltpu.VMEM(table, jnp.float32),
            pltpu.VMEM((2, count, tall, lanes), jnp.float32),
        ]
        operands += [coef, tiles]
        in_specs += [whole, anywhere]
        out_specs += [outside] * 3
    received, *rest = pl.pallas_call(
        functools.partial(post_kernel, has_coef),
        out_shape=out_shape,
        in_specs=in_specs,
        out_specs=out_specs,
        scratch_shapes=scratch,
        compiler_params=pltpu.CompilerParams(
            collective_id=collective_id, has_side_effects=True, vmem_limit_bytes=BIG if has_coef else 4 << 20
        ),
    )(*operands)
    return (received.reshape(packet.shape), *rest)


def spread_kernel(
    levels, packet, seen, lower, upper, cells_out, turned, observed, other, cells, sem
):
    total, lanes = packet.shape
    per_row = lanes // PAD
    tiles = total // lanes
    level_lane = PAD - 8
    sublane = lax.broadcasted_iota(jnp.int32, (8, lanes), 0)
    for tile in range(tiles):
        flipped = packet[pl.ds(tile * lanes, lanes), :].T
        turned[pl.ds(tile * lanes, lanes), :] = flipped
        for q in range(per_row):
            last = flipped[PAD * q + level_lane : PAD * (q + 1)].astype(jnp.int32)
            last = jnp.where(sublane == 5, last * DEEP, jnp.where(sublane == 6, lanes - last, last))
            cells_out[tile * per_row + q] = last
    copy = pltpu.make_async_copy(cells_out, cells, sem)
    copy.start()

    lane = lane_ids((lanes, lanes)).astype(jnp.float32)
    for tile in range(tiles):
        rows = packet[pl.ds(tile * lanes, lanes), :]
        for q in range(per_row):
            first, second, third, fourth, row, column = (
                jnp.broadcast_to(rows[:, n : n + 1], (lanes, lanes))
                for n in range(PAD * q + level_lane + 1, PAD * q + level_lane + 7)
            )
            here = lane == column
            beside = lane == column + 1.0
            block = pl.ds((tile * per_row + q) * lanes, lanes)
            lower[block, :] = jnp.where(here, first, jnp.where(beside, second, 0.0))
            upper[block, :] = jnp.where(here, third, jnp.where(beside, fourth, 0.0))

    is_level = lax.broadcasted_iota(jnp.int32, (PAD, lanes), 0) < levels
    parts = (observed, other)
    for part in parts:
        part[...] = jnp.zeros_like(part)
    copy.wait()

    def spread_block(block, carry):
        values = jnp.where(is_level, turned[pl.ds(pl.multiple_of(block * PAD, PAD), PAD), :], 0.0)

        def spread_group(group, carry):
            moved = pltpu.roll(values, lax.rem(lanes - group * UNROLL, lanes), 1)
            for u in range(UNROLL):
                spot = group * UNROLL + u
                value = jnp.broadcast_to(moved[:, u : u + 1], (PAD, lanes)).reshape(
                    PAD // 8, 8, lanes
                )
                part = parts[u % len(parts)]
                for table, offset in ((lower, 0), (upper, DEEP)):
                    start = pl.multiple_of(cells[block, 5, spot] + offset, 8)
                    added = (value * row_of(table, block * lanes + spot)).reshape(PAD, lanes)
                    part[pl.ds(start, PAD), :] = part[pl.ds(start, PAD), :] + added
            return carry

        lax.fori_loop(0, lanes // UNROLL, spread_group, 0)
        return carry

    lax.fori_loop(0, tiles * per_row, spread_block, 0)
    rows = seen.shape[1]
    for level in range(levels):
        at = pl.ds(level, rows, stride=DEEP)
        seen[level] = observed[at, :] + other[at, :]


def spread(packet, levels, rows):
    total, lanes = packet.shape
    whole = pl.BlockSpec(memory_space=pltpu.VMEM)
    blocks = total // PAD
    masks = jax.ShapeDtypeStruct((blocks * lanes, lanes), jnp.float32)
    return pl.pallas_call(
        functools.partial(spread_kernel, levels),
        out_shape=(
            jax.ShapeDtypeStruct((levels, rows, lanes), jnp.float32),
            masks,
            masks,
            jax.ShapeDtypeStruct((blocks, 8, lanes), jnp.int32),
        ),
        in_specs=[whole],
        out_specs=(whole,) * 4,
        scratch_shapes=[
            pltpu.VMEM(packet.shape, jnp.float32),
            pltpu.VMEM((rows * DEEP, lanes), jnp.float32),
            pltpu.VMEM((rows * DEEP, lanes), jnp.float32),
            pltpu.SMEM((blocks, 8, lanes), jnp.int32),
            pltpu.SemaphoreType.DMA,
        ],
        compiler_params=pltpu.CompilerParams(vmem_limit_bytes=20 << 20),
    )(packet)


def combine_kernel(cells, seen, early, middle, late, norm, field):
    slots, _, depth, lanes = early.shape
    n_lon = lax.axis_size("lon")
    per_device = slots // n_lon
    per_row = lanes // PAD
    row_group = CAPACITY * PAD // lanes
    base = lax.axis_index("lat") * n_lon

    def one_tile(slot, carry):
        at = (base + slot // per_device) * row_group
        block = (at // lanes) * per_row + lax.rem(slot, per_device)
        rows = pl.ds(pl.multiple_of(cells[block, 7, lax.rem(at, lanes)] * depth, depth), depth)
        start = 0
        for tiles in (
            early[slot],
            middle[slot // per_device, :, lax.rem(slot, per_device)],
            late[slot],
        ):
            part = pl.ds(start, tiles.shape[0])
            start += tiles.shape[0]
            field[part, rows, :] = norm[part, rows, :] * (seen[part, rows, :] + tiles)
        return carry

    lax.fori_loop(0, slots, one_tile, 0)


def combine(cells, seen, early, middle, late, norm):
    whole = pl.BlockSpec(memory_space=pltpu.VMEM)
    return pl.pallas_call(
        combine_kernel,
        out_shape=jax.ShapeDtypeStruct(norm.shape, jnp.float32),
        in_specs=[pl.BlockSpec(memory_space=pltpu.SMEM)] + [whole] * 5,
        out_specs=whole,
        compiler_params=pltpu.CompilerParams(vmem_limit_bytes=8 << 20),
    )(cells, seen, early, middle, late, norm)


def collect_kernel(levels, returned, slots, out):
    total, lanes = returned.shape
    flipped = jnp.concatenate(
        [returned[pl.ds(start, lanes), :].T for start in range(0, total, lanes)], axis=1
    )
    values = jnp.zeros((PAD, slots.shape[1]), jnp.float32)
    for q in range(lanes // PAD):
        values += jnp.dot(
            flipped[PAD * q : PAD * (q + 1)],
            one_hot_slots(slots[...], q, total),
            precision=lax.Precision.HIGHEST,
            preferred_element_type=jnp.float32,
        )
    out[...] = values[:levels]


def collect(returned, slots, levels):
    whole = pl.BlockSpec(memory_space=pltpu.VMEM)
    return pl.pallas_call(
        functools.partial(collect_kernel, levels),
        out_shape=jax.ShapeDtypeStruct((levels, slots.shape[1]), jnp.float32),
        in_specs=[whole] * 2,
        out_specs=whole,
        compiler_params=pltpu.CompilerParams(vmem_limit_bytes=8 << 20),
    )(returned, slots)


def on_device(
    innovations,
    owners,
    prof_row,
    prof_col,
    interp_weights,
    model_tiles,
    model_ids,
    face_x,
    face_y,
    cross_term,
    wet_mask,
    norm_factor,
):
    levels, rows, lanes = norm_factor.shape
    n_lat = lax.axis_size("lat")
    n_lon = lax.axis_size("lon")
    early = lax.all_to_all(
        jnp.transpose(model_tiles[:EARLY], (1, 0, 2, 3)), "lon", split_axis=0, concat_axis=0, tiled=True
    )
    coef = jnp.stack([face_x, face_y, cross_term, wet_mask.astype(jnp.float32)])
    place = jnp.stack([prof_row, prof_col])
    packet, slots = route(innovations, interp_weights, place, owners, model_ids, n_lat * n_lon)
    packet, weights, middle, late = post(packet, n_lat, n_lon, 1, coef, model_tiles)
    late = lax.all_to_all(late, "lon", split_axis=0, concat_axis=0, tiled=True)
    seen, lower, upper, cells = spread(packet, levels, rows)
    field = combine(cells, seen, early, middle, late, norm_factor)
    halos = exchange(field, n_lat, n_lon)
    smoothed, sampled = diffuse(field, norm_factor, halos, weights, lower, upper, cells, n_lat)
    (returned,) = post(sampled, n_lat, n_lon, 2)
    profile_values = collect(returned, slots, levels)
    return (smoothed, profile_values)


def solution(mesh):
    in_specs = (
        P(None, ("lat", "lon")),
        P(("lat", "lon"), None),
        P(("lat", "lon")),
        P(("lat", "lon")),
        P(None, ("lat", "lon")),
        P(None, ("lat", "lon"), None, None),
        P(None, ("lat", "lon")),
        P("lat", "lon"),
        P("lat", "lon"),
        P("lat", "lon"),
        P("lat", "lon"),
        P(None, "lat", "lon"),
    )
    out_specs = (P(None, "lat", "lon"), P(None, ("lat", "lon")))
    return jax.shard_map(
        on_device, mesh=mesh, in_specs=in_specs, out_specs=out_specs, check_vma=False
    )
```

```python
import functools

import jax
import jax.numpy as jnp
from jax import lax
from jax.experimental import pallas as pl
from jax.experimental.pallas import tpu as pltpu
from jax.sharding import PartitionSpec as P

STEPS = 10
CAPACITY = 8
PAD = 32
DEEP = 40
UNROLL = 128
BIG = 62 << 20
HALO = 16
LANES = 128
COLS = 12
PAIRS = 6
COEF_PAIRS = 5
EARLY = 10
MIDDLE = 5
CHUNK = 40
EDGE = 4
MESH = pl.DeviceIdType.MESH


def lane_ids(shape):
    return lax.broadcasted_iota(jnp.int32, shape, len(shape) - 1)


SPARE = ((0, 60, 50, 4, 60), (0, 124, 114, 4, 120), (1, 60, 50, 2, 52))


def spare_columns(cols, last):
    values = jnp.zeros(cols.shape[1:], jnp.float32)
    lane = lane_ids(values.shape)
    place = COLS - STEPS if last else LANES // 2 - COLS
    for tile, first_lane, last_lane, width, _ in SPARE:
        moved = turn(cols[tile], place - (last_lane if last else first_lane))
        values = jnp.where(within(lane, place, width), moved, values)
        place += width
    return values


def within(lane, start, width):
    start = start % LANES
    return jnp.logical_and(lane >= start, lane < start + width)


def turn(values, shift):
    shift = shift % LANES
    return pltpu.roll(values, shift, 1) if shift else values


def packed_columns(plane_of, planes, rows, cols, first_pair, pairs):
    lane = lane_ids((rows, LANES))
    low = jnp.zeros((rows, LANES), jnp.float32)
    high = jnp.zeros((rows, LANES), jnp.float32)
    for k in range(pairs):
        for half in range(2):
            plane = 2 * (first_pair + k) + half
            if plane >= planes:
                continue
            shift = cols * k + (LANES // 2) * half
            values = turn(plane_of(plane), shift)
            low = jnp.where(within(lane, shift, cols), values, low)
            high = jnp.where(within(lane, LANES - cols + shift, cols), values, high)
    return low, high


def strip_plane(first, second, east, west, k, cols, inside):
    half = LANES // 2
    lane = lane_ids(first.shape)
    upper_half = lane >= half
    lane = lane % half
    west_side = lane < half // 2
    low = jnp.where(west_side, turn(first, COLS), turn(first, half - COLS))
    high = jnp.where(west_side, turn(second, COLS + half), turn(second, -COLS))
    own = jnp.where(upper_half, high, low)
    east = jnp.where(
        jnp.logical_and(inside, within(lane, half - COLS, cols)),
        east if k is None else turn(east, half - COLS - cols * k),
        0.0,
    )
    west = jnp.where(
        jnp.logical_and(inside, within(lane, COLS - cols, cols)),
        west if k is None else turn(west, COLS - cols * k),
        east,
    )
    return jnp.where(jnp.logical_and(lane >= COLS, lane < half - COLS), own, west)


def inside_domain(shape, rows, has_south, has_north):
    row = lax.broadcasted_iota(jnp.int32, shape, 0)
    return jnp.logical_and(
        jnp.logical_or(row >= HALO, has_south), jnp.logical_or(row < HALO + rows, has_north)
    )


def neighbours(n_lat, n_lon):
    lat = lax.axis_index("lat")
    lon = lax.axis_index("lon")
    up = lax.rem(lat + 1, n_lat)
    down = lax.rem(lat + n_lat - 1, n_lat)
    right = lax.rem(lon + 1, n_lon)
    left = lax.rem(lon + n_lon - 1, n_lon)
    return lat, lon, up, down, right, left


def exchange_kernel(
    n_lat,
    n_lon,
    field,
    west_cols,
    east_cols,
    south_rows,
    north_rows,
    pack_first,
    pack_last,
    pack_low,
    pack_high,
    send_sem,
    recv_sem,
):
    lat, lon, up, down, right, left = neighbours(n_lat, n_lon)
    levels, rows = field.shape[:2]

    barrier = pltpu.get_barrier_semaphore()
    for there in (
        (lat, right),
        (lat, left),
        (up, lon),
        (down, lon),
        (up, right),
        (up, left),
        (down, right),
        (down, left),
    ):
        pl.semaphore_signal(barrier, inc=1, device_id=there, device_id_type=MESH)

    copies = []

    def send(source, target, there):
        number = len(copies)
        copy = pltpu.make_async_remote_copy(
            src_ref=source,
            dst_ref=target,
            send_sem=send_sem.at[number],
            recv_sem=recv_sem.at[number],
            device_id=there,
            device_id_type=MESH,
        )
        copy.start()
        copies.append(copy)

    for level in range(levels):
        at = pl.ds(STEPS * level, STEPS)
        pack_high[at, :] = field[level, pl.ds(rows - STEPS, STEPS), :]
        pack_low[at, :] = field[level, pl.ds(0, STEPS), :]
    lane = lane_ids((rows, LANES))
    for tile in range(pack_first.shape[0]):
        low, high = packed_columns(
            lambda plane: field[plane], levels, rows, STEPS, tile * PAIRS, PAIRS
        )
        for at, first_lane, last_lane, width, shift in SPARE:
            if at == tile:
                values = turn(field[levels - 1], shift)
                low = jnp.where(within(lane, first_lane, width), values, low)
                high = jnp.where(within(lane, last_lane, width), values, high)
        pack_first[tile] = low
        pack_last[tile] = high
    pl.semaphore_wait(barrier, 8)
    first = pl.ds(0, HALO)
    last = pl.ds(rows - HALO, HALO)
    own = pl.ds(HALO, rows)
    above = pl.ds(HALO + rows, HALO)
    send(pack_last, west_cols.at[:, own, :], (lat, right))
    send(pack_first, east_cols.at[:, own, :], (lat, left))
    send(pack_last.at[:, last, :], west_cols.at[:, first, :], (up, right))
    send(pack_first.at[:, last, :], east_cols.at[:, first, :], (up, left))
    send(pack_last.at[:, first, :], west_cols.at[:, above, :], (down, right))
    send(pack_first.at[:, first, :], east_cols.at[:, above, :], (down, left))
    send(pack_high, south_rows, (up, lon))
    send(pack_low, north_rows, (down, lon))
    for copy in copies:
        copy.wait()


def exchange(field, n_lat, n_lon):
    levels, rows, lanes = field.shape
    tiles = levels // 2 // PAIRS
    edge = -(-levels * STEPS // 8) * 8
    whole = pl.BlockSpec(memory_space=pltpu.VMEM)
    packed = jax.ShapeDtypeStruct((tiles, rows + 2 * HALO, lanes), jnp.float32)
    edges = jax.ShapeDtypeStruct((edge, lanes), jnp.float32)
    return pl.pallas_call(
        functools.partial(exchange_kernel, n_lat, n_lon),
        out_shape=(packed, packed, edges, edges),
        in_specs=[whole],
        out_specs=[whole] * 4,
        scratch_shapes=[
            pltpu.VMEM((tiles, rows, lanes), jnp.float32),
            pltpu.VMEM((tiles, rows, lanes), jnp.float32),
            pltpu.VMEM((edge, lanes), jnp.float32),
            pltpu.VMEM((edge, lanes), jnp.float32),
            pltpu.SemaphoreType.DMA((8,)),
            pltpu.SemaphoreType.DMA((8,)),
        ],
        compiler_params=pltpu.CompilerParams(
            collective_id=0, has_side_effects=True, vmem_limit_bytes=8 << 20
        ),
    )(field)


def step_coefficients(
    n_lat, coef, west_cols, east_cols, south_coef, north_coef, weights, raw
):
    rows, lanes = coef.shape[1:]
    tall = rows + 2 * HALO
    half = lanes // 2
    has_south = lax.axis_index("lat") > 0
    has_north = lax.axis_index("lat") < n_lat - 1
    inside = inside_domain((tall, lanes), rows, has_south, has_north)
    upper_half = lane_ids((tall, lanes)) >= half
    for n in range(coef.shape[0]):
        plane = jnp.concatenate(
            [
                jnp.where(has_south, south_coef[n], 0.0),
                coef[n],
                jnp.where(has_north, north_coef[n], 0.0),
            ],
            axis=0,
        )
        raw[0, n] = plane
        both = strip_plane(plane, plane, east_cols[...], west_cols[...], n // 2, COLS, inside)
        mirrored = turn(both, half)
        raw[1, n] = jnp.where(upper_half, *((mirrored, both) if n % 2 == 0 else (both, mirrored)))

    def make_weights(step, carry):
        start = EDGE + step * CHUNK
        here = pl.ds(start, CHUNK)
        below = pl.ds(start - 1, CHUNK)
        above = pl.ds(start + 1, CHUNK)
        for kind in range(2):
            wet = raw[kind, 3, here, :]
            east = raw[kind, 0, here, :] * wet * turn(wet, -1)
            west = turn(east, 1)
            twist = 0.25 * raw[kind, 2, here, :] * wet
            north = raw[kind, 1, here, :] * wet * raw[kind, 3, above, :]
            south = raw[kind, 1, below, :] * raw[kind, 3, below, :] * wet
            keep = 1.0 - (east + west + north + south)
            for number, value in enumerate(
                (keep, north, south, west, turn(twist, 1), east, -turn(twist, -1))
            ):
                weights[kind, number, pl.ds(step * CHUNK, CHUNK), :] = value
        return carry

    lax.fori_loop(0, (tall - 2 * EDGE) // CHUNK, make_weights, 0)


def diffuse_kernel(
    n_lat,
    field,
    norm,
    west_cols,
    east_cols,
    south_rows,
    north_rows,
    weights,
    lower,
    upper,
    cells,
    out,
    sampled,
    grid,
    other,
    turned,
    gathered,
):
    levels, rows, lanes = field.shape
    tall = rows + 2 * HALO
    half = lanes // 2
    strips = (levels + 1) // 2
    has_south = lax.axis_index("lat") > 0
    has_north = lax.axis_index("lat") < n_lat - 1
    inside = inside_domain((tall, lanes), rows, has_south, has_north)

    for level in range(levels):
        at = pl.ds(STEPS * level, STEPS)
        grid[level, pl.ds(0, HALO), :] = jnp.zeros((HALO, lanes), jnp.float32)
        grid[level, pl.ds(HALO + rows, HALO), :] = jnp.zeros((HALO, lanes), jnp.float32)
        grid[level, pl.ds(HALO - STEPS, STEPS), :] = jnp.where(has_south, south_rows[at, :], 0.0)
        grid[level, pl.ds(HALO, rows), :] = field[level]
        grid[level, pl.ds(HALO + rows, STEPS), :] = jnp.where(has_north, north_rows[at, :], 0.0)
    for pair in range(strips):
        tile, k = divmod(pair, PAIRS)
        alone = 2 * pair + 1 >= levels
        grid[levels + pair] = strip_plane(
            grid[2 * pair],
            grid[min(2 * pair + 1, levels - 1)],
            spare_columns(east_cols, False) if alone else east_cols[tile],
            spare_columns(west_cols, True) if alone else west_cols[tile],
            None if alone else k,
            STEPS,
            inside,
        )

    count = (tall - 2 * EDGE) // CHUNK

    def sweep(source, target):
        def one_chunk(step, carry):
            start = EDGE + step * CHUNK
            here = pl.ds(start, CHUNK)
            below = pl.ds(start - 1, CHUNK)
            above = pl.ds(start + 1, CHUNK)
            own = pl.ds(step * CHUNK, CHUNK)
            for kind, planes in enumerate((range(levels), range(levels, levels + strips))):
                keep, north, south, to_left, twist_left, to_right, twist_right = (
                    weights[kind, number, own, :] for number in range(7)
                )
                for plane in planes:
                    centre = source[plane, here, :]
                    upper = source[plane, above, :]
                    lower = source[plane, below, :]
                    tilt = upper - lower
                    target[plane, here, :] = (
                        keep * centre
                        + (north * upper + south * lower)
                        + turn(to_left * centre + twist_left * tilt, -1)
                        + turn(to_right * centre + twist_right * tilt, 1)
                    )
            return carry

        lax.fori_loop(0, count, one_chunk, 0)

    def two_steps(number, carry):
        sweep(grid, other)
        sweep(other, grid)
        return carry

    lax.fori_loop(0, STEPS // 2, two_steps, 0)

    column = lane_ids((rows, lanes))
    inner = pl.ds(HALO, rows)
    for level in range(levels):
        edges = grid[levels + level // 2, inner, :]
        move = half * (level % 2)
        result = jnp.where(
            column < STEPS,
            turn(edges, -COLS - move),
            jnp.where(column >= lanes - STEPS, turn(edges, half + COLS - move), grid[level, inner, :]),
        )
        result = norm[level] * result
        out[level] = result
        turned[pl.ds(level, rows, stride=DEEP), :] = result
    for level in range(levels, PAD):
        turned[pl.ds(level, rows, stride=DEEP), :] = jnp.zeros((rows, lanes), jnp.float32)

    even = lane_ids((PAD, lanes)) % 2 == 0
    per_row = lanes // PAD

    def sample_tile(tile, carry):
        for q in range(per_row):
            block = tile * per_row + q

            def sample_group(group, found):
                found = list(found)
                for u in range(UNROLL):
                    spot = group * UNROLL + u
                    start = pl.multiple_of(cells[block, 5, spot], 8)
                    low = turned[pl.ds(start, PAD), :].reshape(PAD // 8, 8, lanes)
                    high = turned[pl.ds(start + DEEP, PAD), :].reshape(PAD // 8, 8, lanes)
                    mixed = low * row_of(lower, block * lanes + spot) + high * row_of(
                        upper, block * lanes + spot
                    )
                    move = (cells[block, 6, spot] + spot) & (lanes - 1)
                    found[u % 2] = found[u % 2] + pltpu.roll(mixed.reshape(PAD, lanes), move, 1)
                return tuple(found)

            zeros = jnp.zeros((PAD, lanes), jnp.float32)
            on_even, on_odd = lax.fori_loop(0, lanes // UNROLL, sample_group, (zeros, zeros))
            gathered[pl.ds(PAD * q, PAD), :] = jnp.where(
                even, on_even + turn(on_even, -1), on_odd + turn(on_odd, -1)
            )
        sampled[pl.ds(pl.multiple_of(tile * lanes, lanes), lanes), :] = gathered[...].T
        return carry

    lax.fori_loop(0, sampled.shape[0] // lanes, sample_tile, 0)


def row_of(table, number):
    return table[pl.ds(number, 8, stride=0), :]


def diffuse(field, norm, halos, weights, lower, upper, cells, n_lat):
    levels, rows, lanes = field.shape
    tall = rows + 2 * HALO
    whole = pl.BlockSpec(memory_space=pltpu.VMEM)
    scalars = pl.BlockSpec(memory_space=pltpu.SMEM)
    planes = levels + (levels + 1) // 2
    return pl.pallas_call(
        functools.partial(diffuse_kernel, n_lat),
        out_shape=(
            jax.ShapeDtypeStruct(field.shape, jnp.float32),
            jax.ShapeDtypeStruct((cells.shape[0] * PAD, lanes), jnp.float32),
        ),
        in_specs=[whole] * 9 + [scalars],
        out_specs=(whole, whole),
        scratch_shapes=[
            pltpu.VMEM((planes, tall, lanes), jnp.float32),
            pltpu.VMEM((planes, tall, lanes), jnp.float32),
            pltpu.VMEM((rows * DEEP, lanes), jnp.float32),
            pltpu.VMEM((lanes, lanes), jnp.float32),
        ],
        compiler_params=pltpu.CompilerParams(vmem_limit_bytes=24 << 20),
    )(field, norm, *halos, weights, lower, upper, cells)


def one_hot_slots(slots, q, rows):
    shape = (rows, slots.shape[1])
    number = lax.broadcasted_iota(jnp.int32, shape, 0) * (LANES // PAD) + q
    return jnp.where(number == slots, 1.0, 0.0)


def route_kernel(innovations, weights, place, owner_column, owner_row, ids, packet, slots, table):
    levels, count = innovations.shape
    total = packet.shape[0]
    same = owner_column[...] == owner_row[...]
    earlier = lax.broadcasted_iota(jnp.int32, (count, count), 0) < lax.broadcasted_iota(
        jnp.int32, (count, count), 1
    )
    rank = jnp.sum(jnp.where(jnp.logical_and(same, earlier), 1, 0), axis=0, keepdims=True)
    slot = owner_row[...] * CAPACITY + rank
    slots[...] = slot

    table[...] = jnp.zeros_like(table)
    table[pl.ds(0, levels), :] = innovations[...]
    table[pl.ds(levels, 4), :] = weights[...]
    table[pl.ds(levels + 4, 2), :] = place[...].astype(jnp.float32)
    flipped = jnp.concatenate(
        [table[:, pl.ds(start, LANES)].T for start in range(0, count, LANES)], axis=0
    )
    sent = jnp.zeros((total, LANES), jnp.float32)
    for q in range(LANES // PAD):
        moved = pltpu.roll(flipped, PAD * q, 1) if q else flipped
        sent += jnp.dot(
            one_hot_slots(slot, q, total),
            moved,
            precision=lax.Precision.HIGHEST,
            preferred_element_type=jnp.float32,
        )
    lane = lane_ids((total, LANES))
    row = lax.broadcasted_iota(jnp.int32, (total, LANES), 0)
    per_device = 2
    row_group = CAPACITY * PAD // LANES
    group = lax.rem(row // row_group, ids.shape[1] // per_device) * per_device
    first_row = lax.rem(row, row_group) == 0
    numbers = jnp.concatenate(
        [ids[...].astype(jnp.float32), jnp.zeros((1, LANES - ids.shape[1]), jnp.float32)], axis=1
    )
    for t in range(per_device):
        number = jnp.sum(jnp.where(lane == group + t, numbers, 0.0), axis=1, keepdims=True)
        spare = jnp.logical_and(first_row, lane == PAD * (t + 1) - 1)
        sent = jnp.where(spare, number, sent)
    packet[...] = sent


def route(innovations, weights, place, owners, ids, devices):
    whole = pl.BlockSpec(memory_space=pltpu.VMEM)
    count = innovations.shape[1]
    return pl.pallas_call(
        route_kernel,
        out_shape=(
            jax.ShapeDtypeStruct((devices * CAPACITY * PAD // LANES, LANES), jnp.float32),
            jax.ShapeDtypeStruct((1, count), jnp.int32),
        ),
        in_specs=[whole] * 6,
        out_specs=(whole, whole),
        scratch_shapes=[pltpu.VMEM((LANES, count), jnp.float32)],
        compiler_params=pltpu.CompilerParams(vmem_limit_bytes=BIG),
    )(innovations, weights, place, owners, owners.reshape(1, count), ids)


def post_kernel(has_coef, source, *refs):
    if has_coef:
        coef, tiles, target, weights_out, middle, late = refs[:6]
        held, send_sem, recv_sem, local_sem, pack_first, pack_last, staged, late_sem = refs[6:14]
        west_cols, east_cols, south_coef, north_coef, weights, raw = refs[14:]
    else:
        target, held, send_sem, recv_sem, local_sem = refs
    n_lat, n_lon = source.shape[:2]
    lat, lon, up, down, right, left = neighbours(n_lat, n_lon)
    across = [lax.rem(lon + step, n_lon) for step in range(1, n_lon)]
    along = [lax.rem(lat + step, n_lat) for step in range(1, n_lat)]
    corners = [(up, right), (up, left), (down, right), (down, left)] if has_coef else []

    barrier = pltpu.get_barrier_semaphore()
    for other in across:
        pl.semaphore_signal(barrier, inc=1, device_id=(lat, other), device_id_type=MESH)
    for other in along:
        pl.semaphore_signal(barrier, inc=1, device_id=(other, lon), device_id_type=MESH)
    for there in corners:
        pl.semaphore_signal(barrier, inc=1, device_id=there, device_id_type=MESH)
    own = pltpu.make_async_copy(source.at[:, lon], held.at[:, lon], local_sem)
    own.start()
    moves = []
    if has_coef:
        count = late.shape[1]
        stage = pltpu.make_async_copy(
            tiles.at[pl.ds(EARLY, MIDDLE + count)], staged, late_sem.at[count]
        )
        stage.start()
        rows = coef.shape[1]
        low, high = packed_columns(
            lambda plane: coef[plane], coef.shape[0], rows, COLS, 0, COEF_PAIRS
        )
        pack_first[...] = low
        pack_last[...] = high
    pl.semaphore_wait(barrier, n_lon + n_lat - 2 + len(corners))

    def push(here, there, number, device):
        copy = pltpu.make_async_remote_copy(
            src_ref=here,
            dst_ref=there,
            send_sem=send_sem.at[number],
            recv_sem=recv_sem.at[number],
            device_id=device,
            device_id_type=MESH,
        )
        copy.start()
        return copy

    copies = [
        push(source.at[:, other], held.at[:, lon], number, (lat, other))
        for number, other in enumerate(across)
    ]
    edges = []
    if has_coef:
        first = pl.ds(0, HALO)
        last = pl.ds(rows - HALO, HALO)
        within_rows = pl.ds(HALO, rows)
        above = pl.ds(HALO + rows, HALO)
        for here, there, device in (
            (coef.at[:, last, :], south_coef, (up, lon)),
            (coef.at[:, first, :], north_coef, (down, lon)),
            (pack_last, west_cols.at[within_rows, :], (lat, right)),
            (pack_first, east_cols.at[within_rows, :], (lat, left)),
            (pack_last.at[last, :], west_cols.at[first, :], (up, right)),
            (pack_first.at[last, :], east_cols.at[first, :], (up, left)),
            (pack_last.at[first, :], west_cols.at[above, :], (down, right)),
            (pack_first.at[first, :], east_cols.at[above, :], (down, left)),
        ):
            edges.append(push(here, there, n_lon + n_lat + len(edges), device))
    if has_coef:
        stage.wait()
        for level in range(count):
            move = pltpu.make_async_copy(
                staged.at[MIDDLE + level], late.at[:, level], late_sem.at[level]
            )
            move.start()
            moves.append(move)
    own.wait()
    for copy in copies:
        copy.wait()
    copies = [
        push(held.at[other], target.at[lat], n_lon + number, (other, lon))
        for number, other in enumerate(along)
    ]
    own = pltpu.make_async_copy(held.at[lat], target.at[lat], local_sem)
    own.start()
    if has_coef:
        per_device = middle.shape[2]
        levels = pl.ds(0, MIDDLE)
        mine = pltpu.make_async_copy(
            staged.at[levels, pl.ds(per_device * lon, per_device)],
            middle.at[lon],
            late_sem.at[count + 1],
        )
        mine.start()
        moves.append(mine)
        for number, other in enumerate(across):
            copies.append(
                push(
                    staged.at[levels, pl.ds(per_device * other, per_device)],
                    middle.at[lon],
                    n_lon + n_lat + 8 + number,
                    (lat, other),
                )
            )
        for copy in edges:
            copy.wait()
        step_coefficients(n_lat, coef, west_cols, east_cols, south_coef, north_coef, weights, raw)
        move = pltpu.make_async_copy(weights, weights_out, late_sem.at[count + 2])
        move.start()
        moves.append(move)
    own.wait()
    for copy in copies + moves:
        copy.wait()


def post(packet, n_lat, n_lon, collective_id, coef=None, tiles=None):
    whole = pl.BlockSpec(memory_space=pltpu.VMEM)
    anywhere = pl.BlockSpec(memory_space=pl.ANY)
    outside = pl.BlockSpec(memory_space=pltpu.HBM)
    blocks = packet.reshape(n_lat, n_lon, -1, LANES)
    has_coef = coef is not None
    sems = n_lon + n_lat + (8 + n_lon) * has_coef
    out_shape = [jax.ShapeDtypeStruct(blocks.shape, jnp.float32)]
    scratch = [
        pltpu.VMEM(blocks.shape, jnp.float32),
        pltpu.SemaphoreType.DMA((sems,)),
        pltpu.SemaphoreType.DMA((sems,)),
        pltpu.SemaphoreType.DMA,
    ]
    operands, in_specs, out_specs = [blocks], [whole], [outside if has_coef else whole]
    if has_coef:
        count, rows, lanes = coef.shape
        levels, slots, depth, _ = tiles.shape
        tall = rows + 2 * HALO
        table = (2, 7, tall - 2 * EDGE, lanes)
        later = levels - EARLY - MIDDLE
        out_shape += [
            jax.ShapeDtypeStruct(shape, jnp.float32)
            for shape in (
                table,
                (n_lon, MIDDLE, slots // n_lon, depth, lanes),
                (slots, later, depth, lanes),
            )
        ]
        scratch += [
            pltpu.VMEM((rows, lanes), jnp.float32),
            pltpu.VMEM((rows, lanes), jnp.float32),
            pltpu.VMEM((MIDDLE + later, slots, depth, lanes), jnp.float32),
            pltpu.SemaphoreType.DMA((later + 3,)),
            pltpu.VMEM((tall, lanes), jnp.float32),
            pltpu.VMEM((tall, lanes), jnp.float32),
            pltpu.VMEM((count, HALO, lanes), jnp.float32),
            pltpu.VMEM((count, HALO, lanes), jnp.float32),
            pltpu.VMEM(table, jnp.float32),
            pltpu.VMEM((2, count, tall, lanes), jnp.float32),
        ]
        operands += [coef, tiles]
        in_specs += [whole, anywhere]
        out_specs += [outside] * 3
    received, *rest = pl.pallas_call(
        functools.partial(post_kernel, has_coef),
        out_shape=out_shape,
        in_specs=in_specs,
        out_specs=out_specs,
        scratch_shapes=scratch,
        compiler_params=pltpu.CompilerParams(
            collective_id=collective_id, has_side_effects=True, vmem_limit_bytes=BIG if has_coef else 4 << 20
        ),
    )(*operands)
    return (received.reshape(packet.shape), *rest)


def spread_kernel(
    levels, packet, seen, lower, upper, cells_out, turned, observed, other, cells, sem
):
    total, lanes = packet.shape
    per_row = lanes // PAD
    tiles = total // lanes
    level_lane = PAD - 8
    sublane = lax.broadcasted_iota(jnp.int32, (8, lanes), 0)
    for tile in range(tiles):
        flipped = packet[pl.ds(tile * lanes, lanes), :].T
        turned[pl.ds(tile * lanes, lanes), :] = flipped
        for q in range(per_row):
            last = flipped[PAD * q + level_lane : PAD * (q + 1)].astype(jnp.int32)
            last = jnp.where(sublane == 5, last * DEEP, jnp.where(sublane == 6, lanes - last, last))
            cells_out[tile * per_row + q] = last
    copy = pltpu.make_async_copy(cells_out, cells, sem)
    copy.start()

    lane = lane_ids((lanes, lanes)).astype(jnp.float32)
    for tile in range(tiles):
        rows = packet[pl.ds(tile * lanes, lanes), :]
        for q in range(per_row):
            first, second, third, fourth, row, column = (
                jnp.broadcast_to(rows[:, n : n + 1], (lanes, lanes))
                for n in range(PAD * q + level_lane + 1, PAD * q + level_lane + 7)
            )
            here = lane == column
            beside = lane == column + 1.0
            block = pl.ds((tile * per_row + q) * lanes, lanes)
            lower[block, :] = jnp.where(here, first, jnp.where(beside, second, 0.0))
            upper[block, :] = jnp.where(here, third, jnp.where(beside, fourth, 0.0))

    is_level = lax.broadcasted_iota(jnp.int32, (PAD, lanes), 0) < levels
    parts = (observed, other)
    for part in parts:
        part[...] = jnp.zeros_like(part)
    copy.wait()

    def spread_block(block, carry):
        values = jnp.where(is_level, turned[pl.ds(pl.multiple_of(block * PAD, PAD), PAD), :], 0.0)

        def spread_group(group, carry):
            moved = pltpu.roll(values, lax.rem(lanes - group * UNROLL, lanes), 1)
            for u in range(UNROLL):
                spot = group * UNROLL + u
                value = jnp.broadcast_to(moved[:, u : u + 1], (PAD, lanes)).reshape(
                    PAD // 8, 8, lanes
                )
                part = parts[u % len(parts)]
                for table, offset in ((lower, 0), (upper, DEEP)):
                    start = pl.multiple_of(cells[block, 5, spot] + offset, 8)
                    added = (value * row_of(table, block * lanes + spot)).reshape(PAD, lanes)
                    part[pl.ds(start, PAD), :] = part[pl.ds(start, PAD), :] + added
            return carry

        lax.fori_loop(0, lanes // UNROLL, spread_group, 0)
        return carry

    lax.fori_loop(0, tiles * per_row, spread_block, 0)
    rows = seen.shape[1]
    for level in range(levels):
        at = pl.ds(level, rows, stride=DEEP)
        seen[level] = observed[at, :] + other[at, :]


def spread(packet, levels, rows):
    total, lanes = packet.shape
    whole = pl.BlockSpec(memory_space=pltpu.VMEM)
    blocks = total // PAD
    masks = jax.ShapeDtypeStruct((blocks * lanes, lanes), jnp.float32)
    return pl.pallas_call(
        functools.partial(spread_kernel, levels),
        out_shape=(
            jax.ShapeDtypeStruct((levels, rows, lanes), jnp.float32),
            masks,
            masks,
            jax.ShapeDtypeStruct((blocks, 8, lanes), jnp.int32),
        ),
        in_specs=[whole],
        out_specs=(whole,) * 4,
        scratch_shapes=[
            pltpu.VMEM(packet.shape, jnp.float32),
            pltpu.VMEM((rows * DEEP, lanes), jnp.float32),
            pltpu.VMEM((rows * DEEP, lanes), jnp.float32),
            pltpu.SMEM((blocks, 8, lanes), jnp.int32),
            pltpu.SemaphoreType.DMA,
        ],
        compiler_params=pltpu.CompilerParams(vmem_limit_bytes=20 << 20),
    )(packet)


def combine_kernel(cells, seen, early, middle, late, norm, field):
    slots, _, depth, lanes = early.shape
    n_lon = lax.axis_size("lon")
    per_device = slots // n_lon
    per_row = lanes // PAD
    row_group = CAPACITY * PAD // lanes
    base = lax.axis_index("lat") * n_lon

    def one_tile(slot, carry):
        at = (base + slot // per_device) * row_group
        block = (at // lanes) * per_row + lax.rem(slot, per_device)
        rows = pl.ds(pl.multiple_of(cells[block, 7, lax.rem(at, lanes)] * depth, depth), depth)
        start = 0
        for tiles in (
            early[slot],
            middle[slot // per_device, :, lax.rem(slot, per_device)],
            late[slot],
        ):
            part = pl.ds(start, tiles.shape[0])
            start += tiles.shape[0]
            field[part, rows, :] = norm[part, rows, :] * (seen[part, rows, :] + tiles)
        return carry

    lax.fori_loop(0, slots, one_tile, 0)


def combine(cells, seen, early, middle, late, norm):
    whole = pl.BlockSpec(memory_space=pltpu.VMEM)
    return pl.pallas_call(
        combine_kernel,
        out_shape=jax.ShapeDtypeStruct(norm.shape, jnp.float32),
        in_specs=[pl.BlockSpec(memory_space=pltpu.SMEM)] + [whole] * 5,
        out_specs=whole,
        compiler_params=pltpu.CompilerParams(vmem_limit_bytes=8 << 20),
    )(cells, seen, early, middle, late, norm)


def collect_kernel(levels, returned, slots, out):
    total, lanes = returned.shape
    flipped = jnp.concatenate(
        [returned[pl.ds(start, lanes), :].T for start in range(0, total, lanes)], axis=1
    )
    values = jnp.zeros((PAD, slots.shape[1]), jnp.float32)
    for q in range(lanes // PAD):
        values += jnp.dot(
            flipped[PAD * q : PAD * (q + 1)],
            one_hot_slots(slots[...], q, total),
            precision=lax.Precision.HIGHEST,
            preferred_element_type=jnp.float32,
        )
    out[...] = values[:levels]


def collect(returned, slots, levels):
    whole = pl.BlockSpec(memory_space=pltpu.VMEM)
    return pl.pallas_call(
        functools.partial(collect_kernel, levels),
        out_shape=jax.ShapeDtypeStruct((levels, slots.shape[1]), jnp.float32),
        in_specs=[whole] * 2,
        out_specs=whole,
        compiler_params=pltpu.CompilerParams(vmem_limit_bytes=8 << 20),
    )(returned, slots)


def on_device(
    innovations,
    owners,
    prof_row,
    prof_col,
    interp_weights,
    model_tiles,
    model_ids,
    face_x,
    face_y,
    cross_term,
    wet_mask,
    norm_factor,
):
    levels, rows, lanes = norm_factor.shape
    n_lat = lax.axis_size("lat")
    n_lon = lax.axis_size("lon")
    early = lax.all_to_all(
        jnp.transpose(model_tiles[:EARLY], (1, 0, 2, 3)), "lon", split_axis=0, concat_axis=0, tiled=True
    )
    coef = jnp.stack([face_x, face_y, cross_term, wet_mask.astype(jnp.float32)])
    place = jnp.stack([prof_row, prof_col])
    packet, slots = route(innovations, interp_weights, place, owners, model_ids, n_lat * n_lon)
    packet, weights, middle, late = post(packet, n_lat, n_lon, 1, coef, model_tiles)
    late = lax.all_to_all(late, "lon", split_axis=0, concat_axis=0, tiled=True)
    seen, lower, upper, cells = spread(packet, levels, rows)
    field = combine(cells, seen, early, middle, late, norm_factor)
    halos = exchange(field, n_lat, n_lon)
    smoothed, sampled = diffuse(field, norm_factor, halos, weights, lower, upper, cells, n_lat)
    (returned,) = post(sampled, n_lat, n_lon, 2)
    profile_values = collect(returned, slots, levels)
    return (smoothed, profile_values)


def solution(mesh):
    in_specs = (
        P(None, ("lat", "lon")),
        P(("lat", "lon"), None),
        P(("lat", "lon")),
        P(("lat", "lon")),
        P(None, ("lat", "lon")),
        P(None, ("lat", "lon"), None, None),
        P(None, ("lat", "lon")),
        P("lat", "lon"),
        P("lat", "lon"),
        P("lat", "lon"),
        P("lat", "lon"),
        P(None, "lat", "lon"),
    )
    out_specs = (P(None, "lat", "lon"), P(None, ("lat", "lon")))
    return jax.shard_map(
        on_device, mesh=mesh, in_specs=in_specs, out_specs=out_specs, check_vma=False
    )
```
